32 devices in a mesh: dp: 8 (over z, y), section: 4 (over x, core).
Axes of the slice: x: 2, y: 2, z: 4, core: 2. Of those that a mesh axis runs over, the one named last changes fastest.
Arguments:
- tokens: bfloat16 [2, 8, 1024, 768], P(None, 'dp'), may hold values from -6 to 6
- lengths: int32 [2, 8], P(None, 'dp'), may hold values from 300 to 1024, as said below
- cotangent: bfloat16 [2, 8, 1024, 768], P(None, 'dp'), may hold values from -6 to 6
- attn_gain: bfloat16 [2, 768], P(None, 'dp'), may hold values from 0.5 to 1.5
- attn_shift: bfloat16 [2, 768], P(None, 'dp'), may hold values from -1.796875 to 1.796875
- qkv_weight: bfloat16 [2, 768, 2304], P(None, 'dp'), may hold values from -0.21875 to 0.21875
- qv_bias: bfloat16 [2, 1536], P(None, 'dp'), may hold values from -3 to 3
- out_weight: bfloat16 [2, 768, 768], P(None, 'dp'), may hold values from -3.5 to 3.5
- out_bias: bfloat16 [2, 768], P(None, 'dp'), may hold values from -1.796875 to 1.796875
- ffn_gain: bfloat16 [2, 768], P(None, 'dp'), may hold values from 0.5 to 1.5
- ffn_shift: bfloat16 [2, 768], P(None, 'dp'), may hold values from -1.796875 to 1.796875
- up_weight: bfloat16 [2, 768, 3072], P(None, 'dp'), may hold values from -0.21875 to 0.21875
- up_bias: bfloat16 [2, 3072], P(None, 'dp'), may hold values from -3 to 3
- down_weight: bfloat16 [2, 3072, 768], P(None, 'dp'), may hold values from -0.109375 to 0.109375
- down_bias: bfloat16 [2, 768], P(None, 'dp'), may hold values from -1.796875 to 1.796875
Outputs:
- encoded: bfloat16 [2, 8, 1024, 768], P(None, 'dp', 'section')
- grad_tokens: bfloat16 [2, 8, 1024, 768], P(None, 'dp', 'section')
- grad_attn_gain: float32 [2, 768], P(None, 'dp')
- grad_attn_shift: float32 [2, 768], P(None, 'dp')
- grad_qkv_weight: float32 [2, 768, 2304], P(None, 'dp')
- grad_qv_bias: float32 [2, 1536], P(None, 'dp')
- grad_out_weight: float32 [2, 768, 768], P(None, 'dp')
- grad_out_bias: float32 [2, 768], P(None, 'dp')
- grad_ffn_gain: float32 [2, 768], P(None, 'dp')
- grad_ffn_shift: float32 [2, 768], P(None, 'dp')
- grad_up_weight: float32 [2, 768, 3072], P(None, 'dp')
- grad_up_bias: float32 [2, 3072], P(None, 'dp')
- grad_down_weight: float32 [2, 3072, 768], P(None, 'dp')
- grad_down_bias: float32 [2, 768], P(None, 'dp')
The draws below stay inside these ranges and needn't reach their ends.
Inputs may be any that keep to these rules, and one draw needn't show every extreme that they name: lengths[m, c] counts the expressed genes of cell c in micro-batch m; in every micro-batch some cell has exactly 1024.
All inputs are finite; a program needn't handle non-finite values.
Results may differ from the reference program's by a relative error of at most 0.013.
Values may be sent and summed in bfloat16 or wider, within the bound.
No kernel may reach another device: no remote copies, remote signals or barrier semaphores. Data moves between devices by JAX's collectives and lax.ppermute only.
A program may use at most 576 MiB of HBM per device.

```python
import math
import jax
import jax.numpy as jnp
from jax import lax

D = 768
HEADS = 12
HEAD = 64
FF = 3072
SEQ = 1024
MIN_LEN = 300
LAYERS = 2
MICRO = 2
CELLS = 8


def draw_lengths(key, part):
    key_one, key_two, key_pick = jax.random.split(key, 3)
    spread = SEQ - MIN_LEN + 1
    early_draw = jax.random.randint(key_one, (MICRO, CELLS), 0, spread)
    later_draw = jax.random.randint(key_two, (MICRO, CELLS), 0, spread)
    sampled = MIN_LEN + jnp.minimum(early_draw, later_draw)
    chosen = jax.random.randint(key_pick, (MICRO, 1), 0, CELLS)
    column_ids = jnp.arange(CELLS, dtype=jnp.int32)[None, :]
    return jnp.where(column_ids == chosen, SEQ, sampled).astype(jnp.int32)


def block_levels(key, shape, shards, least, high):
    def one(axis_at, blocks):
        heights = jax.random.uniform(jax.random.fold_in(jax.random.fold_in(key, 6), axis_at), (blocks,), jnp.float32, least / len(shards), high / len(shards))
        return jnp.repeat(jnp.exp(heights), shape[axis_at] // blocks).reshape((-1,) + (1,) * (len(shape) - axis_at - 1))

    level = one(*shards[0])
    for cut in shards[1:]:
        level = level * one(*cut)
    return level


def bell_draw(key, dims, deviation, bound, cuts=(), kind=jnp.bfloat16):
    drawn = deviation * jax.random.normal(key, dims, jnp.float32)
    if cuts:
        drawn = drawn * block_levels(key, dims, cuts, -0.22, 0.18)
    return jnp.clip(drawn, -bound, bound).astype(kind)


def setup_inputs(seed: int = 0) -> dict:
    splits = jax.random.split(jax.random.key(seed), 16)
    tokens = bell_draw(splits[0], (MICRO, CELLS, SEQ, D), 1.0, 6.0, ((1, 8),))
    lengths = draw_lengths(jax.random.fold_in(splits[15], 71), 0)
    cotangent = bell_draw(splits[2], (MICRO, CELLS, SEQ, D), 1.0, 6.0, ((1, 8),))
    attn_gain = jnp.clip(1.0 + 0.1 * jax.random.normal(splits[3], (LAYERS, D), jnp.float32), 0.5, 1.5).astype(jnp.bfloat16)
    attn_shift = bell_draw(splits[4], (LAYERS, D), 0.3, 1.796875, ((1, 8),))
    qkv_weight = bell_draw(splits[5], (LAYERS, D, 3 * D), D ** -0.5, 0.21875, ((1, 8),))
    qv_bias = bell_draw(splits[6], (LAYERS, 2 * D), 0.5, 3.0, ((1, 8),))
    out_weight = bell_draw(splits[7], (LAYERS, D, D), (D * 4 // SEQ) ** -0.5, 3.5, ((1, 8),))
    out_bias = bell_draw(splits[8], (LAYERS, D), 0.3, 1.796875, ((1, 8),))
    ffn_gain = jnp.clip(1.0 + 0.1 * jax.random.normal(splits[9], (LAYERS, D), jnp.float32), 0.5, 1.5).astype(jnp.bfloat16)
    ffn_shift = bell_draw(splits[10], (LAYERS, D), 0.3, 1.796875, ((1, 8),))
    up_weight = bell_draw(splits[11], (LAYERS, D, FF), D ** -0.5, 0.21875, ((1, 8),))
    up_bias = bell_draw(splits[12], (LAYERS, FF), 0.5, 3.0, ((1, 8),))
    down_weight = bell_draw(splits[13], (LAYERS, FF, D), FF ** -0.5, 0.109375, ((1, 8),))
    down_bias = bell_draw(splits[14], (LAYERS, D), 0.3, 1.796875, ((1, 8),))
    return {"tokens": tokens, "lengths": lengths, "cotangent": cotangent, "attn_gain": attn_gain, "attn_shift": attn_shift, "qkv_weight": qkv_weight, "qv_bias": qv_bias, "out_weight": out_weight, "out_bias": out_bias, "ffn_gain": ffn_gain, "ffn_shift": ffn_shift, "up_weight": up_weight, "up_bias": up_bias, "down_weight": down_weight, "down_bias": down_bias}


@jax.custom_vjp
def low(v):
    return lax.optimization_barrier(v.astype(jnp.bfloat16)).astype(jnp.float32)

@jax.custom_vjp
def low_back(v):
    return v

def low_keep(v):
    return (low(v), None)

def low_pass(kept, grad):
    return (grad,)

def back_keep(v):
    return (v, None)

def back_low(kept, grad):
    return (low(grad),)
low.defvjp(low_keep, low_pass)
low_back.defvjp(back_keep, back_low)
NORM_EPS = 1e-05
MASK_FLOOR = -1e+30

def norm_rows(stream, norm_gain, norm_shift):
    center = stream - lax.optimization_barrier(jnp.mean(stream, axis=-1, keepdims=True))
    spread = lax.optimization_barrier(jnp.mean(center * center, axis=-1, keepdims=True))
    return center * lax.rsqrt(spread + NORM_EPS) * norm_gain + norm_shift

def product(left, right):
    return jnp.dot(left, right, precision=lax.Precision.HIGHEST)

def attention_cell(stream, key_valid, norm_gain, norm_shift, qkv_weight, qv_bias, out_weight, out_bias):
    seq_len = stream.shape[0]
    model_width = stream.shape[1]
    normed = low(norm_rows(stream, norm_gain, norm_shift))
    projected = product(normed, qkv_weight)
    queries = low(low_back(projected[:, :model_width] + qv_bias[:model_width]))
    keys_all = low(low_back(projected[:, model_width:2 * model_width]))
    values_all = low(low_back(projected[:, 2 * model_width:] + qv_bias[model_width:]))
    query_heads = queries.reshape(seq_len, HEADS, HEAD)
    key_heads = keys_all.reshape(seq_len, HEADS, HEAD)
    value_heads = values_all.reshape(seq_len, HEADS, HEAD)
    score_scale = 1.0 / math.sqrt(HEAD)
    scores = jnp.einsum('qhd,khd->hqk', query_heads, key_heads, precision=lax.Precision.HIGHEST) * score_scale
    masked = low_back(jnp.where(key_valid[None, None, :], scores, MASK_FLOOR))
    attend_p = jax.nn.softmax(masked, axis=-1)
    mixed_out = jnp.einsum('hqk,khd->qhd', low(attend_p), value_heads, precision=lax.Precision.HIGHEST)
    mixed_out = low(low_back(mixed_out.reshape(seq_len, model_width)))
    return low(low_back(stream + product(mixed_out, out_weight) + out_bias))

def ffn_cell(stream, norm_gain, norm_shift, up_weight, up_bias, down_weight, down_bias):
    normed = low(norm_rows(stream, norm_gain, norm_shift))
    up_proj = low_back(product(normed, up_weight) + up_bias)
    hidden = low(jax.nn.gelu(up_proj, approximate=False))
    return low(low_back(stream + product(hidden, down_weight) + down_bias))

def run_blocks(stream, key_valid, attn_gain, attn_shift, qkv_weight, qv_bias, out_weight, out_bias, ffn_gain, ffn_shift, up_weight, up_bias, down_weight, down_bias):
    stream = low_back(stream)
    for layer_id in range(LAYERS):

        def attention_step(pair, layer_id=layer_id):
            cell_rows, cell_valid = pair
            return attention_cell(cell_rows, cell_valid, attn_gain[layer_id], attn_shift[layer_id], qkv_weight[layer_id], qv_bias[layer_id], out_weight[layer_id], out_bias[layer_id])
        stream = lax.map(jax.checkpoint(attention_step), (stream, key_valid))

        def ffn_step(cell_rows, layer_id=layer_id):
            return ffn_cell(cell_rows, ffn_gain[layer_id], ffn_shift[layer_id], up_weight[layer_id], up_bias[layer_id], down_weight[layer_id], down_bias[layer_id])
        stream = lax.map(jax.checkpoint(ffn_step), stream)
    return stream

def reference(tokens, lengths, cotangent, attn_gain, attn_shift, qkv_weight, qv_bias, out_weight, out_bias, ffn_gain, ffn_shift, up_weight, up_bias, down_weight, down_bias):
    cell_total = MICRO * CELLS
    flat_tokens = tokens.reshape(cell_total, SEQ, D).astype(jnp.float32)
    key_valid = jnp.arange(SEQ, dtype=jnp.int32)[None, :] < lengths.reshape(cell_total, 1).astype(jnp.int32)
    params = tuple((item.astype(jnp.float32) for item in (attn_gain, attn_shift, qkv_weight, qv_bias, out_weight, out_bias, ffn_gain, ffn_shift, up_weight, up_bias, down_weight, down_bias)))

    def forward(stream, *weights):
        return run_blocks(stream, key_valid, *weights)
    result, pull = jax.vjp(forward, flat_tokens, *params)
    grads = pull(cotangent.reshape(cell_total, SEQ, D).astype(jnp.float32))
    encoded = result.reshape(MICRO, CELLS, SEQ, D).astype(jnp.bfloat16)
    grad_tokens = grads[0].reshape(MICRO, CELLS, SEQ, D).astype(jnp.bfloat16)
    return (encoded, grad_tokens, grads[1], grads[2], grads[3], grads[4], grads[5], grads[6], grads[7], grads[8], grads[9], grads[10], grads[11], grads[12])
```

```python
from functools import partial
import math

import jax
import jax.numpy as jnp
from jax import lax
from jax.experimental import pallas as pl
from jax.experimental.pallas import tpu as pltpu
from jax.sharding import PartitionSpec as P

HEAD = 64
PAIR = 2 * HEAD
NORM_EPS = 1e-05
MASK_FLOOR = -1e30
F32 = jnp.float32
BF16 = jnp.bfloat16


def nt_dot(left, right):
    return lax.dot_general(left, right, (((1,), (1,)), ((), ())), preferred_element_type=F32)


def nn_dot(left, right):
    return jnp.dot(left, right, preferred_element_type=F32)


def tn_dot(left, right):
    return lax.dot_general(left, right, (((0,), (0,)), ((), ())), preferred_element_type=F32)


def head_lanes(block, head):
    lane = lax.broadcasted_iota(jnp.int32, block.shape, 1)
    keep = (lane < HEAD) if head == 0 else (lane >= HEAD)
    return jnp.where(keep, block, jnp.zeros_like(block))


def attend_kernel(lens_ref, q_ref, ko_ref, kp_ref, vo_ref, vp_ref, o_ref, prob_ref):
    rows = q_ref.shape[0]
    score_scale = 1.0 / math.sqrt(HEAD)
    query_pair = q_ref[...] * jnp.asarray(score_scale, BF16)
    value_t = [vo_ref[...].T, vp_ref[...].T]
    mixed = []
    for head in range(2):
        query = head_lanes(query_pair, head)
        scores = []
        for part, key_ref in enumerate((ko_ref, kp_ref)):
            part_scores = nt_dot(key_ref[...], query)
            key_row = lax.broadcasted_iota(jnp.int32, part_scores.shape, 0)
            scores.append(jnp.where(key_row < lens_ref[part], part_scores, MASK_FLOOR))
        row_max = jnp.maximum(
            jnp.max(scores[0], axis=0, keepdims=True), jnp.max(scores[1], axis=0, keepdims=True)
        )
        raised = [jnp.exp(item - row_max) for item in scores]
        total = jnp.sum(raised[0], axis=0, keepdims=True) + jnp.sum(
            raised[1], axis=0, keepdims=True
        )
        inverse = 1.0 / total
        head_out = jnp.zeros((HEAD, rows), F32)
        for part in range(2):
            prob = (raised[part] * inverse).astype(BF16)
            prob_ref[head, part * rows : (part + 1) * rows, :] = prob
            head_out = head_out + nn_dot(
                value_t[part][head * HEAD : (head + 1) * HEAD, :], prob
            )
        mixed.append(head_out)
    o_ref[...] = jnp.concatenate(mixed, axis=0).T.astype(BF16)


def attend(queries, key_own, key_peer, value_own, value_peer, lens):
    rows, width = queries.shape
    pairs = width // PAIR
    block = pl.BlockSpec((rows, PAIR), lambda p, lens: (0, p))
    return pl.pallas_call(
        attend_kernel,
        grid_spec=pltpu.PrefetchScalarGridSpec(
            num_scalar_prefetch=1,
            grid=(pairs,),
            in_specs=[block] * 5,
            out_specs=[
                block,
                pl.BlockSpec((2, 2 * rows, rows), lambda p, lens: (p, 0, 0)),
            ],
        ),
        out_shape=[
            jax.ShapeDtypeStruct((rows, width), BF16),
            jax.ShapeDtypeStruct((2 * pairs, 2 * rows, rows), BF16),
        ],
        compiler_params=pltpu.CompilerParams(vmem_limit_bytes=48 << 20),
        cost_estimate=pl.CostEstimate(
            flops=2 * 2 * rows * 2 * rows * width * 4,
            transcendentals=2 * pairs * 2 * rows * rows,
            bytes_accessed=2 * pairs * 2 * rows * rows * 2 + 6 * rows * width * 2,
        ),
    )(lens, queries, key_own, key_peer, value_own, value_peer)


def attend_back_kernel(
    q_ref, ko_ref, kp_ref, vo_ref, vp_ref, o_ref, go_ref, prob_ref,
    gq_ref, gko_ref, gkp_ref, gvo_ref, gvp_ref,
):
    rows = q_ref.shape[0]
    score_scale = 1.0 / math.sqrt(HEAD)
    query_pair = q_ref[...] * jnp.asarray(score_scale, BF16)
    grad_pair = go_ref[...]
    inner = (o_ref[...].astype(F32) * grad_pair.astype(F32)).T
    key_refs = (ko_ref, kp_ref)
    value_refs = (vo_ref, vp_ref)
    key_t = [ref[...].T for ref in key_refs]
    grad_key = [None, None]
    grad_value = [None, None]
    grad_query = []
    for head in range(2):
        query = head_lanes(query_pair, head)
        grad_out = head_lanes(grad_pair, head)
        inner_row = jnp.sum(inner[head * HEAD : (head + 1) * HEAD, :], axis=0, keepdims=True)
        head_query = jnp.zeros((HEAD, rows), F32)
        for part in range(2):
            prob = prob_ref[head, part * rows : (part + 1) * rows, :]
            grad_prob = nt_dot(value_refs[part][...], grad_out)
            grad_score = (prob.astype(F32) * (grad_prob - inner_row)).astype(BF16)
            value_term = nn_dot(prob, grad_out)
            key_term = nn_dot(grad_score, query)
            grad_value[part] = value_term if head == 0 else grad_value[part] + value_term
            grad_key[part] = key_term if head == 0 else grad_key[part] + key_term
            head_query = head_query + nn_dot(
                key_t[part][head * HEAD : (head + 1) * HEAD, :], grad_score
            )
        grad_query.append(head_query * score_scale)
    gq_ref[...] = jnp.concatenate(grad_query, axis=0).T.astype(BF16)
    gko_ref[...] = grad_key[0]
    gkp_ref[...] = grad_key[1].astype(BF16)
    gvo_ref[...] = grad_value[0]
    gvp_ref[...] = grad_value[1].astype(BF16)


def attend_back(queries, key_own, key_peer, value_own, value_peer, mixed, grad_mixed, probs):
    rows, width = queries.shape
    pairs = width // PAIR
    block = pl.BlockSpec((rows, PAIR), lambda p: (0, p))
    low = jax.ShapeDtypeStruct((rows, width), BF16)
    full = jax.ShapeDtypeStruct((rows, width), F32)
    return pl.pallas_call(
        attend_back_kernel,
        grid=(pairs,),
        in_specs=[block] * 7 + [pl.BlockSpec((2, 2 * rows, rows), lambda p: (p, 0, 0))],
        out_specs=[block] * 5,
        out_shape=[low, full, low, full, low],
        compiler_params=pltpu.CompilerParams(vmem_limit_bytes=48 << 20),
        cost_estimate=pl.CostEstimate(
            flops=2 * 2 * rows * 2 * rows * width * 8,
            transcendentals=0,
            bytes_accessed=2 * pairs * 2 * rows * rows * 2 + 14 * rows * width * 2,
        ),
    )(queries, key_own, key_peer, value_own, value_peer, mixed, grad_mixed, probs)


def norm_stats(stream):
    center = stream - jnp.mean(stream, axis=-1, keepdims=True)
    spread = jnp.mean(center * center, axis=-1, keepdims=True)
    return center, lax.rsqrt(spread + NORM_EPS)


def norm_rows(stream_low, gain, shift):
    center, root = norm_stats(stream_low.astype(F32))
    return (center * root * gain.astype(F32) + shift.astype(F32)).astype(BF16)


def norm_back(stream_low, gain, grad_normed, grad_low):
    center, root = norm_stats(stream_low.astype(F32))
    unit = center * root
    grad_gain = jnp.sum(grad_normed * unit, axis=0)
    grad_shift = jnp.sum(grad_normed, axis=0)
    grad_unit = grad_normed * gain.astype(F32)
    grad_stream = root * (
        grad_unit
        - jnp.mean(grad_unit, axis=-1, keepdims=True)
        - unit * jnp.mean(grad_unit * unit, axis=-1, keepdims=True)
    )
    return (grad_low.astype(F32) + grad_stream).astype(BF16), grad_gain, grad_shift


def gelu_value(up_proj):
    return 0.5 * up_proj * (1.0 + lax.erf(up_proj * math.sqrt(0.5)))


def gelu_slope(up_proj):
    bell = jnp.exp(-0.5 * up_proj * up_proj) * (1.0 / math.sqrt(2.0 * math.pi))
    return 0.5 * (1.0 + lax.erf(up_proj * math.sqrt(0.5))) + up_proj * bell


def local(
    tokens, lengths, cotangent, attn_gain, attn_shift, qkv_weight, qv_bias, out_weight, out_bias,
    ffn_gain, ffn_shift, up_weight, up_bias, down_weight, down_bias,
):
    layers, _, width3 = qkv_weight.shape
    width = width3 // 3
    micro_count, cell_count, seq_len, _ = tokens.shape
    section_id = lax.axis_index("section")
    section_count = lax.axis_size("section")
    share = section_count // micro_count
    assert cell_count == 1 and share == 2
    cell = section_id // share
    half = section_id % share
    rows = seq_len // share
    swap = [(i, i ^ 1) for i in range(section_count)]

    def to_peer(block):
        return lax.ppermute(block, "section", swap)

    def mine(whole):
        return lax.dynamic_slice(
            whole, (cell, 0, half * rows, 0), (1, 1, rows, width)
        ).reshape(rows, width)

    stream = mine(tokens)
    grad = mine(cotangent)
    length = lax.dynamic_slice(lengths, (cell, 0), (1, 1)).reshape(())
    lens = jnp.stack([length - half * rows, length - (1 - half) * rows])

    def whole(shard):
        return lax.all_gather(shard, "dp", axis=0, tiled=True)

    vec = [
        [whole(item[l]) for item in (attn_gain, attn_shift, qv_bias, out_bias, ffn_gain, ffn_shift, up_bias, down_bias)]
        for l in range(layers)
    ]
    mats = [[whole(item[l]) for item in (qkv_weight, out_weight, up_weight, down_weight)] for l in range(layers)]

    saved = []
    for l in range(layers):
        a_gain, a_shift, qv_b, out_b, f_gain, f_shift, up_b, down_b = vec[l]
        qkv_w, out_w, up_w, down_w = mats[l]
        attn_in = stream
        normed = norm_rows(stream, a_gain, a_shift)
        qb = jnp.concatenate([qv_b[:width], jnp.zeros((width,), BF16), qv_b[width:]]).astype(F32)
        proj = (nn_dot(normed, qkv_w) + qb).astype(BF16)
        queries, key_own, value_own = proj[:, :width], proj[:, width : 2 * width], proj[:, 2 * width :]
        key_peer, value_peer = to_peer(key_own), to_peer(value_own)
        mixed, probs = attend(queries, key_own, key_peer, value_own, value_peer, lens)
        stream = (attn_in.astype(F32) + nn_dot(mixed, out_w) + out_b.astype(F32)).astype(BF16)
        ffn_in = stream
        normed2 = norm_rows(stream, f_gain, f_shift)
        up_proj = nn_dot(normed2, up_w) + up_b.astype(F32)
        hidden = gelu_value(up_proj).astype(BF16)
        stream = (ffn_in.astype(F32) + nn_dot(hidden, down_w) + down_b.astype(F32)).astype(BF16)
        saved.append(
            (attn_in, normed, queries, key_own, key_peer, value_own, value_peer, mixed, probs,
             ffn_in, normed2, up_proj, hidden)
        )

    def redistribute(block):
        quarter = rows // 2
        route_a = [(2 * c + h, 2 * h + c) for c in range(2) for h in range(2)]
        route_b = [(2 * c + h, 2 * h + 1 - c) for c in range(2) for h in range(2)]
        low_half, high_half = block[:quarter], block[quarter:]
        first = cell == 0
        send_a = jnp.where(first, low_half, high_half)
        send_b = jnp.where(first, high_half, low_half)
        got_a = lax.ppermute(send_a, "section", route_a)
        got_b = lax.ppermute(send_b, "section", route_b)
        even = section_id % 2 == 0
        return jnp.stack([jnp.where(even, got_a, got_b), jnp.where(even, got_b, got_a)])[:, None]

    encoded = redistribute(stream)

    def scatter(term):
        shard = lax.psum_scatter(term.astype(BF16), "dp", scatter_dimension=0, tiled=True)
        return lax.psum(shard, "section").astype(F32)

    grads = [None] * layers
    for l in reversed(range(layers)):
        a_gain, a_shift, qv_b, out_b, f_gain, f_shift, up_b, down_b = vec[l]
        qkv_w, out_w, up_w, down_w = mats[l]
        (attn_in, normed, queries, key_own, key_peer, value_own, value_peer, mixed, probs,
         ffn_in, normed2, up_proj, hidden) = saved[l]
        g_down_b = jnp.sum(grad.astype(F32), axis=0)
        g_down = tn_dot(hidden, grad)
        grad_up = (nt_dot(grad, down_w) * gelu_slope(up_proj)).astype(BF16)
        g_up_b = jnp.sum(grad_up.astype(F32), axis=0)
        g_up = tn_dot(normed2, grad_up)
        grad, g_f_gain, g_f_shift = norm_back(ffn_in, f_gain, nt_dot(grad_up, up_w), grad)
        g_out_b = jnp.sum(grad.astype(F32), axis=0)
        g_out = tn_dot(mixed, grad)
        grad_mixed = nt_dot(grad, out_w).astype(BF16)
        grad_q, gk_own, gk_peer, gv_own, gv_peer = attend_back(
            queries, key_own, key_peer, value_own, value_peer, mixed, grad_mixed, probs
        )
        grad_k = (gk_own + to_peer(gk_peer).astype(F32)).astype(BF16)
        grad_v = (gv_own + to_peer(gv_peer).astype(F32)).astype(BF16)
        g_qv_b = jnp.concatenate(
            [jnp.sum(grad_q.astype(F32), axis=0), jnp.sum(grad_v.astype(F32), axis=0)]
        )
        grad_proj = jnp.concatenate([grad_q, grad_k, grad_v], axis=1)
        g_qkv = tn_dot(normed, grad_proj)
        grad, g_a_gain, g_a_shift = norm_back(attn_in, a_gain, nt_dot(grad_proj, qkv_w), grad)
        grads[l] = [
            scatter(item)
            for item in (g_a_gain, g_a_shift, g_qkv, g_qv_b, g_out, g_out_b, g_f_gain, g_f_shift,
                         g_up, g_up_b, g_down, g_down_b)
        ]
    grad_tokens = redistribute(grad)
    return (encoded, grad_tokens) + tuple(jnp.stack(pair) for pair in zip(*grads))


def solution(mesh):
    flat, rows4 = P(None, "dp"), P(None, "dp", None, None)
    mat, spread = P(None, "dp", None), P(None, "dp", "section", None)
    in_specs = (
        rows4, flat, rows4, flat, flat, mat, flat, mat, flat, flat, flat, mat, flat, mat, flat,
    )
    out_specs = (
        spread, spread, flat, flat, mat, flat, mat, flat, flat, flat, mat, flat, mat, flat,
    )
    return jax.shard_map(local, mesh=mesh, in_specs=in_specs, out_specs=out_specs, check_vma=False)
```

```python
from functools import partial
import math

import jax
import jax.numpy as jnp
from jax import lax
from jax.experimental import pallas as pl
from jax.experimental.pallas import tpu as pltpu
from jax.sharding import PartitionSpec as P

HEAD = 64
PAIR = 2 * HEAD
NORM_EPS = 1e-05
MASK_FLOOR = -1e30
F32 = jnp.float32
BF16 = jnp.bfloat16
VMEM_ROOM = 56 << 20
WHOLE = pl.BlockSpec(memory_space=pltpu.VMEM)
PLACED = pl.BlockSpec(memory_space=pl.ANY)


def nt_dot(left, right):
    return lax.dot_general(left, right, (((1,), (1,)), ((), ())), preferred_element_type=F32)


def nn_dot(left, right):
    return jnp.dot(left, right, preferred_element_type=F32)


def tn_dot(left, right):
    return lax.dot_general(left, right, (((0,), (0,)), ((), ())), preferred_element_type=F32)


def lasting(micros):
    return pl.CostEstimate(flops=micros << 28, transcendentals=0, bytes_accessed=1 << 16)


def struct(shape, kind):
    return jax.ShapeDtypeStruct(shape, kind)


def call(body, outs, operands, placed=(), scratch=(), micros=2, out_placed=()):
    return pl.pallas_call(
        body,
        in_specs=[PLACED if n in placed else WHOLE for n in range(len(operands))],
        out_specs=[PLACED if n in out_placed else WHOLE for n in range(len(outs))],
        out_shape=outs,
        scratch_shapes=list(scratch),
        compiler_params=pltpu.CompilerParams(vmem_limit_bytes=VMEM_ROOM),
        cost_estimate=lasting(micros),
    )(*operands)


def start_copy(src, dst, sem):
    copy = pltpu.make_async_copy(src, dst, sem)
    copy.start()
    return copy


def head_lanes(block, head):
    lane = lax.broadcasted_iota(jnp.int32, block.shape, 1)
    keep = (lane < HEAD) if head == 0 else (lane >= HEAD)
    return jnp.where(keep, block, jnp.zeros_like(block))


def attend_kernel(lens_ref, q_ref, ko_ref, kp_ref, vo_ref, vp_ref, o_ref, raised_ref, scale_ref):
    rows = q_ref.shape[0]
    score_scale = 1.0 / math.sqrt(HEAD)
    query_pair = q_ref[...] * jnp.asarray(score_scale, BF16)
    value_t = [vo_ref[...].T, vp_ref[...].T]
    mixed, scales = [], []
    for head in range(2):
        query = head_lanes(query_pair, head)
        scores = []
        for part, key_ref in enumerate((ko_ref, kp_ref)):
            part_scores = nt_dot(key_ref[...], query)
            key_row = lax.broadcasted_iota(jnp.int32, part_scores.shape, 0)
            scores.append(jnp.where(key_row < lens_ref[part], part_scores, MASK_FLOOR))
        row_max = jnp.maximum(
            jnp.max(scores[0], axis=0, keepdims=True), jnp.max(scores[1], axis=0, keepdims=True)
        )
        total = jnp.zeros((1, rows), F32)
        head_out = jnp.zeros((HEAD, rows), F32)
        for part in range(2):
            raised = jnp.exp(scores[part] - row_max)
            total = total + jnp.sum(raised, axis=0, keepdims=True)
            low = raised.astype(BF16)
            raised_ref[head, part * rows : (part + 1) * rows, :] = low
            head_out = head_out + nn_dot(value_t[part][head * HEAD : (head + 1) * HEAD, :], low)
        inverse = 1.0 / total
        mixed.append(head_out * inverse)
        scales.append(jnp.broadcast_to(inverse, (HEAD, rows)))
    o_ref[...] = jnp.concatenate(mixed, axis=0).T.astype(BF16)
    scale_ref[...] = jnp.concatenate(scales, axis=0).T


def attend(queries, own, peer, lens):
    rows, width = queries.shape
    pairs = width // PAIR
    block = pl.BlockSpec((rows, PAIR), lambda p, lens: (0, p))
    key = pl.BlockSpec((None, rows, PAIR), lambda p, lens: (0, 0, p))
    value = pl.BlockSpec((None, rows, PAIR), lambda p, lens: (1, 0, p))
    return pl.pallas_call(
        attend_kernel,
        grid_spec=pltpu.PrefetchScalarGridSpec(
            num_scalar_prefetch=1,
            grid=(pairs,),
            in_specs=[block, key, key, value, value],
            out_specs=[
                block, pl.BlockSpec((2, 2 * rows, rows), lambda p, lens: (p, 0, 0)), block,
            ],
        ),
        out_shape=[
            struct((rows, width), BF16), struct((2 * pairs, 2 * rows, rows), BF16),
            struct((rows, width), F32),
        ],
        compiler_params=pltpu.CompilerParams(vmem_limit_bytes=48 << 20),
        cost_estimate=lasting(16),
    )(lens, queries, own, peer, own, peer)


def attend_back_kernel(
    q_ref, ko_ref, kp_ref, vo_ref, vp_ref, o_ref, go_ref, raised_ref, scale_ref,
    gq_ref, own_ref, peer_ref,
):
    rows = q_ref.shape[0]
    score_scale = 1.0 / math.sqrt(HEAD)
    query_pair = q_ref[...] * jnp.asarray(score_scale, BF16)
    query_t = query_pair.T
    grad_pair = (go_ref[...].astype(F32) * scale_ref[...]).astype(BF16)
    grad_t = grad_pair.T
    inner = (o_ref[...].astype(F32) * grad_pair.astype(F32)).T
    value_refs = (vo_ref, vp_ref)
    key_t = [ko_ref[...].T, kp_ref[...].T]
    grad_key = [[], []]
    grad_value = [[], []]
    grad_query = []
    for head in range(2):
        lanes = slice(head * HEAD, (head + 1) * HEAD)
        grad_out = head_lanes(grad_pair, head)
        inner_row = jnp.sum(inner[lanes, :], axis=0, keepdims=True)
        head_query = jnp.zeros((HEAD, rows), F32)
        for part in range(2):
            raised = raised_ref[head, part * rows : (part + 1) * rows, :]
            grad_prob = nt_dot(value_refs[part][...], grad_out)
            grad_score = (raised.astype(F32) * (grad_prob - inner_row)).astype(BF16)
            grad_value[part].append(nt_dot(grad_t[lanes, :], raised))
            grad_key[part].append(nt_dot(query_t[lanes, :], grad_score))
            head_query = head_query + nn_dot(key_t[part][lanes, :], grad_score)
        grad_query.append(head_query * score_scale)
    gq_ref[...] = jnp.concatenate(grad_query, axis=0).T.astype(BF16)
    for n, grads in enumerate((grad_key, grad_value)):
        own_ref[n] = jnp.concatenate(grads[0], axis=0).T
        peer_ref[n] = jnp.concatenate(grads[1], axis=0).T.astype(BF16)


def attend_back(queries, own, peer, mixed, grad_mixed, raised, scale):
    rows, width = queries.shape
    pairs = width // PAIR
    block = pl.BlockSpec((rows, PAIR), lambda p: (0, p))
    key = pl.BlockSpec((None, rows, PAIR), lambda p: (0, 0, p))
    value = pl.BlockSpec((None, rows, PAIR), lambda p: (1, 0, p))
    both = pl.BlockSpec((2, rows, PAIR), lambda p: (0, 0, p))
    low, full = struct((rows, width), BF16), struct((2, rows, width), F32)
    sent = struct((2, rows, width), BF16)
    return pl.pallas_call(
        attend_back_kernel,
        grid=(pairs,),
        in_specs=[
            block, key, key, value, value, block, block,
            pl.BlockSpec((2, 2 * rows, rows), lambda p: (p, 0, 0)), block,
        ],
        out_specs=[block, both, both],
        out_shape=[low, full, sent],
        compiler_params=pltpu.CompilerParams(vmem_limit_bytes=48 << 20),
        cost_estimate=lasting(16),
    )(queries, own, peer, own, peer, mixed, grad_mixed, raised, scale)


def norm_unit(stream):
    center = stream - jnp.mean(stream, axis=-1, keepdims=True)
    spread = jnp.mean(center * center, axis=-1, keepdims=True)
    root = lax.rsqrt(spread + NORM_EPS)
    return center * root, root


def norm_back(stream, gain, grad_normed, grad_low):
    unit, root = norm_unit(stream)
    grad_gain = jnp.sum(grad_normed * unit, axis=0, keepdims=True)
    grad_shift = jnp.sum(grad_normed, axis=0, keepdims=True)
    grad_unit = grad_normed * gain
    grad_stream = root * (
        grad_unit
        - jnp.mean(grad_unit, axis=-1, keepdims=True)
        - unit * jnp.mean(grad_unit * unit, axis=-1, keepdims=True)
    )
    return (grad_low.astype(F32) + grad_stream).astype(BF16), grad_gain, grad_shift


def block_ref(refs, n, which):
    if len(refs) == 2:
        return refs[n % 2].at[which, n // 2]
    return refs[0].at[:, jnp.bitwise_xor(lax.axis_index("section"), n), which]


def start_section(refs, which, wanted, dst_refs, sems):
    here = lax.axis_index("section")
    waits = []
    for slot, block in enumerate(wanted):
        if len(refs) == 1:
            waits.append(start_copy(refs[0].at[:, block, which], dst_refs.at[slot], sems.at[slot]))
            continue
        place = jnp.bitwise_xor(here, block)
        for n in range(4):
            @pl.when(place == n)
            def _():
                start_copy(block_ref(refs, n, which), dst_refs.at[slot], sems.at[slot])
        waits.append(
            pltpu.make_async_copy(block_ref(refs, 0, which), dst_refs.at[slot], sems.at[slot])
        )
    return waits


def block_shape(blocks):
    shape = blocks[0].shape
    return shape[-3:] if len(blocks) == 2 else shape[:1] + shape[-2:]


def square(block):
    return block.reshape(block.shape[-3] * block.shape[-2], block.shape[-1])


def qkv_kernel(which, count, h_ref, vec_ref, *refs):
    blocks = refs[:count]
    a_hbm, q_hbm, kv_hbm, mat, a_ref, q_ref, kv_ref, sems, outs = refs[count:]
    waits = start_section(blocks, which, (1, 2, 0), mat, sems)
    unit, _ = norm_unit(h_ref[...].astype(F32))
    normed = (unit * vec_ref[0:1, :] + vec_ref[1:2, :]).astype(BF16)
    a_ref[...] = normed
    copies = [start_copy(a_ref, a_hbm, outs.at[0])]
    waits[0].wait()
    kv_ref[0] = nn_dot(normed, square(mat[0])).astype(BF16)
    copies.append(start_copy(kv_ref.at[0], kv_hbm.at[0], outs.at[1]))
    waits[1].wait()
    kv_ref[1] = (nn_dot(normed, square(mat[1])) + vec_ref[3:4, :]).astype(BF16)
    copies.append(start_copy(kv_ref.at[1], kv_hbm.at[1], outs.at[2]))
    waits[2].wait()
    q_ref[...] = (nn_dot(normed, square(mat[2])) + vec_ref[2:3, :]).astype(BF16)
    copies.append(start_copy(q_ref, q_hbm, outs.at[3]))
    for item in copies:
        item.wait()


def qkv_part(stream, vec, attn):
    rows, width = stream.shape
    blocks, which = attn
    low, both = struct((rows, width), BF16), struct((2, rows, width), BF16)
    return call(
        partial(qkv_kernel, which, len(blocks)), [low, low, both], (stream, vec, *blocks), (2, 3),
        (
            pltpu.VMEM((3,) + block_shape(blocks), BF16), pltpu.VMEM(low.shape, BF16),
            pltpu.VMEM(low.shape, BF16), pltpu.VMEM(both.shape, BF16),
            pltpu.SemaphoreType.DMA((3,)), pltpu.SemaphoreType.DMA((4,)),
        ), micros=5, out_placed=(0, 1, 2),
    )


def out_kernel(which, count, h_ref, o_ref, vec_ref, *refs):
    y_ref, mat, sems = refs[count:]
    start_section(refs[:count], which, (3,), mat, sems)[0].wait()
    y_ref[...] = (
        h_ref[...].astype(F32) + nn_dot(o_ref[...], square(mat[0])) + vec_ref[4:5, :]
    ).astype(BF16)


def out_part(stream, mixed, vec, attn):
    rows, width = stream.shape
    blocks, which = attn
    return call(
        partial(out_kernel, which, len(blocks)), [struct((rows, width), BF16)],
        (stream, mixed, vec, *blocks), (3, 4),
        (pltpu.VMEM((1,) + block_shape(blocks), BF16), pltpu.SemaphoreType.DMA((1,))), micros=4,
    )[0]


def up_kernel(which, count, h_ref, vec_ref, *refs):
    a_ref, g_hbm, slope_hbm, mat, g_ref, slope_ref, sems, outs = refs[count:]
    here = lax.axis_index("section")
    waits = [
        start_copy(block_ref(refs[:count], n, which), mat.at[n], sems.at[n]) for n in range(4)
    ]
    unit, _ = norm_unit(h_ref[...].astype(F32))
    normed = (unit * vec_ref[5:6, :] + vec_ref[6:7, :]).astype(BF16)
    a_ref[...] = normed
    copies = []
    for n in range(4):
        waits[n].wait()
        bias = vec_ref[pl.ds(7 + jnp.bitwise_xor(here, n), 1), :]
        up_proj = nn_dot(normed, square(mat[n])) + bias
        below = 0.5 * (1.0 + lax.erf(up_proj * math.sqrt(0.5)))
        bell = jnp.exp(-0.5 * up_proj * up_proj) * (1.0 / math.sqrt(2.0 * math.pi))
        g_ref[n] = (up_proj * below).astype(BF16)
        slope_ref[n] = (below + up_proj * bell).astype(BF16)
        copies.append(start_copy(g_ref.at[n], g_hbm.at[n], outs.at[0, n]))
        copies.append(start_copy(slope_ref.at[n], slope_hbm.at[n], outs.at[1, n]))
    for item in copies:
        item.wait()


def up_part(stream, vec, ups):
    rows, width = stream.shape
    wide = struct((4, rows, width), BF16)
    blocks, which = ups
    return call(
        partial(up_kernel, which, len(blocks)), [struct((rows, width), BF16), wide, wide],
        (stream, vec, *blocks), (2, 3),
        (
            pltpu.VMEM((4,) + block_shape(blocks), BF16), pltpu.VMEM(wide.shape, BF16),
            pltpu.VMEM(wide.shape, BF16), pltpu.SemaphoreType.DMA((4,)),
            pltpu.SemaphoreType.DMA((2, 4)),
        ), micros=9, out_placed=(1, 2),
    )


def start_down(refs, which, n, mat, sems):
    here = lax.axis_index("section")
    size = mat.shape[1] // 8
    waits = []
    for side in range(2):
        owner = 2 * jnp.bitwise_xor(here, n) + side
        for k in range(4):
            if len(refs) == 1:
                src, start = refs[0].at[owner, k, which], (side * 4 + k) * size
            else:
                src = block_ref(refs, k, which).at[owner]
                start = side * 4 * size + jnp.bitwise_xor(here, k) * size
            waits.append(
                start_copy(
                    src, mat.at[n, pl.ds(pl.multiple_of(start, size), size)],
                    sems.at[n, 2 * k + side],
                )
            )
    return waits


def down_kernel(which, count, h_ref, g_hbm, vec_ref, *refs):
    y_ref, mat, g_ref, sems, g_sems = refs[count:]
    waits = []
    for n in range(4):
        found = start_down(refs[:count], which, n, mat, sems)
        waits.append(found + [start_copy(g_hbm.at[n], g_ref.at[n], g_sems.at[n])])
    total = h_ref[...].astype(F32) + vec_ref[11:12, :]
    for n in range(4):
        for item in waits[n]:
            item.wait()
        total = total + nn_dot(g_ref[n], mat[n])
    y_ref[...] = total.astype(BF16)


def down_part(stream, hidden, vec, downs):
    rows, width = stream.shape
    blocks, which = downs
    return call(
        partial(down_kernel, which, len(blocks)), [struct((rows, width), BF16)],
        (stream, hidden, vec, *blocks), (1, 3, 4),
        (
            pltpu.VMEM((4, width, width), BF16), pltpu.VMEM((4, rows, width), BF16),
            pltpu.SemaphoreType.DMA((4, 8)), pltpu.SemaphoreType.DMA((4,)),
        ), micros=6,
    )[0]


def ffn_back_kernel(
    places, counts, gy_ref, h_ref, a_ref, g_hbm, slope_hbm, vec_ref, *refs
):
    (up_at, down_at, attn_at), (up_count, down_count, attn_count) = places, counts
    up_refs, refs = refs[:up_count], refs[up_count:]
    down_refs, refs = refs[:down_count], refs[down_count:]
    attn_refs, refs = refs[:attn_count], refs[attn_count:]
    (
        gh_ref, go_ref, keep_hbm, send_hbm, vg_ref,
        g_ref, slope_ref, mat, up_mat, out_mat, up_grad, down_grad,
        in_sems, sems, out_sems, up_sems, down_sems,
    ) = refs
    here = lax.axis_index("section")
    size, width = keep_hbm.shape[-2:]
    waits = []
    for n in range(4):
        found = start_down(down_refs, down_at, n, mat, sems)
        found.append(start_copy(slope_hbm.at[n], slope_ref.at[n], in_sems.at[0, n]))
        found.append(start_copy(g_hbm.at[n], g_ref.at[n], in_sems.at[1, n]))
        found.append(
            start_copy(block_ref(up_refs, n, up_at), up_mat.at[n], in_sems.at[2, n])
        )
        waits.append(found)
    out_wait = start_section(attn_refs, attn_at, (3,), out_mat, out_sems)[0]
    grad = gy_ref[...]
    normed = a_ref[...]
    vg_ref[...] = jnp.zeros_like(vg_ref)
    vg_ref[6:7, :] = jnp.sum(grad.astype(F32), axis=0, keepdims=True)
    grad_normed = None
    copies = []
    for n in range(4):
        for item in waits[n]:
            item.wait()
        block = jnp.bitwise_xor(here, n)
        grad_up = nt_dot(grad, mat[n]) * slope_ref[n].astype(F32)
        grad_up = grad_up.astype(BF16)
        vg_ref[pl.ds(2 + block, 1), :] = jnp.sum(grad_up.astype(F32), axis=0, keepdims=True)
        up_grad[n] = tn_dot(normed, grad_up).astype(BF16).reshape(8, size, width)
        out = keep_hbm if n in (0, 2) else send_hbm
        copies.append(start_copy(up_grad.at[n], out.at[n // 2, 0], up_sems.at[n]))
        down_grad[n] = tn_dot(g_ref[n], grad).astype(BF16).reshape(8, size, width)
        for j in range(4):
            place = jnp.bitwise_xor(here, j)
            for side in range(2):
                src, sem = down_grad.at[n, 4 * side + j], down_sems.at[n, 4 * side + j]

                @pl.when(place % 2 == 0)
                def _():
                    start_copy(src, keep_hbm.at[place // 2, 1, 2 * block + side], sem)

                @pl.when(place % 2 == 1)
                def _():
                    start_copy(src, send_hbm.at[place // 2, 1, 2 * block + side], sem)

                copies.append(pltpu.make_async_copy(src, keep_hbm.at[0, 1, 0], sem))
        term = nt_dot(grad_up, square(up_mat[n]))
        grad_normed = term if n == 0 else grad_normed + term
    grad_in, grad_gain, grad_shift = norm_back(
        h_ref[...].astype(F32), vec_ref[5:6, :], grad_normed, grad
    )
    gh_ref[...] = grad_in
    vg_ref[0:1, :] = grad_gain
    vg_ref[1:2, :] = grad_shift
    out_wait.wait()
    go_ref[...] = nt_dot(grad_in, square(out_mat[0])).astype(BF16)
    for item in copies:
        item.wait()


def ffn_back(grad, stream, normed, hidden, slope, vec, ups, downs, attn):
    rows, width = grad.shape
    sets = (ups, downs, attn)
    counts, places = tuple(len(item[0]) for item in sets), tuple(item[1] for item in sets)
    blocks = [ref for item in sets for ref in item[0]]
    block = block_shape(ups[0])
    part = struct((2, 2) + block, BF16)
    low = struct((rows, width), BF16)
    dma = pltpu.SemaphoreType.DMA
    return call(
        partial(ffn_back_kernel, places, counts),
        [low, low, part, part, struct((8, width), F32)],
        (grad, stream, normed, hidden, slope, vec, *blocks),
        (3, 4, *range(6, 6 + len(blocks))),
        (
            pltpu.VMEM((4, rows, width), BF16), pltpu.VMEM((4, rows, width), BF16),
            pltpu.VMEM((4, width, width), BF16), pltpu.VMEM((4,) + block, BF16),
            pltpu.VMEM((1,) + block, BF16), pltpu.VMEM((4,) + block, BF16),
            pltpu.VMEM((4,) + block, BF16), dma((3, 4)), dma((4, 8)), dma((1,)), dma((4,)),
            dma((4, 8)),
        ), micros=20, out_placed=(2, 3),
    )


def qkv_back_kernel(
    which, count, gy_ref, h_ref, a_ref, o_ref, gq_ref, own_hbm, got_ref, vec_ref, *refs
):
    gh_ref, keep_hbm, send_hbm, vg_ref, mat, own_ref, term, sems, own_sems, out_sems = refs[count:]
    waits = start_section(refs[:count], which, (0, 1, 2), mat, sems)
    own_waits = [start_copy(own_hbm.at[n], own_ref.at[n], own_sems.at[n]) for n in range(2)]
    here = lax.axis_index("section")
    grad = gy_ref[...]
    normed = a_ref[...]
    vg_ref[...] = jnp.zeros_like(vg_ref)
    copies = []

    def give(block, left, right):
        term[block] = tn_dot(left, right).astype(BF16).reshape(term.shape[1:])
        place = jnp.bitwise_xor(here, block)

        @pl.when(place % 2 == 0)
        def _():
            start_copy(term.at[block], keep_hbm.at[place // 2, 0], out_sems.at[block])

        @pl.when(place % 2 == 1)
        def _():
            start_copy(term.at[block], send_hbm.at[place // 2, 0], out_sems.at[block])

        copies.append(pltpu.make_async_copy(term.at[block], keep_hbm.at[0, 0], out_sems.at[block]))

    vg_ref[4:5, :] = jnp.sum(grad.astype(F32), axis=0, keepdims=True)
    give(3, o_ref[...], grad)
    grad_q = gq_ref[...]
    vg_ref[2:3, :] = jnp.sum(grad_q.astype(F32), axis=0, keepdims=True)
    give(0, normed, grad_q)
    own_waits[0].wait()
    grad_k = (own_ref[0] + got_ref[0].astype(F32)).astype(BF16)
    give(1, normed, grad_k)
    own_waits[1].wait()
    grad_v = (own_ref[1] + got_ref[1].astype(F32)).astype(BF16)
    vg_ref[3:4, :] = jnp.sum(grad_v.astype(F32), axis=0, keepdims=True)
    give(2, normed, grad_v)
    for item in waits:
        item.wait()
    grad_normed = (
        nt_dot(grad_q, square(mat[0])) + nt_dot(grad_k, square(mat[1])) + nt_dot(grad_v, square(mat[2]))
    )
    gh_ref[...], grad_gain, grad_shift = norm_back(
        h_ref[...].astype(F32), vec_ref[0:1, :], grad_normed, grad
    )
    vg_ref[0:1, :] = grad_gain
    vg_ref[1:2, :] = grad_shift
    for item in copies:
        item.wait()


def qkv_back(grad, stream, normed, mixed, parts, vec, attn):
    rows, width = grad.shape
    blocks, which = attn
    block = block_shape(blocks)
    part = struct((2, 1) + block, BF16)
    dma = pltpu.SemaphoreType.DMA
    return call(
        partial(qkv_back_kernel, which, len(blocks)),
        [struct((rows, width), BF16), part, part, struct((8, width), F32)],
        (grad, stream, normed, mixed, *parts, vec, *blocks),
        (5, *range(8, 8 + len(blocks))),
        (
            pltpu.VMEM((3,) + block, BF16), pltpu.VMEM((2, rows, width), F32),
            pltpu.VMEM((4,) + block, BF16), dma((3,)), dma((2,)), dma((4,)),
        ), micros=10, out_placed=(1, 2),
    )


def over(block, axis, move):
    count = lax.axis_size(axis)
    return lax.ppermute(block, axis, [(i, move(i)) for i in range(count)])


def to_core(block):
    return over(block, "section", lambda i: i ^ 1)


def to_x(block):
    return over(block, "section", lambda i: i ^ 2)


def to_y(block):
    return over(block, "dp", lambda i: i ^ 1)


def to_z(block, steps):
    return over(block, "dp", lambda i: (i + 2 * steps) % 8)


ALONG = [[0, 2, 4, 6], [1, 3, 5, 7]]


def gather_along(block):
    return lax.all_gather(block, "dp", axis=0, axis_index_groups=ALONG)


def all_z(block):
    return tuple(to_z(block, k) for k in (1, 2, 3))


class Line:
    def __init__(self, start):
        self.token = start

    def fence(self, arrays):
        *arrays, self.token = lax.optimization_barrier(tuple(arrays) + (self.token,))
        return arrays

    def run(self, body, *operands):
        flat, shape = jax.tree.flatten(operands)
        arrays = self.fence([item for item in flat if not isinstance(item, int)])
        flat = [item if isinstance(item, int) else arrays.pop(0) for item in flat]
        flat, shape = jax.tree.flatten(body(*jax.tree.unflatten(shape, flat)))
        return jax.tree.unflatten(shape, self.fence(flat))


def pick_kernel(
    qkv_ref, out_ref, up_ref, down_ref, again, ashift, qvb, outb, fgain, fshift, upb, downb,
    a1, f1, rest, ride,
):
    size, width = f1.shape[1:]
    here = lax.axis_index("section")
    group = lax.axis_index("dp")
    ride[...] = jnp.zeros_like(ride)
    for i in range(8):
        @pl.when(group == i)
        def _():
            for l in range(2):
                def put(row, start, ref):
                    wide = ref.shape[1]
                    at = slice(start % width, start % width + wide)
                    ride[16 * l + row : 16 * l + row + 1, at] = ref[l : l + 1, :].astype(F32)

                put(0, size * i, again)
                put(1, size * i, ashift)
                put(2 + 2 * size * i // width, 2 * size * i, qvb)
                put(4, size * i, outb)
                put(5, size * i, fgain)
                put(6, size * i, fshift)
                put(7 + 4 * size * i // width, 4 * size * i, upb)
                put(11, size * i, downb)

    a1[size:] = ride[...].astype(BF16)
    for m in range(4):
        @pl.when(here == m)
        def _():
            for l in range(2):
                attn = qkv_ref[l, :, m * width : (m + 1) * width] if m < 3 else out_ref[l]
                ffn = f1 if l == 0 else rest
                ffn[0] = up_ref[l, :, m * width : (m + 1) * width]
                ffn[1] = down_ref[l, m * size : (m + 1) * size]
                if l == 0:
                    a1[:size] = attn
                else:
                    rest[2] = attn


def pick_blocks(*operands):
    size = operands[0].shape[1]
    width = operands[1].shape[2]
    return call(
        pick_kernel,
        [
            struct((size + 32, width), BF16), struct((2, size, width), BF16),
            struct((3, size, width), BF16),
        ],
        operands, (), (pltpu.VMEM((32, width), F32),), micros=4,
    )


def split_kernel(near_ref, *out_refs):
    at = 0
    for left_ref, right_ref in zip(out_refs[::2], out_refs[1::2]):
        count, wide = left_ref.shape[1], left_ref.shape[-1]
        left_ref[...] = near_ref[:, at : at + count, :, :wide]
        right_ref[...] = near_ref[:, at : at + count, :, wide:]
        at += count


def split_near(near, counts):
    size, width = near.shape[2:]
    outs = []
    for count in counts:
        outs += [struct((4, count, size, width // 2), BF16)] * 2
    return call(split_kernel, outs, (near,))


def middle_kernel(left_ref, left_got, right_ref, right_got, x_ref, y_ref):
    side = lax.axis_index("dp") % 2
    for along in range(4):
        x_ref[2 * along + side] = left_ref[along]
        x_ref[2 * along + 1 - side] = left_got[along]
    y_ref[0] = right_ref[...]
    y_ref[1] = right_got[...]


def middle(left, left_got, right, right_got):
    part = left.shape[1:]
    return call(
        middle_kernel, [struct((8,) + part, BF16), struct((2, 4) + part, BF16)],
        (left, left_got, right, right_got), micros=60,
    )


def whole_kernel(x_ref, x_got, y_ref, y_got, out_ref, *ride_refs):
    side = lax.axis_index("dp") % 2
    count, size, wide = out_ref.shape[0], out_ref.shape[3], x_ref.shape[3]
    for c in range(count):
        for n, ref in enumerate((x_ref, x_got)):
            out_ref[c, n, :, :, :wide] = ref[:, c, :size]
            for along in range(4):
                out_ref[c, n, 2 * along + side, :, wide:] = y_ref[n, along, c, :size]
                out_ref[c, n, 2 * along + 1 - side, :, wide:] = y_got[n, along, c, :size]
    if ride_refs:
        vec_ref = ride_refs[0]
        left = jnp.sum(x_ref[:, 0, size:].astype(F32), axis=0)
        right = jnp.sum(y_ref[0, :, 0, size:].astype(F32), axis=0)
        right = right + jnp.sum(y_got[0, :, 0, size:].astype(F32), axis=0)
        for l in range(2):
            vec_ref[l, :, :wide] = left[16 * l : 16 * l + 16]
            vec_ref[l, :, wide:] = right[16 * l : 16 * l + 16]


def whole_blocks(x_send, x_got, y_send, y_got, size):
    _, count, full, wide = x_send.shape
    outs = [struct((count, 2, 8, size, 2 * wide), BF16)]
    if full > size:
        outs.append(struct((2, 16, 2 * wide), F32))
    return call(whole_kernel, outs, (x_send, x_got, y_send, y_got))


class Gather:
    def __init__(self, line, left, right, size):
        self.line, self.left, self.right, self.size = line, left, right, size
        self.left_got, self.right_got = to_y(left), to_x(right)

    def middle(self):
        self.x_send, self.y_send = self.line.run(
            middle, self.left, self.left_got, self.right, self.right_got
        )
        self.x_got, self.y_got = to_x(self.x_send), to_y(self.y_send)

    def whole(self):
        found = self.line.run(
            lambda *items: whole_blocks(*items, self.size),
            self.x_send, self.x_got, self.y_send, self.y_got,
        )
        self.pair = (found[0], to_core(found[0]))
        return found[1:]


def first_kernel(keep_ref, got_ref, x_ref, y_ref, left_ref, right_ref):
    wide = x_ref.shape[-1]
    side = lax.axis_index("dp") % 2
    for c in range(keep_ref.shape[1]):
        for n, ref in enumerate((left_ref, x_ref)):
            ref[c] = (
                keep_ref[n, c, :, :, :wide].astype(F32) + got_ref[n, c, :, :, :wide].astype(F32)
            ).astype(BF16)
        for n in range(2):
            for along in range(4):
                for ref, pick in ((right_ref, side), (y_ref, 1 - side)):
                    at = 2 * along + pick
                    ref[n, c, along] = (
                        keep_ref[n, c, at, :, wide:].astype(F32)
                        + got_ref[n, c, at, :, wide:].astype(F32)
                    ).astype(BF16)


def add_first(keep, got):
    _, count, _, size, width = keep.shape
    x_part = struct((count, 8, size, width // 2), BF16)
    y_part = struct((2, count, 4, size, width // 2), BF16)
    return call(first_kernel, [x_part, y_part, x_part, y_part], (keep, got), micros=5)


def both_kernel(keep_ref, got_ref, out_ref):
    out_ref[0] = (
        keep_ref[:, :, 0].astype(F32) + got_ref[:, :, 0].astype(F32)
    ).astype(BF16)


def add_both(keep, got):
    _, count, parts, size, width = keep.shape
    spec = pl.BlockSpec((2, count, 1, size, width), lambda i: (0, 0, i, 0, 0))
    return pl.pallas_call(
        both_kernel,
        grid=(parts,),
        in_specs=[spec, spec],
        out_specs=pl.BlockSpec((1, 2, count, size, width), lambda i: (i, 0, 0, 0, 0)),
        out_shape=struct((parts, 2, count, size, width), BF16),
        compiler_params=pltpu.CompilerParams(vmem_limit_bytes=VMEM_ROOM),
        cost_estimate=lasting(60),
    )(keep, got)


def scatter_both(block):
    return lax.psum_scatter(block, "dp", scatter_dimension=0, tiled=True)[0]


def second_kernel(left_ref, x_got, right_ref, y_got, y_ref, x_ref, near_ref, rest_ref):
    side = lax.axis_index("dp") % 2
    for c in range(left_ref.shape[0]):
        for along in range(4):
            for ref, pick in ((near_ref, side), (y_ref, 1 - side)):
                at = 2 * along + pick
                ref[c, along] = (
                    left_ref[c, at].astype(F32) + x_got[c, at].astype(F32)
                ).astype(BF16)
        for n, ref in enumerate((rest_ref, x_ref)):
            ref[c] = (right_ref[n, c].astype(F32) + y_got[n, c].astype(F32)).astype(BF16)


def add_second(left, x_got, right, y_got):
    part = struct(right.shape[1:], BF16)
    return call(second_kernel, [part] * 4, (left, x_got, right, y_got), micros=120)


def third_kernel(near_ref, y_got, rest_ref, x_got, out_ref):
    wide = near_ref.shape[-1]
    for c in range(near_ref.shape[0]):
        for along in range(4):
            out_ref[along, c, :, :wide] = (
                near_ref[c, along].astype(F32) + y_got[c, along].astype(F32)
            ).astype(BF16)
            out_ref[along, c, :, wide:] = (
                rest_ref[c, along].astype(F32) + x_got[c, along].astype(F32)
            ).astype(BF16)


def add_third(near, y_got, rest, x_got):
    count, _, size, wide = near.shape
    return call(
        third_kernel, [struct((4, count, size, 2 * wide), BF16)], (near, y_got, rest, x_got),
        micros=60,
    )[0]


def split_kernel_back(near_ref, y_got, rest_ref, x_got, o0, o1, o2, o3):
    along = lax.axis_index("dp") // 2
    wide = near_ref.shape[-1]
    for c in range(near_ref.shape[0]):
        for k, ref in enumerate((o0, o1, o2, o3)):
            pick = lax.rem(along + k, 4)
            ref[c, :, :wide] = (
                near_ref[c, pick].astype(F32) + y_got[c, pick].astype(F32)
            ).astype(BF16)
            ref[c, :, wide:] = (
                rest_ref[c, pick].astype(F32) + x_got[c, pick].astype(F32)
            ).astype(BF16)


def add_third_split(near, y_got, rest, x_got):
    count, _, size, wide = near.shape
    part = struct((count, size, 2 * wide), BF16)
    return call(split_kernel_back, [part] * 4, (near, y_got, rest, x_got), micros=60)


def last_kernel(o0, o1, o2, o3, out_ref):
    out_ref[...] = (
        o0[...].astype(F32) + o1[...].astype(F32) + o2[...].astype(F32) + o3[...].astype(F32)
    ).astype(BF16)


def add_last(*parts):
    return call(last_kernel, [struct(parts[0].shape, BF16)], parts)[0]


def across(own):
    far = to_x(own)
    return own, to_core(own), far, to_core(far)


class Reduce:
    def __init__(self, line, x_send, y_send, left, right):
        self.line, self.left, self.right = line, left, right
        self.x_got, self.y_got = to_x(x_send), to_y(y_send)

    def second(self):
        y_send, x_send, self.near, self.rest = self.line.run(
            add_second, self.left, self.x_got, self.right, self.y_got
        )
        self.y_got, self.x_got = to_y(y_send), to_x(x_send)

    def third(self):
        whole = self.line.run(add_third, self.near, self.y_got, self.rest, self.x_got)
        self.shard = lax.psum_scatter(
            whole, "dp", scatter_dimension=0, tiled=True, axis_index_groups=ALONG
        )[0]

    def third_split(self):
        self.parts = self.line.run(
            add_third_split, self.near, self.y_got, self.rest, self.x_got
        )
        self.z_got = [to_z(self.parts[k], k) for k in (1, 2, 3)]

    def last(self):
        self.shard = self.line.run(add_last, self.parts[0], *self.z_got)


def finish_kernel(*refs):
    attn, ffn, (rest_ref, qkv_ref, out_ref, up_ref, down_ref) = refs[:4], refs[4:8], refs[8:]
    here = lax.axis_index("section")
    size, width = rest_ref.shape[-2:]

    def put(l, b, found):
        if b < 3:
            qkv_ref[l, :, b * width : (b + 1) * width] = found.astype(F32)
        else:
            out_ref[l] = found.astype(F32)

    def put_ffn(l, b, ups, downs):
        up_ref[l, :, b * width : (b + 1) * width] = ups.astype(F32)
        down_ref[l, b * size : (b + 1) * size] = downs.astype(F32)

    for m in range(4):
        @pl.when(here == m)
        def _():
            for b in range(4):
                put(0, b, attn[m ^ b][0])
                put_ffn(0, b, ffn[m ^ b][0], ffn[m ^ b][1])

    for b in range(4):
        put(1, b, rest_ref[b, 2])
        put_ffn(1, b, rest_ref[b, 0], rest_ref[b, 1])


def finish(*held):
    _, size, width = held[0].shape
    return call(
        finish_kernel,
        [
            struct((2, size, 3 * width), F32), struct((2, size, width), F32),
            struct((2, size, 4 * width), F32), struct((2, 4 * size, width), F32),
        ],
        held, micros=5,
    )


def pick_row(stacked, index):
    return lax.dynamic_index_in_dim(stacked, index, 0, keepdims=False)


def local(
    tokens, lengths, cotangent, attn_gain, attn_shift, qkv_weight, qv_bias, out_weight, out_bias,
    ffn_gain, ffn_shift, up_weight, up_bias, down_weight, down_bias,
):
    layers, size, width3 = qkv_weight.shape
    width = width3 // 3
    eighth = width // 8
    micro_count, cell_count, seq_len, _ = tokens.shape
    section_id = lax.axis_index("section")
    section_count = lax.axis_size("section")
    group = lax.axis_size("dp")
    dp_id = lax.axis_index("dp")
    share = section_count // micro_count
    assert cell_count == 1 and share == 2 and section_count == 4 and layers == 2
    cell = section_id // share
    half = section_id % share
    rows = seq_len // share
    direct = group == 8
    line = Line(jnp.zeros((1, 1), F32))

    def mine(stacked):
        return lax.dynamic_slice(
            stacked, (cell, 0, half * rows, 0), (1, 1, rows, width)
        ).reshape(rows, width)

    stream = mine(tokens)
    length = lax.dynamic_slice(lengths, (cell, 0), (1, 1)).reshape(())
    lens = jnp.stack([length - half * rows, length - (1 - half) * rows])

    def attn_first(l, vec, blocks):
        normed, queries, own = line.run(qkv_part, stream, vec, blocks)
        return normed, queries, own, to_core(own)

    if direct:
        a1_block, f1_block, rest_block = line.run(
            pick_blocks, qkv_weight, out_weight, up_weight, down_weight,
            attn_gain, attn_shift, qv_bias, out_bias, ffn_gain, ffn_shift, up_bias, down_bias,
        )
        a1_near = gather_along(a1_block[None])
        f1_near = gather_along(f1_block)
        rest = lax.all_gather(rest_block, ("dp", "section"), axis=0, tiled=False)
        rest = rest.reshape(8, 4, 3, size, width)
        a1 = Gather(line, *line.run(lambda near: split_near(near, (1,)), a1_near), size)
        a1.middle()
        u1_d1 = line.run(lambda near: split_near(near, (1, 1)), f1_near)
        u1 = Gather(line, *u1_d1[:2], size)
        d1 = Gather(line, *u1_d1[2:], size)
        vecs = a1.whole()[0]
        vec1, vec2 = vecs[0], vecs[1]
        attn1 = (a1.pair, 0)
    else:
        def gather(block, axis):
            return lax.all_gather(block, "dp", axis=axis, tiled=True)

        def relative(blocks):
            found = [pick_row(blocks, section_id ^ n) for n in range(4)]
            return jnp.stack([found[0], found[2]])[None], jnp.stack([found[1], found[3]])[None]

        def attn_blocks(l):
            whole = gather(jnp.concatenate([qkv_weight[l], out_weight[l]], axis=1), 0)
            return relative(whole.reshape(8, eighth, 4, width).transpose(2, 0, 1, 3))

        def up_blocks(l):
            return relative(gather(up_weight[l], 0).reshape(8, eighth, 4, width).transpose(2, 0, 1, 3))

        def down_blocks(l):
            return relative(gather(down_weight[l], 0).reshape(8, 4, eighth, width).transpose(1, 0, 2, 3))

        def spread_vectors():
            def at(block, row_count):
                empty = jnp.zeros((layers, row_count, width), BF16)
                flat = block.shape[-1] * dp_id
                return lax.dynamic_update_slice(empty, block, (0, flat // width, flat % width))

            six = jnp.stack([attn_gain, attn_shift, out_bias, ffn_gain, ffn_shift, down_bias], axis=1)
            six = lax.dynamic_update_slice(
                jnp.zeros((layers, 6, width), BF16), six, (0, 0, dp_id * size)
            )
            qv = at(qv_bias[:, None], 2)
            ups = at(up_bias[:, None], 4)
            return jnp.concatenate(
                [six[:, :2], qv, six[:, 2:5], ups, six[:, 5:], jnp.zeros((layers, 4, width), BF16)],
                axis=1,
            )

        vecs = lax.psum(spread_vectors().astype(F32), "dp")
        vec1, vec2 = vecs[0], vecs[1]
        attn1, ups1, downs1 = [(blocks(0), 0) for blocks in (attn_blocks, up_blocks, down_blocks)]
        attn2, ups2, downs2 = [(blocks(1), 0) for blocks in (attn_blocks, up_blocks, down_blocks)]

    def redistribute_start(block):
        quarter = rows // 2
        route_a = [(2 * c + h, 2 * h + c) for c in range(2) for h in range(2)]
        route_b = [(2 * c + h, 2 * h + 1 - c) for c in range(2) for h in range(2)]
        low_half, high_half = block[:quarter], block[quarter:]
        first = cell == 0
        send_a, send_b = line.run(
            lambda low, high: (jnp.where(first, low, high), jnp.where(first, high, low)),
            low_half, high_half,
        )
        return lax.ppermute(send_a, "section", route_a), lax.ppermute(send_b, "section", route_b)

    def redistribute_end(got_a, got_b):
        even = section_id % 2 == 0
        return line.run(
            lambda a, b: jnp.stack([jnp.where(even, a, b), jnp.where(even, b, a)])[:, None],
            got_a, got_b,
        )

    attn_in1 = stream
    normed1, queries1, own1 = line.run(qkv_part, stream, vec1, attn1)
    peer1 = to_core(own1)
    if direct:
        u1.middle()
        d1.middle()
    mixed1, raised1, scale1 = line.run(attend, queries1, own1, peer1, lens)
    if direct:
        u1.whole()
        ups1 = (u1.pair, 0)
    ffn_in1 = line.run(out_part, attn_in1, mixed1, vec1, attn1)
    if direct:
        d1.whole()
        downs1 = (d1.pair, 0)
    normed2_1, hidden1, slope1 = line.run(up_part, ffn_in1, vec1, ups1)
    stream = line.run(down_part, ffn_in1, hidden1, vec1, downs1)
    attn_in2 = stream
    if direct:
        ups2, downs2, attn2 = ((rest,), 0), ((rest,), 1), ((rest,), 2)
    normed2, queries2, own2 = line.run(qkv_part, stream, vec2, attn2)
    peer2 = to_core(own2)
    mixed2, raised2, scale2 = line.run(attend, queries2, own2, peer2, lens)
    ffn_in2 = line.run(out_part, attn_in2, mixed2, vec2, attn2)
    normed2_2, hidden2, slope2 = line.run(up_part, ffn_in2, vec2, ups2)
    stream = line.run(down_part, ffn_in2, hidden2, vec2, downs2)

    encoded_got = redistribute_start(stream)
    grad = mine(cotangent)
    grad, grad_mixed, f2_keep, f2_send, f2_vec = line.run(
        ffn_back, grad, ffn_in2, normed2_2, hidden2, slope2, vec2, ups2, downs2, attn2
    )
    encoded = redistribute_end(*encoded_got)
    if direct:
        f2_got = to_core(f2_send)
    grad_q, kv_own, kv_peer = line.run(
        attend_back, queries2, own2, peer2, mixed2, grad_mixed, raised2, scale2
    )
    kv_got = to_core(kv_peer)
    if direct:
        f2_part = scatter_both(line.run(add_both, f2_keep, f2_got))
    grad, a2_keep, a2_send, a2_vec = line.run(
        qkv_back, grad, attn_in2, normed2, mixed2, (grad_q, kv_own, kv_got), vec2, attn2
    )
    if direct:
        a2_got = to_core(a2_send)
    grad, grad_mixed, f1_keep, f1_send, f1_vec = line.run(
        ffn_back, grad, ffn_in1, normed2_1, hidden1, slope1, vec1, ups1, downs1, attn1
    )
    if direct:
        f1_got = to_core(f1_send)
        a2r = Reduce(line, *line.run(add_first, a2_keep, a2_got))
    grad_q, kv_own, kv_peer = line.run(
        attend_back, queries1, own1, peer1, mixed1, grad_mixed, raised1, scale1
    )
    kv_got = to_core(kv_peer)
    if direct:
        a2r.second()
        f1r = Reduce(line, *line.run(add_first, f1_keep, f1_got))
    grad, a1_keep, a1_send, a1_vec = line.run(
        qkv_back, grad, attn_in1, normed1, mixed1, (grad_q, kv_own, kv_got), vec1, attn1
    )
    if direct:
        a1_got = to_core(a1_send)
        f1r.second()
        a2r.third()
        vec_grads = line.run(
            lambda a, b, c, d: jnp.stack([jnp.concatenate([a, b]), jnp.concatenate([c, d])]),
            a1_vec, f1_vec, a2_vec, f2_vec,
        )
        vec_all = lax.all_gather(vec_grads, ("dp", "section"), axis=0, tiled=False)
        a1r = Reduce(line, *line.run(add_first, a1_keep, a1_got))
        f1r.third_split()
        a1r.second()
        f1r.last()
        f1_held = across(f1r.shard)
        a1r.third_split()
        tokens_got = redistribute_start(grad)
        f2_far = to_x(f2_part[1])
        rest_own = line.run(
            lambda near, far, attn: jnp.concatenate([near[0] + far, attn]), f2_part, f2_far, a2r.shard
        )
        rest_held = lax.all_gather(rest_own, "section", axis=0)
        a1r.last()
        a1_held = across(a1r.shard)
        grad_tokens = redistribute_end(*tokens_got)
        total = line.run(lambda a: jnp.sum(a, axis=0), vec_all)
        g_qkv, g_out, g_up, g_down = line.run(finish, *a1_held, *f1_held, rest_held)
    else:
        grad_tokens = redistribute_end(*redistribute_start(grad))
        vec_grads = jnp.stack(
            [jnp.concatenate([a1_vec, f1_vec]), jnp.concatenate([a2_vec, f2_vec])]
        )

        def canonical(keep, send):
            blocks = jnp.stack([keep[0], send[0], keep[1], send[1]])
            return jnp.stack([pick_row(blocks, section_id ^ n) for n in range(4)])

        def scatter(whole):
            part = lax.psum_scatter(whole, "dp", scatter_dimension=0, tiled=True)
            return lax.psum(part, "section").astype(F32)

        def wide(blocks):
            return blocks.transpose(1, 2, 0, 3).reshape(width, 4 * width)

        both = [
            (canonical(a1_keep, a1_send), canonical(f1_keep, f1_send)),
            (canonical(a2_keep, a2_send), canonical(f2_keep, f2_send)),
        ]
        attn_all = jnp.stack([scatter(wide(attn[:, 0])) for attn, _ in both])
        g_qkv, g_out = attn_all[:, :, :width3], attn_all[:, :, width3:]
        g_up = jnp.stack([scatter(wide(ffn[:, 0])) for _, ffn in both])
        g_down = jnp.stack(
            [scatter(ffn[:, 1].transpose(1, 0, 2, 3).reshape(4 * width, width)) for _, ffn in both]
        )
        total = lax.psum(vec_grads, ("dp", "section"))

    total = total + line.token
    my_vec = lax.dynamic_slice_in_dim(total, dp_id * size, size, 2)
    qv = lax.dynamic_slice_in_dim(total[:, 2:4].reshape(layers, 2 * width), dp_id * 2 * size, 2 * size, 1)
    ups = lax.dynamic_slice_in_dim(total[:, 10:14].reshape(layers, 4 * width), dp_id * 4 * size, 4 * size, 1)
    return (
        encoded, grad_tokens, my_vec[:, 0], my_vec[:, 1], g_qkv, qv, g_out, my_vec[:, 4],
        my_vec[:, 8], my_vec[:, 9], g_up, ups, g_down, my_vec[:, 14],
    )


def solution(mesh):
    flat, rows4 = P(None, "dp"), P(None, "dp", None, None)
    mat, spread = P(None, "dp", None), P(None, "dp", "section", None)
    in_specs = (
        rows4, flat, rows4, flat, flat, mat, flat, mat, flat, flat, flat, mat, flat, mat, flat,
    )
    out_specs = (
        spread, spread, flat, flat, mat, flat, mat, flat, flat, flat, mat, flat, mat, flat,
    )
    return jax.shard_map(local, mesh=mesh, in_specs=in_specs, out_specs=out_specs, check_vma=False)
```

```python
from functools import partial
import math

import jax
import jax.numpy as jnp
from jax import lax
from jax.experimental import pallas as pl
from jax.experimental.pallas import tpu as pltpu
from jax.sharding import PartitionSpec as P

HEAD = 64
PAIR = 2 * HEAD
NORM_EPS = 1e-05
MASK_FLOOR = -1e30
F32 = jnp.float32
BF16 = jnp.bfloat16
VMEM_ROOM = 56 << 20
WHOLE = pl.BlockSpec(memory_space=pltpu.VMEM)
PLACED = pl.BlockSpec(memory_space=pl.ANY)


def nt_dot(left, right):
    return lax.dot_general(left, right, (((1,), (1,)), ((), ())), preferred_element_type=F32)


def nn_dot(left, right):
    return jnp.dot(left, right, preferred_element_type=F32)


def tn_dot(left, right):
    return lax.dot_general(left, right, (((0,), (0,)), ((), ())), preferred_element_type=F32)


def lasting(micros):
    return pl.CostEstimate(flops=micros << 28, transcendentals=0, bytes_accessed=1 << 16)


def struct(shape, kind):
    return jax.ShapeDtypeStruct(shape, kind)


def call(body, outs, operands, placed=(), scratch=(), micros=2, out_placed=()):
    return pl.pallas_call(
        body,
        in_specs=[PLACED if n in placed else WHOLE for n in range(len(operands))],
        out_specs=[PLACED if n in out_placed else WHOLE for n in range(len(outs))],
        out_shape=outs,
        scratch_shapes=list(scratch),
        compiler_params=pltpu.CompilerParams(vmem_limit_bytes=VMEM_ROOM),
        cost_estimate=lasting(micros),
    )(*operands)


def start_copy(src, dst, sem):
    copy = pltpu.make_async_copy(src, dst, sem)
    copy.start()
    return copy


def head_lanes(block, head):
    lane = lax.broadcasted_iota(jnp.int32, block.shape, 1)
    keep = (lane < HEAD) if head == 0 else (lane >= HEAD)
    return jnp.where(keep, block, jnp.zeros_like(block))


def attend_kernel(lens_ref, q_ref, ko_ref, kp_ref, vo_ref, vp_ref, o_ref, raised_ref, scale_ref):
    rows = q_ref.shape[0]
    score_scale = 1.0 / math.sqrt(HEAD)
    query_pair = q_ref[...] * jnp.asarray(score_scale, BF16)
    value_t = [vo_ref[...].T, vp_ref[...].T]
    mixed, scales = [], []
    for head in range(2):
        query = head_lanes(query_pair, head)
        scores = []
        for part, key_ref in enumerate((ko_ref, kp_ref)):
            part_scores = nt_dot(key_ref[...], query)
            key_row = lax.broadcasted_iota(jnp.int32, part_scores.shape, 0)
            scores.append(jnp.where(key_row < lens_ref[part], part_scores, MASK_FLOOR))
        row_max = jnp.maximum(
            jnp.max(scores[0], axis=0, keepdims=True), jnp.max(scores[1], axis=0, keepdims=True)
        )
        total = jnp.zeros((1, rows), F32)
        head_out = jnp.zeros((HEAD, rows), F32)
        for part in range(2):
            raised = jnp.exp(scores[part] - row_max)
            total = total + jnp.sum(raised, axis=0, keepdims=True)
            low = raised.astype(BF16)
            raised_ref[head, part * rows : (part + 1) * rows, :] = low
            head_out = head_out + nn_dot(value_t[part][head * HEAD : (head + 1) * HEAD, :], low)
        inverse = 1.0 / total
        mixed.append(head_out * inverse)
        scales.append(jnp.broadcast_to(inverse, (HEAD, rows)))
    o_ref[...] = jnp.concatenate(mixed, axis=0).T.astype(BF16)
    scale_ref[...] = jnp.concatenate(scales, axis=0).T


def attend(queries, own, peer, lens):
    rows, width = queries.shape
    pairs = width // PAIR
    block = pl.BlockSpec((rows, PAIR), lambda p, lens: (0, p))
    key = pl.BlockSpec((None, rows, PAIR), lambda p, lens: (0, 0, p))
    value = pl.BlockSpec((None, rows, PAIR), lambda p, lens: (1, 0, p))
    return pl.pallas_call(
        attend_kernel,
        grid_spec=pltpu.PrefetchScalarGridSpec(
            num_scalar_prefetch=1,
            grid=(pairs,),
            in_specs=[block, key, key, value, value],
            out_specs=[
                block, pl.BlockSpec((2, 2 * rows, rows), lambda p, lens: (p, 0, 0)), block,
            ],
        ),
        out_shape=[
            struct((rows, width), BF16), struct((2 * pairs, 2 * rows, rows), BF16),
            struct((rows, width), F32),
        ],
        compiler_params=pltpu.CompilerParams(vmem_limit_bytes=48 << 20),
        cost_estimate=lasting(16),
    )(lens, queries, own, peer, own, peer)


def attend_back_kernel(
    q_ref, ko_ref, kp_ref, vo_ref, vp_ref, o_ref, go_ref, raised_ref, scale_ref,
    gq_ref, own_ref, peer_ref,
):
    rows = q_ref.shape[0]
    score_scale = 1.0 / math.sqrt(HEAD)
    query_pair = q_ref[...] * jnp.asarray(score_scale, BF16)
    query_t = query_pair.T
    grad_pair = (go_ref[...].astype(F32) * scale_ref[...]).astype(BF16)
    grad_t = grad_pair.T
    inner = (o_ref[...].astype(F32) * grad_pair.astype(F32)).T
    value_refs = (vo_ref, vp_ref)
    key_t = [ko_ref[...].T, kp_ref[...].T]
    grad_key = [[], []]
    grad_value = [[], []]
    grad_query = []
    for head in range(2):
        lanes = slice(head * HEAD, (head + 1) * HEAD)
        grad_out = head_lanes(grad_pair, head)
        inner_row = jnp.sum(inner[lanes, :], axis=0, keepdims=True)
        head_query = jnp.zeros((HEAD, rows), F32)
        for part in range(2):
            raised = raised_ref[head, part * rows : (part + 1) * rows, :]
            grad_prob = nt_dot(value_refs[part][...], grad_out)
            grad_score = (raised.astype(F32) * (grad_prob - inner_row)).astype(BF16)
            grad_value[part].append(nt_dot(grad_t[lanes, :], raised))
            grad_key[part].append(nt_dot(query_t[lanes, :], grad_score))
            head_query = head_query + nn_dot(key_t[part][lanes, :], grad_score)
        grad_query.append(head_query * score_scale)
    gq_ref[...] = jnp.concatenate(grad_query, axis=0).T.astype(BF16)
    for n, grads in enumerate((grad_key, grad_value)):
        own_ref[n] = jnp.concatenate(grads[0], axis=0).T
        peer_ref[n] = jnp.concatenate(grads[1], axis=0).T.astype(BF16)


def attend_back(queries, own, peer, mixed, grad_mixed, raised, scale):
    rows, width = queries.shape
    pairs = width // PAIR
    block = pl.BlockSpec((rows, PAIR), lambda p: (0, p))
    key = pl.BlockSpec((None, rows, PAIR), lambda p: (0, 0, p))
    value = pl.BlockSpec((None, rows, PAIR), lambda p: (1, 0, p))
    both = pl.BlockSpec((2, rows, PAIR), lambda p: (0, 0, p))
    low, full = struct((rows, width), BF16), struct((2, rows, width), F32)
    sent = struct((2, rows, width), BF16)
    return pl.pallas_call(
        attend_back_kernel,
        grid=(pairs,),
        in_specs=[
            block, key, key, value, value, block, block,
            pl.BlockSpec((2, 2 * rows, rows), lambda p: (p, 0, 0)), block,
        ],
        out_specs=[block, both, both],
        out_shape=[low, full, sent],
        compiler_params=pltpu.CompilerParams(vmem_limit_bytes=48 << 20),
        cost_estimate=lasting(16),
    )(queries, own, peer, own, peer, mixed, grad_mixed, raised, scale)


def norm_unit(stream):
    center = stream - jnp.mean(stream, axis=-1, keepdims=True)
    spread = jnp.mean(center * center, axis=-1, keepdims=True)
    root = lax.rsqrt(spread + NORM_EPS)
    return center * root, root


def norm_back(stream, gain, grad_normed, grad_low):
    unit, root = norm_unit(stream)
    grad_gain = jnp.sum(grad_normed * unit, axis=0, keepdims=True)
    grad_shift = jnp.sum(grad_normed, axis=0, keepdims=True)
    grad_unit = grad_normed * gain
    grad_stream = root * (
        grad_unit
        - jnp.mean(grad_unit, axis=-1, keepdims=True)
        - unit * jnp.mean(grad_unit * unit, axis=-1, keepdims=True)
    )
    return (grad_low.astype(F32) + grad_stream).astype(BF16), grad_gain, grad_shift


def block_ref(refs, n, which):
    if len(refs) == 2:
        return refs[n % 2].at[which, n // 2]
    return refs[0].at[:, jnp.bitwise_xor(lax.axis_index("section"), n), which]


def start_section(refs, which, wanted, dst_refs, sems):
    here = lax.axis_index("section")
    waits = []
    for slot, block in enumerate(wanted):
        if len(refs) == 1:
            waits.append(start_copy(refs[0].at[:, block, which], dst_refs.at[slot], sems.at[slot]))
            continue
        place = jnp.bitwise_xor(here, block)
        for n in range(4):
            @pl.when(place == n)
            def _():
                start_copy(block_ref(refs, n, which), dst_refs.at[slot], sems.at[slot])
        waits.append(
            pltpu.make_async_copy(block_ref(refs, 0, which), dst_refs.at[slot], sems.at[slot])
        )
    return waits


def block_shape(blocks):
    shape = blocks[0].shape
    return shape[-3:] if len(blocks) == 2 else shape[:1] + shape[-2:]


def square(block):
    return block.reshape(block.shape[-3] * block.shape[-2], block.shape[-1])


def qkv_kernel(which, count, h_ref, vec_ref, *refs):
    blocks = refs[:count]
    a_hbm, q_hbm, kv_hbm, mat, a_ref, q_ref, kv_ref, sems, outs = refs[count:]
    waits = start_section(blocks, which, (1, 2, 0), mat, sems)
    unit, _ = norm_unit(h_ref[...].astype(F32))
    normed = (unit * vec_ref[0:1, :] + vec_ref[1:2, :]).astype(BF16)
    a_ref[...] = normed
    copies = [start_copy(a_ref, a_hbm, outs.at[0])]
    waits[0].wait()
    kv_ref[0] = nn_dot(normed, square(mat[0])).astype(BF16)
    copies.append(start_copy(kv_ref.at[0], kv_hbm.at[0], outs.at[1]))
    waits[1].wait()
    kv_ref[1] = (nn_dot(normed, square(mat[1])) + vec_ref[3:4, :]).astype(BF16)
    copies.append(start_copy(kv_ref.at[1], kv_hbm.at[1], outs.at[2]))
    waits[2].wait()
    q_ref[...] = (nn_dot(normed, square(mat[2])) + vec_ref[2:3, :]).astype(BF16)
    copies.append(start_copy(q_ref, q_hbm, outs.at[3]))
    for item in copies:
        item.wait()


def qkv_part(stream, vec, attn):
    rows, width = stream.shape
    blocks, which = attn
    low, both = struct((rows, width), BF16), struct((2, rows, width), BF16)
    return call(
        partial(qkv_kernel, which, len(blocks)), [low, low, both], (stream, vec, *blocks), (2, 3),
        (
            pltpu.VMEM((3,) + block_shape(blocks), BF16), pltpu.VMEM(low.shape, BF16),
            pltpu.VMEM(low.shape, BF16), pltpu.VMEM(both.shape, BF16),
            pltpu.SemaphoreType.DMA((3,)), pltpu.SemaphoreType.DMA((4,)),
        ), micros=5, out_placed=(0, 1, 2),
    )


def out_kernel(which, count, h_ref, o_ref, vec_ref, *refs):
    y_ref, mat, sems = refs[count:]
    start_section(refs[:count], which, (3,), mat, sems)[0].wait()
    y_ref[...] = (
        h_ref[...].astype(F32) + nn_dot(o_ref[...], square(mat[0])) + vec_ref[4:5, :]
    ).astype(BF16)


def out_part(stream, mixed, vec, attn):
    rows, width = stream.shape
    blocks, which = attn
    return call(
        partial(out_kernel, which, len(blocks)), [struct((rows, width), BF16)],
        (stream, mixed, vec, *blocks), (3, 4),
        (pltpu.VMEM((1,) + block_shape(blocks), BF16), pltpu.SemaphoreType.DMA((1,))), micros=4,
    )[0]


def up_kernel(which, count, h_ref, vec_ref, *refs):
    a_ref, g_hbm, slope_hbm, mat, g_ref, slope_ref, sems, outs = refs[count:]
    here = lax.axis_index("section")
    waits = [
        start_copy(block_ref(refs[:count], n, which), mat.at[n], sems.at[n]) for n in range(4)
    ]
    unit, _ = norm_unit(h_ref[...].astype(F32))
    normed = (unit * vec_ref[5:6, :] + vec_ref[6:7, :]).astype(BF16)
    a_ref[...] = normed
    copies = []
    for n in range(4):
        waits[n].wait()
        bias = vec_ref[pl.ds(7 + jnp.bitwise_xor(here, n), 1), :]
        up_proj = nn_dot(normed, square(mat[n])) + bias
        below = 0.5 * (1.0 + lax.erf(up_proj * math.sqrt(0.5)))
        bell = jnp.exp(-0.5 * up_proj * up_proj) * (1.0 / math.sqrt(2.0 * math.pi))
        g_ref[n] = (up_proj * below).astype(BF16)
        slope_ref[n] = (below + up_proj * bell).astype(BF16)
        copies.append(start_copy(g_ref.at[n], g_hbm.at[n], outs.at[0, n]))
        copies.append(start_copy(slope_ref.at[n], slope_hbm.at[n], outs.at[1, n]))
    for item in copies:
        item.wait()


def up_part(stream, vec, ups):
    rows, width = stream.shape
    wide = struct((4, rows, width), BF16)
    blocks, which = ups
    return call(
        partial(up_kernel, which, len(blocks)), [struct((rows, width), BF16), wide, wide],
        (stream, vec, *blocks), (2, 3),
        (
            pltpu.VMEM((4,) + block_shape(blocks), BF16), pltpu.VMEM(wide.shape, BF16),
            pltpu.VMEM(wide.shape, BF16), pltpu.SemaphoreType.DMA((4,)),
            pltpu.SemaphoreType.DMA((2, 4)),
        ), micros=9, out_placed=(1, 2),
    )


def start_down(refs, which, n, mat, sems):
    here = lax.axis_index("section")
    size = mat.shape[1] // 8
    waits = []
    for side in range(2):
        owner = 2 * jnp.bitwise_xor(here, n) + side
        for k in range(4):
            if len(refs) == 1:
                src, start = refs[0].at[owner, k, which], (side * 4 + k) * size
            else:
                src = block_ref(refs, k, which).at[owner]
                start = side * 4 * size + jnp.bitwise_xor(here, k) * size
            waits.append(
                start_copy(
                    src, mat.at[n, pl.ds(pl.multiple_of(start, size), size)],
                    sems.at[n, 2 * k + side],
                )
            )
    return waits


def down_kernel(which, count, h_ref, g_hbm, vec_ref, *refs):
    y_ref, mat, g_ref, sems, g_sems = refs[count:]
    waits = []
    for n in range(4):
        found = start_down(refs[:count], which, n, mat, sems)
        waits.append(found + [start_copy(g_hbm.at[n], g_ref.at[n], g_sems.at[n])])
    total = h_ref[...].astype(F32) + vec_ref[11:12, :]
    for n in range(4):
        for item in waits[n]:
            item.wait()
        total = total + nn_dot(g_ref[n], mat[n])
    y_ref[...] = total.astype(BF16)


def down_part(stream, hidden, vec, downs):
    rows, width = stream.shape
    blocks, which = downs
    return call(
        partial(down_kernel, which, len(blocks)), [struct((rows, width), BF16)],
        (stream, hidden, vec, *blocks), (1, 3, 4),
        (
            pltpu.VMEM((4, width, width), BF16), pltpu.VMEM((4, rows, width), BF16),
            pltpu.SemaphoreType.DMA((4, 8)), pltpu.SemaphoreType.DMA((4,)),
        ), micros=6,
    )[0]


def ffn_back_kernel(
    places, counts, gy_ref, h_ref, a_ref, g_hbm, slope_hbm, vec_ref, *refs
):
    (up_at, down_at, attn_at), (up_count, down_count, attn_count) = places, counts
    up_refs, refs = refs[:up_count], refs[up_count:]
    down_refs, refs = refs[:down_count], refs[down_count:]
    attn_refs, refs = refs[:attn_count], refs[attn_count:]
    (
        gh_ref, go_ref, keep_hbm, send_up, send_down, vg_ref,
        g_ref, slope_ref, mat, up_mat, out_mat, up_grad, down_grad,
        in_sems, sems, out_sems, up_sems, down_sems,
    ) = refs
    here = lax.axis_index("section")
    size, width = keep_hbm.shape[-2:]
    waits = []
    for n in range(4):
        found = start_down(down_refs, down_at, n, mat, sems)
        found.append(start_copy(slope_hbm.at[n], slope_ref.at[n], in_sems.at[0, n]))
        found.append(start_copy(g_hbm.at[n], g_ref.at[n], in_sems.at[1, n]))
        found.append(
            start_copy(block_ref(up_refs, n, up_at), up_mat.at[n], in_sems.at[2, n])
        )
        waits.append(found)
    out_wait = start_section(attn_refs, attn_at, (3,), out_mat, out_sems)[0]
    grad = gy_ref[...]
    normed = a_ref[...]
    vg_ref[...] = jnp.zeros_like(vg_ref)
    vg_ref[6:7, :] = jnp.sum(grad.astype(F32), axis=0, keepdims=True)
    grad_normed = None
    copies = []
    for n in range(4):
        for item in waits[n]:
            item.wait()
        block = jnp.bitwise_xor(here, n)
        grad_up = nt_dot(grad, mat[n]) * slope_ref[n].astype(F32)
        grad_up = grad_up.astype(BF16)
        vg_ref[pl.ds(2 + block, 1), :] = jnp.sum(grad_up.astype(F32), axis=0, keepdims=True)
        up_grad[n] = tn_dot(normed, grad_up).astype(BF16).reshape(8, size, width)
        out = (keep_hbm.at[:, 0], send_up.at[:, 0])[n % 2]
        copies.append(start_copy(up_grad.at[n], out.at[n // 2], up_sems.at[n]))
        down_grad[n] = tn_dot(g_ref[n], grad).astype(BF16).reshape(8, size, width)
        for j in range(4):
            place = jnp.bitwise_xor(here, j)
            for side in range(2):
                src, sem = down_grad.at[n, 4 * side + j], down_sems.at[n, 4 * side + j]

                @pl.when(place % 2 == 0)
                def _():
                    start_copy(src, keep_hbm.at[place // 2, 1, 2 * block + side], sem)

                @pl.when(place % 2 == 1)
                def _():
                    start_copy(src, send_down.at[place // 2, 0, 2 * block + side], sem)

                copies.append(pltpu.make_async_copy(src, keep_hbm.at[0, 1, 0], sem))
        term = nt_dot(grad_up, square(up_mat[n]))
        grad_normed = term if n == 0 else grad_normed + term
    grad_in, grad_gain, grad_shift = norm_back(
        h_ref[...].astype(F32), vec_ref[5:6, :], grad_normed, grad
    )
    gh_ref[...] = grad_in
    vg_ref[0:1, :] = grad_gain
    vg_ref[1:2, :] = grad_shift
    out_wait.wait()
    go_ref[...] = nt_dot(grad_in, square(out_mat[0])).astype(BF16)
    for item in copies:
        item.wait()


def ffn_back(grad, stream, normed, hidden, slope, vec, ups, downs, attn):
    rows, width = grad.shape
    sets = (ups, downs, attn)
    counts, places = tuple(len(item[0]) for item in sets), tuple(item[1] for item in sets)
    blocks = [ref for item in sets for ref in item[0]]
    block = block_shape(ups[0])
    part, half = struct((2, 2) + block, BF16), struct((2, 1) + block, BF16)
    low = struct((rows, width), BF16)
    dma = pltpu.SemaphoreType.DMA
    return call(
        partial(ffn_back_kernel, places, counts),
        [low, low, part, half, half, struct((8, width), F32)],
        (grad, stream, normed, hidden, slope, vec, *blocks),
        (3, 4, *range(6, 6 + len(blocks))),
        (
            pltpu.VMEM((4, rows, width), BF16), pltpu.VMEM((4, rows, width), BF16),
            pltpu.VMEM((4, width, width), BF16), pltpu.VMEM((4,) + block, BF16),
            pltpu.VMEM((1,) + block, BF16), pltpu.VMEM((4,) + block, BF16),
            pltpu.VMEM((4,) + block, BF16), dma((3, 4)), dma((4, 8)), dma((1,)), dma((4,)),
            dma((4, 8)),
        ), micros=20, out_placed=(2, 3, 4),
    )


def qkv_back_kernel(
    which, count, gy_ref, h_ref, a_ref, o_ref, gq_ref, own_hbm, got_ref, vec_ref, *refs
):
    gh_ref, keep_hbm, send_hbm, vg_ref, mat, own_ref, term, sems, own_sems, out_sems = refs[count:]
    waits = start_section(refs[:count], which, (0, 1, 2), mat, sems)
    own_waits = [start_copy(own_hbm.at[n], own_ref.at[n], own_sems.at[n]) for n in range(2)]
    here = lax.axis_index("section")
    grad = gy_ref[...]
    normed = a_ref[...]
    vg_ref[...] = jnp.zeros_like(vg_ref)
    copies = []

    def give(block, left, right):
        term[block] = tn_dot(left, right).astype(BF16).reshape(term.shape[1:])
        place = jnp.bitwise_xor(here, block)

        @pl.when(place % 2 == 0)
        def _():
            start_copy(term.at[block], keep_hbm.at[place // 2, 0], out_sems.at[block])

        @pl.when(place % 2 == 1)
        def _():
            start_copy(term.at[block], send_hbm.at[place // 2, 0], out_sems.at[block])

        copies.append(pltpu.make_async_copy(term.at[block], keep_hbm.at[0, 0], out_sems.at[block]))

    vg_ref[4:5, :] = jnp.sum(grad.astype(F32), axis=0, keepdims=True)
    give(3, o_ref[...], grad)
    grad_q = gq_ref[...]
    vg_ref[2:3, :] = jnp.sum(grad_q.astype(F32), axis=0, keepdims=True)
    give(0, normed, grad_q)
    own_waits[0].wait()
    grad_k = (own_ref[0] + got_ref[0].astype(F32)).astype(BF16)
    give(1, normed, grad_k)
    own_waits[1].wait()
    grad_v = (own_ref[1] + got_ref[1].astype(F32)).astype(BF16)
    vg_ref[3:4, :] = jnp.sum(grad_v.astype(F32), axis=0, keepdims=True)
    give(2, normed, grad_v)
    for item in waits:
        item.wait()
    grad_normed = (
        nt_dot(grad_q, square(mat[0])) + nt_dot(grad_k, square(mat[1])) + nt_dot(grad_v, square(mat[2]))
    )
    gh_ref[...], grad_gain, grad_shift = norm_back(
        h_ref[...].astype(F32), vec_ref[0:1, :], grad_normed, grad
    )
    vg_ref[0:1, :] = grad_gain
    vg_ref[1:2, :] = grad_shift
    for item in copies:
        item.wait()


def qkv_back(grad, stream, normed, mixed, parts, vec, attn):
    rows, width = grad.shape
    blocks, which = attn
    block = block_shape(blocks)
    part = struct((2, 1) + block, BF16)
    dma = pltpu.SemaphoreType.DMA
    return call(
        partial(qkv_back_kernel, which, len(blocks)),
        [struct((rows, width), BF16), part, part, struct((8, width), F32)],
        (grad, stream, normed, mixed, *parts, vec, *blocks),
        (5, *range(8, 8 + len(blocks))),
        (
            pltpu.VMEM((3,) + block, BF16), pltpu.VMEM((2, rows, width), F32),
            pltpu.VMEM((4,) + block, BF16), dma((3,)), dma((2,)), dma((4,)),
        ), micros=10, out_placed=(1, 2),
    )


def over(block, axis, move):
    count = lax.axis_size(axis)
    return lax.ppermute(block, axis, [(i, move(i)) for i in range(count)])


def to_core(block):
    return over(block, "section", lambda i: i ^ 1)


def to_x(block):
    return over(block, "section", lambda i: i ^ 2)


def to_y(block):
    return over(block, "dp", lambda i: i ^ 1)


def to_z(block, steps):
    return over(block, "dp", lambda i: (i + 2 * steps) % 8)


ALONG = [[0, 2, 4, 6], [1, 3, 5, 7]]


def gather_along(block):
    return lax.all_gather(block, "dp", axis=0, axis_index_groups=ALONG)


def all_z(block):
    return tuple(to_z(block, k) for k in (1, 2, 3))


class Line:
    def __init__(self, start):
        self.token = start

    def fence(self, arrays):
        *arrays, self.token = lax.optimization_barrier(tuple(arrays) + (self.token,))
        return arrays

    def run(self, body, *operands):
        flat, shape = jax.tree.flatten(operands)
        arrays = self.fence([item for item in flat if not isinstance(item, int)])
        flat = [item if isinstance(item, int) else arrays.pop(0) for item in flat]
        flat, shape = jax.tree.flatten(body(*jax.tree.unflatten(shape, flat)))
        return jax.tree.unflatten(shape, self.fence(flat))


def pick_kernel(
    qkv_ref, out_ref, up_ref, down_ref, again, ashift, qvb, outb, fgain, fshift, upb, downb,
    a1, f1, rest, ride,
):
    size, width = f1.shape[1:]
    here = lax.axis_index("section")
    group = lax.axis_index("dp")
    ride[...] = jnp.zeros_like(ride)
    for i in range(8):
        @pl.when(group == i)
        def _():
            for l in range(2):
                def put(row, start, ref):
                    wide = ref.shape[1]
                    at = slice(start % width, start % width + wide)
                    ride[16 * l + row : 16 * l + row + 1, at] = ref[l : l + 1, :].astype(F32)

                put(0, size * i, again)
                put(1, size * i, ashift)
                put(2 + 2 * size * i // width, 2 * size * i, qvb)
                put(4, size * i, outb)
                put(5, size * i, fgain)
                put(6, size * i, fshift)
                put(7 + 4 * size * i // width, 4 * size * i, upb)
                put(11, size * i, downb)

    a1[size:] = ride[...].astype(BF16)
    for m in range(4):
        @pl.when(here == m)
        def _():
            for l in range(2):
                attn = qkv_ref[l, :, m * width : (m + 1) * width] if m < 3 else out_ref[l]
                ffn = f1 if l == 0 else rest
                ffn[0] = up_ref[l, :, m * width : (m + 1) * width]
                ffn[1] = down_ref[l, m * size : (m + 1) * size]
                if l == 0:
                    a1[:size] = attn
                else:
                    rest[2] = attn


def pick_blocks(*operands):
    size = operands[0].shape[1]
    width = operands[1].shape[2]
    return call(
        pick_kernel,
        [
            struct((size + 32, width), BF16), struct((2, size, width), BF16),
            struct((3, size, width), BF16),
        ],
        operands, (), (pltpu.VMEM((32, width), F32),), micros=4,
    )


def split_kernel(near_ref, *out_refs):
    at = 0
    for left_ref, right_ref in zip(out_refs[::2], out_refs[1::2]):
        count, wide = left_ref.shape[1], left_ref.shape[-1]
        left_ref[...] = near_ref[:, at : at + count, :, :wide]
        right_ref[...] = near_ref[:, at : at + count, :, wide:]
        at += count


def split_near(near, counts):
    size, width = near.shape[2:]
    outs = []
    for count in counts:
        outs += [struct((4, count, size, width // 2), BF16)] * 2
    return call(split_kernel, outs, (near,))


def middle_kernel(left_ref, left_got, right_ref, right_got, x_ref, y_ref):
    side = lax.axis_index("dp") % 2
    for along in range(4):
        x_ref[2 * along + side] = left_ref[along]
        x_ref[2 * along + 1 - side] = left_got[along]
    y_ref[0] = right_ref[...]
    y_ref[1] = right_got[...]


def middle(left, left_got, right, right_got):
    part = left.shape[1:]
    return call(
        middle_kernel, [struct((8,) + part, BF16), struct((2, 4) + part, BF16)],
        (left, left_got, right, right_got), micros=120,
    )


def whole_kernel(x_ref, x_got, y_ref, y_got, out_ref, *ride_refs):
    side = lax.axis_index("dp") % 2
    count, size, wide = out_ref.shape[0], out_ref.shape[3], x_ref.shape[3]
    for c in range(count):
        for n, ref in enumerate((x_ref, x_got)):
            out_ref[c, n, :, :, :wide] = ref[:, c, :size]
            for along in range(4):
                out_ref[c, n, 2 * along + side, :, wide:] = y_ref[n, along, c, :size]
                out_ref[c, n, 2 * along + 1 - side, :, wide:] = y_got[n, along, c, :size]
    if ride_refs:
        left = jnp.sum(x_ref[:, 0, size:].astype(F32), axis=0)
        right = jnp.sum(y_ref[0, :, 0, size:].astype(F32), axis=0)
        right = right + jnp.sum(y_got[0, :, 0, size:].astype(F32), axis=0)
        for l in range(2):
            ride_refs[l][:, :wide] = left[16 * l : 16 * l + 16]
            ride_refs[l][:, wide:] = right[16 * l : 16 * l + 16]


def whole_blocks(x_send, x_got, y_send, y_got, size):
    _, count, full, wide = x_send.shape
    outs = [struct((count, 2, 8, size, 2 * wide), BF16)]
    if full > size:
        outs += [struct((16, 2 * wide), F32)] * 2
    return call(whole_kernel, outs, (x_send, x_got, y_send, y_got))


class Gather:
    def __init__(self, line, left, right, size):
        self.line, self.left, self.right, self.size = line, left, right, size
        self.left_got, self.right_got = to_y(left), to_x(right)

    def middle(self):
        self.x_send, self.y_send = self.line.run(
            middle, self.left, self.left_got, self.right, self.right_got
        )
        self.x_got, self.y_got = to_x(self.x_send), to_y(self.y_send)

    def whole(self):
        found = self.line.run(
            lambda *items: whole_blocks(*items, self.size),
            self.x_send, self.x_got, self.y_send, self.y_got,
        )
        self.pair = (found[0], to_core(found[0]))
        return found[1:]


def first_kernel(keep_ref, *refs):
    got_refs, (x_ref, y_ref, left_ref, right_ref) = refs[:-4], refs[-4:]
    wide = x_ref.shape[-1]
    side = lax.axis_index("dp") % 2
    for c in range(keep_ref.shape[1]):
        for n, ref in enumerate((left_ref, x_ref)):
            ref[c] = (
                keep_ref[n, c, :, :, :wide].astype(F32)
                + got_refs[c][n, 0, :, :, :wide].astype(F32)
            ).astype(BF16)
        for n in range(2):
            for along in range(4):
                for ref, pick in ((right_ref, side), (y_ref, 1 - side)):
                    at = 2 * along + pick
                    ref[n, c, along] = (
                        keep_ref[n, c, at, :, wide:].astype(F32)
                        + got_refs[c][n, 0, at, :, wide:].astype(F32)
                    ).astype(BF16)


def add_first(keep, *got):
    _, count, _, size, width = keep.shape
    x_part = struct((count, 8, size, width // 2), BF16)
    y_part = struct((2, count, 4, size, width // 2), BF16)
    return call(first_kernel, [x_part, y_part, x_part, y_part], (keep, *got), micros=5)


def both_kernel(keep_ref, up_ref, down_ref, out_ref):
    for c, ref in enumerate((up_ref, down_ref)):
        for n in range(2):
            out_ref[:, n, c] = (
                keep_ref[n, c].astype(F32) + ref[n, 0].astype(F32)
            ).astype(BF16)


def add_both(keep, *got):
    _, count, parts, size, width = keep.shape
    step = parts // 4
    spec = pl.BlockSpec((2, count, step, size, width), lambda i: (0, 0, i, 0, 0))
    half = pl.BlockSpec((2, 1, step, size, width), lambda i: (0, 0, i, 0, 0))
    return pl.pallas_call(
        both_kernel,
        grid=(4,),
        in_specs=[spec, half, half],
        out_specs=pl.BlockSpec((step, 2, count, size, width), lambda i: (i, 0, 0, 0, 0)),
        out_shape=struct((parts, 2, count, size, width), BF16),
        compiler_params=pltpu.CompilerParams(vmem_limit_bytes=VMEM_ROOM),
        cost_estimate=lasting(80),
    )(keep, *got)


def scatter_both(block):
    return lax.psum_scatter(block, "dp", scatter_dimension=0, tiled=True)[0]


def second_kernel(left_ref, x_got, right_ref, y_got, y_ref, x_ref, near_ref, rest_ref):
    side = lax.axis_index("dp") % 2
    for c in range(left_ref.shape[0]):
        for along in range(4):
            for ref, pick in ((near_ref, side), (y_ref, 1 - side)):
                at = 2 * along + pick
                ref[c, along] = (
                    left_ref[c, at].astype(F32) + x_got[c, at].astype(F32)
                ).astype(BF16)
        for n, ref in enumerate((rest_ref, x_ref)):
            ref[c] = (right_ref[n, c].astype(F32) + y_got[n, c].astype(F32)).astype(BF16)


def add_second(left, x_got, right, y_got):
    part = struct(right.shape[1:], BF16)
    return call(second_kernel, [part] * 4, (left, x_got, right, y_got), micros=120)


def third_kernel(near_ref, y_got, rest_ref, x_got, out_ref):
    wide = near_ref.shape[-1]
    for c in range(near_ref.shape[0]):
        for along in range(4):
            out_ref[along, c, :, :wide] = (
                near_ref[c, along].astype(F32) + y_got[c, along].astype(F32)
            ).astype(BF16)
            out_ref[along, c, :, wide:] = (
                rest_ref[c, along].astype(F32) + x_got[c, along].astype(F32)
            ).astype(BF16)


def add_third(micros, near, y_got, rest, x_got):
    count, _, size, wide = near.shape
    return call(
        third_kernel, [struct((4, count, size, 2 * wide), BF16)], (near, y_got, rest, x_got),
        micros=micros,
    )[0]


def split_kernel_back(near_ref, y_got, rest_ref, x_got, o0, o1, o2, o3):
    along = lax.axis_index("dp") // 2
    wide = near_ref.shape[-1]
    for c in range(near_ref.shape[0]):
        for k, ref in enumerate((o0, o1, o2, o3)):
            pick = lax.rem(along + k, 4)
            ref[c, :, :wide] = (
                near_ref[c, pick].astype(F32) + y_got[c, pick].astype(F32)
            ).astype(BF16)
            ref[c, :, wide:] = (
                rest_ref[c, pick].astype(F32) + x_got[c, pick].astype(F32)
            ).astype(BF16)


def add_third_split(near, y_got, rest, x_got):
    count, _, size, wide = near.shape
    part = struct((count, size, 2 * wide), BF16)
    return call(split_kernel_back, [part] * 4, (near, y_got, rest, x_got), micros=60)


def last_kernel(o0, o1, o2, o3, out_ref):
    out_ref[...] = (
        o0[...].astype(F32) + o1[...].astype(F32) + o2[...].astype(F32) + o3[...].astype(F32)
    ).astype(BF16)


def add_last(*parts):
    return call(last_kernel, [struct(parts[0].shape, BF16)], parts)[0]


def across(own):
    far = to_x(own)
    return own, to_core(own), far, to_core(far)


class Reduce:
    def __init__(self, line, x_send, y_send, left, right):
        self.line, self.left, self.right = line, left, right
        self.x_got, self.y_got = to_x(x_send), to_y(y_send)

    def second(self):
        y_send, x_send, self.near, self.rest = self.line.run(
            add_second, self.left, self.x_got, self.right, self.y_got
        )
        self.y_got, self.x_got = to_y(y_send), to_x(x_send)

    def third(self, micros):
        whole = self.line.run(
            partial(add_third, micros), self.near, self.y_got, self.rest, self.x_got
        )
        self.shard = lax.psum_scatter(
            whole, "dp", scatter_dimension=0, tiled=True, axis_index_groups=ALONG
        )[0]

    def third_split(self):
        self.parts = self.line.run(
            add_third_split, self.near, self.y_got, self.rest, self.x_got
        )
        self.z_got = [to_z(self.parts[k], k) for k in (1, 2, 3)]

    def last(self):
        self.shard = self.line.run(add_last, self.parts[0], *self.z_got)


def finish_kernel(a0, a1, a2, a3, f1_ref, rest_ref, qkv_ref, out_ref, up_ref, down_ref):
    here = lax.axis_index("section")
    size, width = f1_ref.shape[-2:]

    def put(l, b, found):
        if b < 3:
            qkv_ref[l, :, b * width : (b + 1) * width] = found.astype(F32)
        else:
            out_ref[l] = found.astype(F32)

    for m in range(4):
        @pl.when(here == m)
        def _():
            for b in range(4):
                put(0, b, (a0, a1, a2, a3)[m ^ b][0])

    for b in range(4):
        put(1, b, rest_ref[b, 2])
        for l, ref in enumerate((f1_ref, rest_ref)):
            up_ref[l, :, b * width : (b + 1) * width] = ref[b, 0].astype(F32)
            down_ref[l, b * size : (b + 1) * size] = ref[b, 1].astype(F32)


def finish(*held):
    _, size, width = held[0].shape
    return call(
        finish_kernel,
        [
            struct((2, size, 3 * width), F32), struct((2, size, width), F32),
            struct((2, size, 4 * width), F32), struct((2, 4 * size, width), F32),
        ],
        held, micros=5,
    )


def pick_row(stacked, index):
    return lax.dynamic_index_in_dim(stacked, index, 0, keepdims=False)


def local(
    tokens, lengths, cotangent, attn_gain, attn_shift, qkv_weight, qv_bias, out_weight, out_bias,
    ffn_gain, ffn_shift, up_weight, up_bias, down_weight, down_bias,
):
    layers, size, width3 = qkv_weight.shape
    width = width3 // 3
    eighth = width // 8
    micro_count, cell_count, seq_len, _ = tokens.shape
    section_id = lax.axis_index("section")
    section_count = lax.axis_size("section")
    group = lax.axis_size("dp")
    dp_id = lax.axis_index("dp")
    share = section_count // micro_count
    assert cell_count == 1 and share == 2 and section_count == 4 and layers == 2
    cell = section_id // share
    half = section_id % share
    rows = seq_len // share
    direct = group == 8
    line = Line(jnp.zeros((1, 1), F32))

    def mine(stacked):
        return lax.dynamic_slice(
            stacked, (cell, 0, half * rows, 0), (1, 1, rows, width)
        ).reshape(rows, width)

    def pinned():
        length = lax.dynamic_slice(lengths, (cell, 0), (1, 1)).reshape(())
        return line.run(
            lambda one, two, size: (
                mine(one), mine(two), jnp.stack([size - half * rows, size - (1 - half) * rows])
            ),
            tokens, cotangent, length,
        )

    if direct:
        a1_block, f1_block, rest_block = line.run(
            pick_blocks, qkv_weight, out_weight, up_weight, down_weight,
            attn_gain, attn_shift, qv_bias, out_bias, ffn_gain, ffn_shift, up_bias, down_bias,
        )
        a1_near = gather_along(a1_block[None])
        f1_near = gather_along(f1_block)
        rest = lax.all_gather(rest_block, ("dp", "section"), axis=0, tiled=False)
        rest = rest.reshape(8, 4, 3, size, width)
        a1 = Gather(line, *line.run(lambda near: split_near(near, (1,)), a1_near), size)
        stream, grad, lens = pinned()
        a1.middle()
        u1_d1 = line.run(lambda near: split_near(near, (1, 1)), f1_near)
        u1 = Gather(line, *u1_d1[:2], size)
        d1 = Gather(line, *u1_d1[2:], size)
        vec1, vec2 = a1.whole()
        u1.middle()
        attn1 = (a1.pair, 0)
    else:
        def gather(block, axis):
            return lax.all_gather(block, "dp", axis=axis, tiled=True)

        def relative(blocks):
            found = [pick_row(blocks, section_id ^ n) for n in range(4)]
            return jnp.stack([found[0], found[2]])[None], jnp.stack([found[1], found[3]])[None]

        def attn_blocks(l):
            whole = gather(jnp.concatenate([qkv_weight[l], out_weight[l]], axis=1), 0)
            return relative(whole.reshape(8, eighth, 4, width).transpose(2, 0, 1, 3))

        def up_blocks(l):
            return relative(gather(up_weight[l], 0).reshape(8, eighth, 4, width).transpose(2, 0, 1, 3))

        def down_blocks(l):
            return relative(gather(down_weight[l], 0).reshape(8, 4, eighth, width).transpose(1, 0, 2, 3))

        def spread_vectors():
            def at(block, row_count):
                empty = jnp.zeros((layers, row_count, width), BF16)
                flat = block.shape[-1] * dp_id
                return lax.dynamic_update_slice(empty, block, (0, flat // width, flat % width))

            six = jnp.stack([attn_gain, attn_shift, out_bias, ffn_gain, ffn_shift, down_bias], axis=1)
            six = lax.dynamic_update_slice(
                jnp.zeros((layers, 6, width), BF16), six, (0, 0, dp_id * size)
            )
            qv = at(qv_bias[:, None], 2)
            ups = at(up_bias[:, None], 4)
            return jnp.concatenate(
                [six[:, :2], qv, six[:, 2:5], ups, six[:, 5:], jnp.zeros((layers, 4, width), BF16)],
                axis=1,
            )

        vecs = lax.psum(spread_vectors().astype(F32), "dp")
        vec1, vec2 = vecs[0], vecs[1]
        attn1, ups1, downs1 = [(blocks(0), 0) for blocks in (attn_blocks, up_blocks, down_blocks)]
        attn2, ups2, downs2 = [(blocks(1), 0) for blocks in (attn_blocks, up_blocks, down_blocks)]

    def redistribute_start(*blocks):
        quarter = rows // 2
        route_a = [(2 * c + h, 2 * h + c) for c in range(2) for h in range(2)]
        route_b = [(2 * c + h, 2 * h + 1 - c) for c in range(2) for h in range(2)]
        first = cell == 0

        def choose(*items):
            low = jnp.stack([item[:quarter] for item in items])
            high = jnp.stack([item[quarter:] for item in items])
            return jnp.where(first, low, high), jnp.where(first, high, low)

        send_a, send_b = line.run(choose, *blocks)
        return lax.ppermute(send_a, "section", route_a), lax.ppermute(send_b, "section", route_b)

    def redistribute_end(got_a, got_b):
        even = section_id % 2 == 0

        def place(a, b):
            pair = jnp.where(even, a, b), jnp.where(even, b, a)
            return tuple(jnp.stack([item[n] for item in pair])[:, None] for n in range(2))

        return line.run(place, got_a, got_b)

    if not direct:
        stream, grad, lens = pinned()

    attn_in1 = stream
    normed1, queries1, own1 = line.run(qkv_part, stream, vec1, attn1)
    peer1 = to_core(own1)
    if direct:
        d1.middle()
    mixed1, raised1, scale1 = line.run(attend, queries1, own1, peer1, lens)
    if direct:
        u1.whole()
        ups1 = (u1.pair, 0)
    ffn_in1 = line.run(out_part, attn_in1, mixed1, vec1, attn1)
    if direct:
        d1.whole()
        downs1 = (d1.pair, 0)
    normed2_1, hidden1, slope1 = line.run(up_part, ffn_in1, vec1, ups1)
    stream = line.run(down_part, ffn_in1, hidden1, vec1, downs1)
    attn_in2 = stream
    if direct:
        ups2, downs2, attn2 = ((rest,), 0), ((rest,), 1), ((rest,), 2)
    normed2, queries2, own2 = line.run(qkv_part, stream, vec2, attn2)
    peer2 = to_core(own2)
    mixed2, raised2, scale2 = line.run(attend, queries2, own2, peer2, lens)
    ffn_in2 = line.run(out_part, attn_in2, mixed2, vec2, attn2)
    normed2_2, hidden2, slope2 = line.run(up_part, ffn_in2, vec2, ups2)
    stream = line.run(down_part, ffn_in2, hidden2, vec2, downs2)

    encoded_mine = stream
    grad, grad_mixed, f2_keep, f2_up, f2_down, f2_vec = line.run(
        ffn_back, grad, ffn_in2, normed2_2, hidden2, slope2, vec2, ups2, downs2, attn2
    )
    if direct:
        f2_got = to_core(f2_up), to_core(f2_down)
    grad_q, kv_own, kv_peer = line.run(
        attend_back, queries2, own2, peer2, mixed2, grad_mixed, raised2, scale2
    )
    kv_got = to_core(kv_peer)
    if direct:
        f2_part = scatter_both(line.run(add_both, f2_keep, *f2_got))
    grad, a2_keep, a2_send, a2_vec = line.run(
        qkv_back, grad, attn_in2, normed2, mixed2, (grad_q, kv_own, kv_got), vec2, attn2
    )
    if direct:
        a2_got = to_core(a2_send)
        a2r = Reduce(line, *line.run(add_first, a2_keep, a2_got))
    grad, grad_mixed, f1_keep, f1_up, f1_down, f1_vec = line.run(
        ffn_back, grad, ffn_in1, normed2_1, hidden1, slope1, vec1, ups1, downs1, attn1
    )
    if direct:
        f1_got = to_core(f1_up), to_core(f1_down)
        a2r.second()
        f1r = Reduce(line, *line.run(add_first, f1_keep, *f1_got))
    grad_q, kv_own, kv_peer = line.run(
        attend_back, queries1, own1, peer1, mixed1, grad_mixed, raised1, scale1
    )
    kv_got = to_core(kv_peer)
    if direct:
        f1r.second()
        a2r.third(2)
    grad, a1_keep, a1_send, a1_vec = line.run(
        qkv_back, grad, attn_in1, normed1, mixed1, (grad_q, kv_own, kv_got), vec1, attn1
    )

    def vector_shares(a, b, c, d):
        total = jnp.stack([jnp.concatenate([a, b]), jnp.concatenate([c, d])])

        def share(lo, hi):
            wide = total[:, lo:hi].reshape(layers, group, hi - lo, size)
            return wide.transpose(1, 0, 2, 3)

        def each(lo, hi):
            wide = total[:, lo:hi].reshape(layers, hi - lo, group, size)
            return wide.transpose(2, 0, 1, 3)

        return jnp.concatenate(
            [each(0, 2), share(2, 4), each(4, 10), share(10, 14), each(14, 16)], axis=2
        )

    if direct:
        a1_got = to_core(a1_send)
        f2_near, f2_send = line.run(lambda part: (part[0], part[1]), f2_part)
        f1r.third(120)
        a1r = Reduce(line, *line.run(add_first, a1_keep, a1_got))
        f2_far = to_x(f2_send)
        rest_own = line.run(
            lambda near, far, attn: jnp.concatenate([near + far, attn]), f2_near, f2_far, a2r.shard
        )
        rest_held = lax.all_gather(rest_own, "section", axis=0)
        a1r.second()
        shares = line.run(
            lambda *vecs: jnp.broadcast_to(
                vector_shares(*vecs)[:, None], (group, section_count, layers, 16, size)
            ).reshape(group * section_count, layers, 16, size),
            a1_vec, f1_vec, a2_vec, f2_vec,
        )
        shares = lax.all_to_all(shares, ("dp", "section"), 0, 0, tiled=True)
        a1r.third_split()
        moved = redistribute_start(encoded_mine, grad)
        my_vec = line.run(lambda got: jnp.sum(got, axis=0), shares)
        f1_held = lax.all_gather(f1r.shard, "section", axis=0)
        a1r.last()
        a1_held = across(a1r.shard)
        encoded, grad_tokens = redistribute_end(*moved)
        g_qkv, g_out, g_up, g_down = line.run(finish, *a1_held, f1_held, rest_held)
    else:
        encoded, grad_tokens = redistribute_end(*redistribute_start(encoded_mine, grad))
        def canonical(keep, send):
            blocks = jnp.stack([keep[0], send[0], keep[1], send[1]])
            return jnp.stack([pick_row(blocks, section_id ^ n) for n in range(4)])

        def scatter(whole):
            part = lax.psum_scatter(whole, "dp", scatter_dimension=0, tiled=True)
            return lax.psum(part, "section").astype(F32)

        def wide(blocks):
            return blocks.transpose(1, 2, 0, 3).reshape(width, 4 * width)

        both = [
            (canonical(a1_keep, a1_send), canonical(f1_keep, jnp.concatenate([f1_up, f1_down], axis=1))),
            (canonical(a2_keep, a2_send), canonical(f2_keep, jnp.concatenate([f2_up, f2_down], axis=1))),
        ]
        attn_all = jnp.stack([scatter(wide(attn[:, 0])) for attn, _ in both])
        g_qkv, g_out = attn_all[:, :, :width3], attn_all[:, :, width3:]
        g_up = jnp.stack([scatter(wide(ffn[:, 0])) for _, ffn in both])
        g_down = jnp.stack(
            [scatter(ffn[:, 1].transpose(1, 0, 2, 3).reshape(4 * width, width)) for _, ffn in both]
        )
        shares = lax.psum(vector_shares(a1_vec, f1_vec, a2_vec, f2_vec), ("dp", "section"))
        my_vec = pick_row(shares, dp_id)

    my_vec = my_vec + line.token
    return (
        encoded, grad_tokens, my_vec[:, 0], my_vec[:, 1], g_qkv,
        my_vec[:, 2:4].reshape(layers, 2 * size), g_out, my_vec[:, 4], my_vec[:, 8], my_vec[:, 9],
        g_up, my_vec[:, 10:14].reshape(layers, 4 * size), g_down, my_vec[:, 14],
    )


def solution(mesh):
    flat, rows4 = P(None, "dp"), P(None, "dp", None, None)
    mat, spread = P(None, "dp", None), P(None, "dp", "section", None)
    in_specs = (
        rows4, flat, rows4, flat, flat, mat, flat, mat, flat, flat, flat, mat, flat, mat, flat,
    )
    out_specs = (
        spread, spread, flat, flat, mat, flat, mat, flat, flat, flat, mat, flat, mat, flat,
    )
    return jax.shard_map(local, mesh=mesh, in_specs=in_specs, out_specs=out_specs, check_vma=False)
```

```python
from functools import partial
import math

import jax
import jax.numpy as jnp
from jax import lax
from jax.experimental import pallas as pl
from jax.experimental.pallas import tpu as pltpu
from jax.sharding import PartitionSpec as P

HEAD = 64
PAIR = 2 * HEAD
NORM_EPS = 1e-05
MASK_FLOOR = -1e30
F32 = jnp.float32
BF16 = jnp.bfloat16
VMEM_ROOM = 56 << 20
WHOLE = pl.BlockSpec(memory_space=pltpu.VMEM)
PLACED = pl.BlockSpec(memory_space=pl.ANY)


def nt_dot(left, right):
    return lax.dot_general(left, right, (((1,), (1,)), ((), ())), preferred_element_type=F32)


def nn_dot(left, right):
    return jnp.dot(left, right, preferred_element_type=F32)


def tn_dot(left, right):
    return lax.dot_general(left, right, (((0,), (0,)), ((), ())), preferred_element_type=F32)


def lasting(micros):
    return pl.CostEstimate(flops=micros << 28, transcendentals=0, bytes_accessed=1 << 16)


def struct(shape, kind):
    return jax.ShapeDtypeStruct(shape, kind)


def call(body, outs, operands, placed=(), scratch=(), micros=2, out_placed=()):
    return pl.pallas_call(
        body,
        in_specs=[PLACED if n in placed else WHOLE for n in range(len(operands))],
        out_specs=[PLACED if n in out_placed else WHOLE for n in range(len(outs))],
        out_shape=outs,
        scratch_shapes=list(scratch),
        compiler_params=pltpu.CompilerParams(vmem_limit_bytes=VMEM_ROOM),
        cost_estimate=lasting(micros),
    )(*operands)


def start_copy(src, dst, sem):
    copy = pltpu.make_async_copy(src, dst, sem)
    copy.start()
    return copy


def head_lanes(block, head):
    lane = lax.broadcasted_iota(jnp.int32, block.shape, 1)
    keep = (lane < HEAD) if head == 0 else (lane >= HEAD)
    return jnp.where(keep, block, jnp.zeros_like(block))


def attend_kernel(lens_ref, q_ref, ko_ref, kp_ref, vo_ref, vp_ref, o_ref, raised_ref, scale_ref):
    rows = q_ref.shape[0]
    score_scale = 1.0 / math.sqrt(HEAD)
    query_pair = q_ref[...] * jnp.asarray(score_scale, BF16)
    value_t = [vo_ref[...].T, vp_ref[...].T]
    mixed, scales = [], []
    for head in range(2):
        query = head_lanes(query_pair, head)
        scores = []
        for part, key_ref in enumerate((ko_ref, kp_ref)):
            part_scores = nt_dot(key_ref[...], query)
            key_row = lax.broadcasted_iota(jnp.int32, part_scores.shape, 0)
            scores.append(jnp.where(key_row < lens_ref[part], part_scores, MASK_FLOOR))
        row_max = jnp.maximum(
            jnp.max(scores[0], axis=0, keepdims=True), jnp.max(scores[1], axis=0, keepdims=True)
        )
        total = jnp.zeros((1, rows), F32)
        head_out = jnp.zeros((HEAD, rows), F32)
        for part in range(2):
            raised = jnp.exp(scores[part] - row_max)
            total = total + jnp.sum(raised, axis=0, keepdims=True)
            low = raised.astype(BF16)
            raised_ref[head, part * rows : (part + 1) * rows, :] = low
            head_out = head_out + nn_dot(value_t[part][head * HEAD : (head + 1) * HEAD, :], low)
        inverse = 1.0 / total
        mixed.append(head_out * inverse)
        scales.append(jnp.broadcast_to(inverse, (HEAD, rows)))
    o_ref[...] = jnp.concatenate(mixed, axis=0).T.astype(BF16)
    scale_ref[...] = jnp.concatenate(scales, axis=0).T


def attend(queries, own, peer, lens):
    rows, width = queries.shape
    pairs = width // PAIR
    block = pl.BlockSpec((rows, PAIR), lambda p, lens: (0, p))
    key = pl.BlockSpec((None, rows, PAIR), lambda p, lens: (0, 0, p))
    value = pl.BlockSpec((None, rows, PAIR), lambda p, lens: (1, 0, p))
    return pl.pallas_call(
        attend_kernel,
        grid_spec=pltpu.PrefetchScalarGridSpec(
            num_scalar_prefetch=1,
            grid=(pairs,),
            in_specs=[block, key, key, value, value],
            out_specs=[
                block, pl.BlockSpec((2, 2 * rows, rows), lambda p, lens: (p, 0, 0)), block,
            ],
        ),
        out_shape=[
            struct((rows, width), BF16), struct((2 * pairs, 2 * rows, rows), BF16),
            struct((rows, width), F32),
        ],
        compiler_params=pltpu.CompilerParams(vmem_limit_bytes=48 << 20),
        cost_estimate=lasting(16),
    )(lens, queries, own, peer, own, peer)


def attend_back_kernel(
    q_ref, ko_ref, kp_ref, vo_ref, vp_ref, o_ref, go_ref, raised_ref, scale_ref,
    gq_ref, own_ref, peer_ref,
):
    rows = q_ref.shape[0]
    score_scale = 1.0 / math.sqrt(HEAD)
    query_pair = q_ref[...] * jnp.asarray(score_scale, BF16)
    query_t = query_pair.T
    grad_pair = (go_ref[...].astype(F32) * scale_ref[...]).astype(BF16)
    grad_t = grad_pair.T
    inner = (o_ref[...].astype(F32) * grad_pair.astype(F32)).T
    value_refs = (vo_ref, vp_ref)
    key_t = [ko_ref[...].T, kp_ref[...].T]
    grad_key = [[], []]
    grad_value = [[], []]
    grad_query = []
    for head in range(2):
        lanes = slice(head * HEAD, (head + 1) * HEAD)
        grad_out = head_lanes(grad_pair, head)
        inner_row = jnp.sum(inner[lanes, :], axis=0, keepdims=True)
        head_query = jnp.zeros((HEAD, rows), F32)
        for part in range(2):
            raised = raised_ref[head, part * rows : (part + 1) * rows, :]
            grad_prob = nt_dot(value_refs[part][...], grad_out)
            grad_score = (raised.astype(F32) * (grad_prob - inner_row)).astype(BF16)
            grad_value[part].append(nt_dot(grad_t[lanes, :], raised))
            grad_key[part].append(nt_dot(query_t[lanes, :], grad_score))
            head_query = head_query + nn_dot(key_t[part][lanes, :], grad_score)
        grad_query.append(head_query * score_scale)
    gq_ref[...] = jnp.concatenate(grad_query, axis=0).T.astype(BF16)
    for n, grads in enumerate((grad_key, grad_value)):
        own_ref[n] = jnp.concatenate(grads[0], axis=0).T
        peer_ref[n] = jnp.concatenate(grads[1], axis=0).T.astype(BF16)


def attend_back(queries, own, peer, mixed, grad_mixed, raised, scale):
    rows, width = queries.shape
    pairs = width // PAIR
    block = pl.BlockSpec((rows, PAIR), lambda p: (0, p))
    key = pl.BlockSpec((None, rows, PAIR), lambda p: (0, 0, p))
    value = pl.BlockSpec((None, rows, PAIR), lambda p: (1, 0, p))
    both = pl.BlockSpec((2, rows, PAIR), lambda p: (0, 0, p))
    low, full = struct((rows, width), BF16), struct((2, rows, width), F32)
    sent = struct((2, rows, width), BF16)
    return pl.pallas_call(
        attend_back_kernel,
        grid=(pairs,),
        in_specs=[
            block, key, key, value, value, block, block,
            pl.BlockSpec((2, 2 * rows, rows), lambda p: (p, 0, 0)), block,
        ],
        out_specs=[block, both, both],
        out_shape=[low, full, sent],
        compiler_params=pltpu.CompilerParams(vmem_limit_bytes=48 << 20),
        cost_estimate=lasting(16),
    )(queries, own, peer, own, peer, mixed, grad_mixed, raised, scale)


def norm_unit(stream):
    center = stream - jnp.mean(stream, axis=-1, keepdims=True)
    spread = jnp.mean(center * center, axis=-1, keepdims=True)
    root = lax.rsqrt(spread + NORM_EPS)
    return center * root, root


def norm_back(stream, gain, grad_normed, grad_low):
    unit, root = norm_unit(stream)
    grad_gain = jnp.sum(grad_normed * unit, axis=0, keepdims=True)
    grad_shift = jnp.sum(grad_normed, axis=0, keepdims=True)
    grad_unit = grad_normed * gain
    grad_stream = root * (
        grad_unit
        - jnp.mean(grad_unit, axis=-1, keepdims=True)
        - unit * jnp.mean(grad_unit * unit, axis=-1, keepdims=True)
    )
    return (grad_low.astype(F32) + grad_stream).astype(BF16), grad_gain, grad_shift


def block_ref(refs, n, which):
    if len(refs) == 2:
        return refs[n % 2].at[which, n // 2]
    return refs[0].at[:, jnp.bitwise_xor(lax.axis_index("section"), n), which]


def start_section(refs, which, wanted, dst_refs, sems):
    here = lax.axis_index("section")
    waits = []
    for slot, block in enumerate(wanted):
        if len(refs) == 1:
            waits.append(start_copy(refs[0].at[:, block, which], dst_refs.at[slot], sems.at[slot]))
            continue
        place = jnp.bitwise_xor(here, block)
        for n in range(4):
            @pl.when(place == n)
            def _():
                start_copy(block_ref(refs, n, which), dst_refs.at[slot], sems.at[slot])
        waits.append(
            pltpu.make_async_copy(block_ref(refs, 0, which), dst_refs.at[slot], sems.at[slot])
        )
    return waits


def block_shape(blocks):
    shape = blocks[0].shape
    return shape[-3:] if len(blocks) == 2 else shape[:1] + shape[-2:]


def square(block):
    return block.reshape(block.shape[-3] * block.shape[-2], block.shape[-1])


def qkv_kernel(which, count, h_ref, vec_ref, *refs):
    blocks = refs[:count]
    a_hbm, q_hbm, kv_hbm, mat, a_ref, q_ref, kv_ref, sems, outs = refs[count:]
    waits = start_section(blocks, which, (1, 2, 0), mat, sems)
    unit, _ = norm_unit(h_ref[...].astype(F32))
    normed = (unit * vec_ref[0:1, :] + vec_ref[1:2, :]).astype(BF16)
    a_ref[...] = normed
    copies = [start_copy(a_ref, a_hbm, outs.at[0])]
    waits[0].wait()
    kv_ref[0] = nn_dot(normed, square(mat[0])).astype(BF16)
    copies.append(start_copy(kv_ref.at[0], kv_hbm.at[0], outs.at[1]))
    waits[1].wait()
    kv_ref[1] = (nn_dot(normed, square(mat[1])) + vec_ref[3:4, :]).astype(BF16)
    copies.append(start_copy(kv_ref.at[1], kv_hbm.at[1], outs.at[2]))
    waits[2].wait()
    q_ref[...] = (nn_dot(normed, square(mat[2])) + vec_ref[2:3, :]).astype(BF16)
    copies.append(start_copy(q_ref, q_hbm, outs.at[3]))
    for item in copies:
        item.wait()


def qkv_part(stream, vec, attn):
    rows, width = stream.shape
    blocks, which = attn
    low, both = struct((rows, width), BF16), struct((2, rows, width), BF16)
    return call(
        partial(qkv_kernel, which, len(blocks)), [low, low, both], (stream, vec, *blocks), (2, 3),
        (
            pltpu.VMEM((3,) + block_shape(blocks), BF16), pltpu.VMEM(low.shape, BF16),
            pltpu.VMEM(low.shape, BF16), pltpu.VMEM(both.shape, BF16),
            pltpu.SemaphoreType.DMA((3,)), pltpu.SemaphoreType.DMA((4,)),
        ), micros=5, out_placed=(0, 1, 2),
    )


def out_kernel(which, count, h_ref, o_ref, vec_ref, *refs):
    y_ref, mat, sems = refs[count:]
    start_section(refs[:count], which, (3,), mat, sems)[0].wait()
    y_ref[...] = (
        h_ref[...].astype(F32) + nn_dot(o_ref[...], square(mat[0])) + vec_ref[4:5, :]
    ).astype(BF16)


def out_part(stream, mixed, vec, attn):
    rows, width = stream.shape
    blocks, which = attn
    return call(
        partial(out_kernel, which, len(blocks)), [struct((rows, width), BF16)],
        (stream, mixed, vec, *blocks), (3, 4),
        (pltpu.VMEM((1,) + block_shape(blocks), BF16), pltpu.SemaphoreType.DMA((1,))), micros=4,
    )[0]


def up_kernel(which, count, h_ref, vec_ref, *refs):
    a_ref, g_hbm, slope_hbm, mat, g_ref, slope_ref, sems, outs = refs[count:]
    here = lax.axis_index("section")
    waits = [
        start_copy(block_ref(refs[:count], n, which), mat.at[n], sems.at[n]) for n in range(4)
    ]
    unit, _ = norm_unit(h_ref[...].astype(F32))
    normed = (unit * vec_ref[5:6, :] + vec_ref[6:7, :]).astype(BF16)
    a_ref[...] = normed
    copies = []
    for n in range(4):
        waits[n].wait()
        bias = vec_ref[pl.ds(7 + jnp.bitwise_xor(here, n), 1), :]
        up_proj = nn_dot(normed, square(mat[n])) + bias
        below = 0.5 * (1.0 + lax.erf(up_proj * math.sqrt(0.5)))
        bell = jnp.exp(-0.5 * up_proj * up_proj) * (1.0 / math.sqrt(2.0 * math.pi))
        g_ref[n] = (up_proj * below).astype(BF16)
        slope_ref[n] = (below + up_proj * bell).astype(BF16)
        copies.append(start_copy(g_ref.at[n], g_hbm.at[n], outs.at[0, n]))
        copies.append(start_copy(slope_ref.at[n], slope_hbm.at[n], outs.at[1, n]))
    for item in copies:
        item.wait()


def up_part(stream, vec, ups):
    rows, width = stream.shape
    wide = struct((4, rows, width), BF16)
    blocks, which = ups
    return call(
        partial(up_kernel, which, len(blocks)), [struct((rows, width), BF16), wide, wide],
        (stream, vec, *blocks), (2, 3),
        (
            pltpu.VMEM((4,) + block_shape(blocks), BF16), pltpu.VMEM(wide.shape, BF16),
            pltpu.VMEM(wide.shape, BF16), pltpu.SemaphoreType.DMA((4,)),
            pltpu.SemaphoreType.DMA((2, 4)),
        ), micros=9, out_placed=(1, 2),
    )


def start_down(refs, which, n, mat, sems):
    here = lax.axis_index("section")
    size = mat.shape[1] // 8
    waits = []
    for side in range(2):
        owner = 2 * jnp.bitwise_xor(here, n) + side
        for k in range(4):
            if len(refs) == 1:
                src, start = refs[0].at[owner, k, which], (side * 4 + k) * size
            else:
                src = block_ref(refs, k, which).at[owner]
                start = side * 4 * size + jnp.bitwise_xor(here, k) * size
            waits.append(
                start_copy(
                    src, mat.at[n, pl.ds(pl.multiple_of(start, size), size)],
                    sems.at[n, 2 * k + side],
                )
            )
    return waits


def down_kernel(which, count, h_ref, g_hbm, vec_ref, *refs):
    y_ref, mat, g_ref, sems, g_sems = refs[count:]
    waits = []
    for n in range(4):
        found = start_down(refs[:count], which, n, mat, sems)
        waits.append(found + [start_copy(g_hbm.at[n], g_ref.at[n], g_sems.at[n])])
    total = h_ref[...].astype(F32) + vec_ref[11:12, :]
    for n in range(4):
        for item in waits[n]:
            item.wait()
        total = total + nn_dot(g_ref[n], mat[n])
    y_ref[...] = total.astype(BF16)


def down_part(stream, hidden, vec, downs):
    rows, width = stream.shape
    blocks, which = downs
    return call(
        partial(down_kernel, which, len(blocks)), [struct((rows, width), BF16)],
        (stream, hidden, vec, *blocks), (1, 3, 4),
        (
            pltpu.VMEM((4, width, width), BF16), pltpu.VMEM((4, rows, width), BF16),
            pltpu.SemaphoreType.DMA((4, 8)), pltpu.SemaphoreType.DMA((4,)),
        ), micros=6,
    )[0]


def ffn_back_kernel(
    places, counts, gy_ref, h_ref, a_ref, g_hbm, slope_hbm, vec_ref, *refs
):
    (up_at, down_at, attn_at), (up_count, down_count, attn_count) = places, counts
    up_refs, refs = refs[:up_count], refs[up_count:]
    down_refs, refs = refs[:down_count], refs[down_count:]
    attn_refs, refs = refs[:attn_count], refs[attn_count:]
    (
        gh_ref, go_ref, keep_hbm, send_up, send_down, vg_ref,
        g_ref, slope_ref, mat, up_mat, out_mat, up_grad, down_grad,
        in_sems, sems, out_sems, up_sems, down_sems,
    ) = refs
    here = lax.axis_index("section")
    size, width = keep_hbm.shape[-2:]
    waits = []
    for n in range(4):
        found = start_down(down_refs, down_at, n, mat, sems)
        found.append(start_copy(slope_hbm.at[n], slope_ref.at[n], in_sems.at[0, n]))
        found.append(start_copy(g_hbm.at[n], g_ref.at[n], in_sems.at[1, n]))
        found.append(
            start_copy(block_ref(up_refs, n, up_at), up_mat.at[n], in_sems.at[2, n])
        )
        waits.append(found)
    out_wait = start_section(attn_refs, attn_at, (3,), out_mat, out_sems)[0]
    grad = gy_ref[...]
    normed = a_ref[...]
    vg_ref[...] = jnp.zeros_like(vg_ref)
    vg_ref[6:7, :] = jnp.sum(grad.astype(F32), axis=0, keepdims=True)
    grad_normed = None
    copies = []
    for n in range(4):
        for item in waits[n]:
            item.wait()
        block = jnp.bitwise_xor(here, n)
        grad_up = nt_dot(grad, mat[n]) * slope_ref[n].astype(F32)
        grad_up = grad_up.astype(BF16)
        vg_ref[pl.ds(2 + block, 1), :] = jnp.sum(grad_up.astype(F32), axis=0, keepdims=True)
        up_grad[n] = tn_dot(normed, grad_up).astype(BF16).reshape(8, size, width)
        out = (keep_hbm.at[:, 0], send_up.at[:, 0])[n % 2]
        copies.append(start_copy(up_grad.at[n], out.at[n // 2], up_sems.at[n]))
        down_grad[n] = tn_dot(g_ref[n], grad).astype(BF16).reshape(8, size, width)
        for j in range(4):
            place = jnp.bitwise_xor(here, j)
            for side in range(2):
                src, sem = down_grad.at[n, 4 * side + j], down_sems.at[n, 4 * side + j]

                @pl.when(place % 2 == 0)
                def _():
                    start_copy(src, keep_hbm.at[place // 2, 1, 2 * block + side], sem)

                @pl.when(place % 2 == 1)
                def _():
                    start_copy(src, send_down.at[place // 2, 0, 2 * block + side], sem)

                copies.append(pltpu.make_async_copy(src, keep_hbm.at[0, 1, 0], sem))
        term = nt_dot(grad_up, square(up_mat[n]))
        grad_normed = term if n == 0 else grad_normed + term
    grad_in, grad_gain, grad_shift = norm_back(
        h_ref[...].astype(F32), vec_ref[5:6, :], grad_normed, grad
    )
    gh_ref[...] = grad_in
    vg_ref[0:1, :] = grad_gain
    vg_ref[1:2, :] = grad_shift
    out_wait.wait()
    go_ref[...] = nt_dot(grad_in, square(out_mat[0])).astype(BF16)
    for item in copies:
        item.wait()


def ffn_back(grad, stream, normed, hidden, slope, vec, ups, downs, attn):
    rows, width = grad.shape
    sets = (ups, downs, attn)
    counts, places = tuple(len(item[0]) for item in sets), tuple(item[1] for item in sets)
    blocks = [ref for item in sets for ref in item[0]]
    block = block_shape(ups[0])
    part, half = struct((2, 2) + block, BF16), struct((2, 1) + block, BF16)
    low = struct((rows, width), BF16)
    dma = pltpu.SemaphoreType.DMA
    return call(
        partial(ffn_back_kernel, places, counts),
        [low, low, part, half, half, struct((8, width), F32)],
        (grad, stream, normed, hidden, slope, vec, *blocks),
        (3, 4, *range(6, 6 + len(blocks))),
        (
            pltpu.VMEM((4, rows, width), BF16), pltpu.VMEM((4, rows, width), BF16),
            pltpu.VMEM((4, width, width), BF16), pltpu.VMEM((4,) + block, BF16),
            pltpu.VMEM((1,) + block, BF16), pltpu.VMEM((4,) + block, BF16),
            pltpu.VMEM((4,) + block, BF16), dma((3, 4)), dma((4, 8)), dma((1,)), dma((4,)),
            dma((4, 8)),
        ), micros=20, out_placed=(2, 3, 4),
    )


def qkv_back_kernel(
    which, count, gy_ref, h_ref, a_ref, o_ref, gq_ref, own_hbm, got_ref, vec_ref, *refs
):
    gh_ref, keep_hbm, send_hbm, vg_ref, mat, own_ref, term, sems, own_sems, out_sems = refs[count:]
    waits = start_section(refs[:count], which, (0, 1, 2), mat, sems)
    own_waits = [start_copy(own_hbm.at[n], own_ref.at[n], own_sems.at[n]) for n in range(2)]
    here = lax.axis_index("section")
    grad = gy_ref[...]
    normed = a_ref[...]
    vg_ref[...] = jnp.zeros_like(vg_ref)
    copies = []

    def give(block, left, right):
        term[block] = tn_dot(left, right).astype(BF16).reshape(term.shape[1:])
        place = jnp.bitwise_xor(here, block)

        @pl.when(place % 2 == 0)
        def _():
            start_copy(term.at[block], keep_hbm.at[place // 2, 0], out_sems.at[block])

        @pl.when(place % 2 == 1)
        def _():
            start_copy(term.at[block], send_hbm.at[place // 2, 0], out_sems.at[block])

        copies.append(pltpu.make_async_copy(term.at[block], keep_hbm.at[0, 0], out_sems.at[block]))

    vg_ref[4:5, :] = jnp.sum(grad.astype(F32), axis=0, keepdims=True)
    give(3, o_ref[...], grad)
    grad_q = gq_ref[...]
    vg_ref[2:3, :] = jnp.sum(grad_q.astype(F32), axis=0, keepdims=True)
    give(0, normed, grad_q)
    own_waits[0].wait()
    grad_k = (own_ref[0] + got_ref[0].astype(F32)).astype(BF16)
    give(1, normed, grad_k)
    own_waits[1].wait()
    grad_v = (own_ref[1] + got_ref[1].astype(F32)).astype(BF16)
    vg_ref[3:4, :] = jnp.sum(grad_v.astype(F32), axis=0, keepdims=True)
    give(2, normed, grad_v)
    for item in waits:
        item.wait()
    grad_normed = (
        nt_dot(grad_q, square(mat[0])) + nt_dot(grad_k, square(mat[1])) + nt_dot(grad_v, square(mat[2]))
    )
    gh_ref[...], grad_gain, grad_shift = norm_back(
        h_ref[...].astype(F32), vec_ref[0:1, :], grad_normed, grad
    )
    vg_ref[0:1, :] = grad_gain
    vg_ref[1:2, :] = grad_shift
    for item in copies:
        item.wait()


def qkv_back(grad, stream, normed, mixed, parts, vec, attn):
    rows, width = grad.shape
    blocks, which = attn
    block = block_shape(blocks)
    part = struct((2, 1) + block, BF16)
    dma = pltpu.SemaphoreType.DMA
    return call(
        partial(qkv_back_kernel, which, len(blocks)),
        [struct((rows, width), BF16), part, part, struct((8, width), F32)],
        (grad, stream, normed, mixed, *parts, vec, *blocks),
        (5, *range(8, 8 + len(blocks))),
        (
            pltpu.VMEM((3,) + block, BF16), pltpu.VMEM((2, rows, width), F32),
            pltpu.VMEM((4,) + block, BF16), dma((3,)), dma((2,)), dma((4,)),
        ), micros=10, out_placed=(1, 2),
    )


def over(block, axis, move):
    count = lax.axis_size(axis)
    return lax.ppermute(block, axis, [(i, move(i)) for i in range(count)])


def to_core(block):
    return over(block, "section", lambda i: i ^ 1)


def to_x(block):
    return over(block, "section", lambda i: i ^ 2)


def to_y(block):
    return over(block, "dp", lambda i: i ^ 1)


def to_z(block, steps):
    return over(block, "dp", lambda i: (i + 2 * steps) % 8)


ALONG = [[0, 2, 4, 6], [1, 3, 5, 7]]


def gather_along(block):
    return lax.all_gather(block, "dp", axis=0, axis_index_groups=ALONG)


def all_z(block):
    return tuple(to_z(block, k) for k in (1, 2, 3))


class Line:
    def __init__(self, start):
        self.token = start

    def fence(self, arrays):
        *arrays, self.token = lax.optimization_barrier(tuple(arrays) + (self.token,))
        return arrays

    def run(self, body, *operands):
        flat, shape = jax.tree.flatten(operands)
        arrays = self.fence([item for item in flat if not isinstance(item, int)])
        flat = [item if isinstance(item, int) else arrays.pop(0) for item in flat]
        flat, shape = jax.tree.flatten(body(*jax.tree.unflatten(shape, flat)))
        return jax.tree.unflatten(shape, self.fence(flat))


def pick_kernel(
    qkv_ref, out_ref, up_ref, down_ref, again, ashift, qvb, outb, fgain, fshift, upb, downb,
    a1, f1, rest, last, ride,
):
    size, width = f1.shape[1:]
    here = lax.axis_index("section")
    group = lax.axis_index("dp")
    ride[...] = jnp.zeros_like(ride)
    for i in range(8):
        @pl.when(group == i)
        def _():
            for l in range(2):
                def put(row, start, ref):
                    wide = ref.shape[1]
                    at = slice(start % width, start % width + wide)
                    ride[16 * l + row : 16 * l + row + 1, at] = ref[l : l + 1, :].astype(F32)

                put(0, size * i, again)
                put(1, size * i, ashift)
                put(2 + 2 * size * i // width, 2 * size * i, qvb)
                put(4, size * i, outb)
                put(5, size * i, fgain)
                put(6, size * i, fshift)
                put(7 + 4 * size * i // width, 4 * size * i, upb)
                put(11, size * i, downb)

    a1[size:] = ride[...].astype(BF16)
    for m in range(4):
        @pl.when(here == m)
        def _():
            for l in range(2):
                attn = qkv_ref[l, :, m * width : (m + 1) * width] if m < 3 else out_ref[l]
                ups, downs = (f1.at[0], f1.at[1]) if l == 0 else (rest.at[0], last.at[0])
                ups[...] = up_ref[l, :, m * width : (m + 1) * width]
                downs[...] = down_ref[l, m * size : (m + 1) * size]
                if l == 0:
                    a1[:size] = attn
                else:
                    rest[1] = attn


def pick_blocks(*operands):
    size = operands[0].shape[1]
    width = operands[1].shape[2]
    return call(
        pick_kernel,
        [
            struct((size + 32, width), BF16), struct((2, size, width), BF16),
            struct((2, size, width), BF16), struct((1, size, width), BF16),
        ],
        operands, (), (pltpu.VMEM((32, width), F32),), micros=4,
    )


def split_kernel(near_ref, *out_refs):
    at = 0
    for left_ref, right_ref in zip(out_refs[::2], out_refs[1::2]):
        count, wide = left_ref.shape[1], left_ref.shape[-1]
        left_ref[...] = near_ref[:, at : at + count, :, :wide]
        right_ref[...] = near_ref[:, at : at + count, :, wide:]
        at += count


def split_near(near, counts):
    size, width = near.shape[2:]
    outs = []
    for count in counts:
        outs += [struct((4, count, size, width // 2), BF16)] * 2
    return call(split_kernel, outs, (near,))


def middle_kernel(left_ref, left_got, right_ref, right_got, x_ref, y_ref):
    side = lax.axis_index("dp") % 2
    for along in range(4):
        x_ref[2 * along + side] = left_ref[along]
        x_ref[2 * along + 1 - side] = left_got[along]
    y_ref[0] = right_ref[...]
    y_ref[1] = right_got[...]


def middle(left, left_got, right, right_got):
    part = left.shape[1:]
    return call(
        middle_kernel, [struct((8,) + part, BF16), struct((2, 4) + part, BF16)],
        (left, left_got, right, right_got), micros=120,
    )


def whole_kernel(x_ref, x_got, y_ref, y_got, out_ref, *ride_refs):
    side = lax.axis_index("dp") % 2
    count, size, wide = out_ref.shape[0], out_ref.shape[3], x_ref.shape[3]
    for c in range(count):
        for n, ref in enumerate((x_ref, x_got)):
            out_ref[c, n, :, :, :wide] = ref[:, c, :size]
            for along in range(4):
                out_ref[c, n, 2 * along + side, :, wide:] = y_ref[n, along, c, :size]
                out_ref[c, n, 2 * along + 1 - side, :, wide:] = y_got[n, along, c, :size]
    if ride_refs:
        left = jnp.sum(x_ref[:, 0, size:].astype(F32), axis=0)
        right = jnp.sum(y_ref[0, :, 0, size:].astype(F32), axis=0)
        right = right + jnp.sum(y_got[0, :, 0, size:].astype(F32), axis=0)
        for l in range(2):
            ride_refs[l][:, :wide] = left[16 * l : 16 * l + 16]
            ride_refs[l][:, wide:] = right[16 * l : 16 * l + 16]


def whole_blocks(x_send, x_got, y_send, y_got, size):
    _, count, full, wide = x_send.shape
    outs = [struct((count, 2, 8, size, 2 * wide), BF16)]
    if full > size:
        outs += [struct((16, 2 * wide), F32)] * 2
    return call(whole_kernel, outs, (x_send, x_got, y_send, y_got))


class Gather:
    def __init__(self, line, left, right, size):
        self.line, self.left, self.right, self.size = line, left, right, size
        self.left_got, self.right_got = to_y(left), to_x(right)

    def middle(self):
        self.x_send, self.y_send = self.line.run(
            middle, self.left, self.left_got, self.right, self.right_got
        )
        self.x_got, self.y_got = to_x(self.x_send), to_y(self.y_send)

    def whole(self):
        found = self.line.run(
            lambda *items: whole_blocks(*items, self.size),
            self.x_send, self.x_got, self.y_send, self.y_got,
        )
        self.pair = (found[0], to_core(found[0]))
        return found[1:]


def first_kernel(keep_ref, *refs):
    got_refs, (x_ref, y_ref, left_ref, right_ref) = refs[:-4], refs[-4:]
    wide = x_ref.shape[-1]
    side = lax.axis_index("dp") % 2
    for c in range(keep_ref.shape[1]):
        for n, ref in enumerate((left_ref, x_ref)):
            ref[c] = (
                keep_ref[n, c, :, :, :wide].astype(F32)
                + got_refs[c][n, 0, :, :, :wide].astype(F32)
            ).astype(BF16)
        for n in range(2):
            for along in range(4):
                for ref, pick in ((right_ref, side), (y_ref, 1 - side)):
                    at = 2 * along + pick
                    ref[n, c, along] = (
                        keep_ref[n, c, at, :, wide:].astype(F32)
                        + got_refs[c][n, 0, at, :, wide:].astype(F32)
                    ).astype(BF16)


def add_first(keep, *got):
    _, count, _, size, width = keep.shape
    x_part = struct((count, 8, size, width // 2), BF16)
    y_part = struct((2, count, 4, size, width // 2), BF16)
    return call(first_kernel, [x_part, y_part, x_part, y_part], (keep, *got), micros=5)


def both_kernel(keep_ref, up_ref, down_ref, out_ref):
    for c, ref in enumerate((up_ref, down_ref)):
        for n in range(2):
            out_ref[:, n, c] = (
                keep_ref[n, c].astype(F32) + ref[n, 0].astype(F32)
            ).astype(BF16)


def add_both(keep, *got):
    _, count, parts, size, width = keep.shape
    step = parts // 4
    spec = pl.BlockSpec((2, count, step, size, width), lambda i: (0, 0, i, 0, 0))
    half = pl.BlockSpec((2, 1, step, size, width), lambda i: (0, 0, i, 0, 0))
    return pl.pallas_call(
        both_kernel,
        grid=(4,),
        in_specs=[spec, half, half],
        out_specs=pl.BlockSpec((step, 2, count, size, width), lambda i: (i, 0, 0, 0, 0)),
        out_shape=struct((parts, 2, count, size, width), BF16),
        compiler_params=pltpu.CompilerParams(vmem_limit_bytes=VMEM_ROOM),
        cost_estimate=lasting(80),
    )(keep, *got)


def scatter_both(block):
    return lax.psum_scatter(block, "dp", scatter_dimension=0, tiled=True)[0]


def second_kernel(left_ref, x_got, right_ref, y_got, y_ref, x_ref, near_ref, rest_ref):
    side = lax.axis_index("dp") % 2
    for c in range(left_ref.shape[0]):
        for along in range(4):
            for ref, pick in ((near_ref, side), (y_ref, 1 - side)):
                at = 2 * along + pick
                ref[c, along] = (
                    left_ref[c, at].astype(F32) + x_got[c, at].astype(F32)
                ).astype(BF16)
        for n, ref in enumerate((rest_ref, x_ref)):
            ref[c] = (right_ref[n, c].astype(F32) + y_got[n, c].astype(F32)).astype(BF16)


def add_second(left, x_got, right, y_got):
    part = struct(right.shape[1:], BF16)
    return call(second_kernel, [part] * 4, (left, x_got, right, y_got), micros=120)


def third_kernel(near_ref, y_got, rest_ref, x_got, out_ref):
    wide = near_ref.shape[-1]
    for c in range(near_ref.shape[0]):
        for along in range(4):
            out_ref[along, c, :, :wide] = (
                near_ref[c, along].astype(F32) + y_got[c, along].astype(F32)
            ).astype(BF16)
            out_ref[along, c, :, wide:] = (
                rest_ref[c, along].astype(F32) + x_got[c, along].astype(F32)
            ).astype(BF16)


def add_third(micros, near, y_got, rest, x_got):
    count, _, size, wide = near.shape
    return call(
        third_kernel, [struct((4, count, size, 2 * wide), BF16)], (near, y_got, rest, x_got),
        micros=micros,
    )[0]


def split_kernel_back(near_ref, y_got, rest_ref, x_got, o0, o1, o2, o3):
    along = lax.axis_index("dp") // 2
    wide = near_ref.shape[-1]
    for c in range(near_ref.shape[0]):
        for k, ref in enumerate((o0, o1, o2, o3)):
            pick = lax.rem(along + k, 4)
            ref[c, :, :wide] = (
                near_ref[c, pick].astype(F32) + y_got[c, pick].astype(F32)
            ).astype(BF16)
            ref[c, :, wide:] = (
                rest_ref[c, pick].astype(F32) + x_got[c, pick].astype(F32)
            ).astype(BF16)


def add_third_split(near, y_got, rest, x_got):
    count, _, size, wide = near.shape
    part = struct((count, size, 2 * wide), BF16)
    return call(split_kernel_back, [part] * 4, (near, y_got, rest, x_got), micros=60)


def last_kernel(o0, o1, o2, o3, out_ref):
    out_ref[...] = (
        o0[...].astype(F32) + o1[...].astype(F32) + o2[...].astype(F32) + o3[...].astype(F32)
    ).astype(BF16)


def add_last(*parts):
    return call(last_kernel, [struct(parts[0].shape, BF16)], parts)[0]


def across(own):
    far = to_x(own)
    return own, to_core(own), far, to_core(far)


class Reduce:
    def __init__(self, line, x_send, y_send, left, right):
        self.line, self.left, self.right = line, left, right
        self.x_got, self.y_got = to_x(x_send), to_y(y_send)

    def second(self):
        y_send, x_send, self.near, self.rest = self.line.run(
            add_second, self.left, self.x_got, self.right, self.y_got
        )
        self.y_got, self.x_got = to_y(y_send), to_x(x_send)

    def third(self, micros):
        whole = self.line.run(
            partial(add_third, micros), self.near, self.y_got, self.rest, self.x_got
        )
        self.shard = lax.psum_scatter(
            whole, "dp", scatter_dimension=0, tiled=True, axis_index_groups=ALONG
        )[0]

    def third_split(self):
        self.parts = self.line.run(
            add_third_split, self.near, self.y_got, self.rest, self.x_got
        )
        self.z_got = [to_z(self.parts[k], k) for k in (1, 2, 3)]

    def last(self):
        self.shard = self.line.run(add_last, self.parts[0], *self.z_got)


def finish_kernel(a0, a1, a2, a3, f1_ref, rest_ref, qkv_ref, out_ref, up_ref, down_ref):
    here = lax.axis_index("section")
    size, width = f1_ref.shape[-2:]

    def put(l, b, found):
        if b < 3:
            qkv_ref[l, :, b * width : (b + 1) * width] = found.astype(F32)
        else:
            out_ref[l] = found.astype(F32)

    for m in range(4):
        @pl.when(here == m)
        def _():
            for b in range(4):
                put(0, b, (a0, a1, a2, a3)[m ^ b][0])

    for b in range(4):
        put(1, b, rest_ref[b, 2])
        for l, ref in enumerate((f1_ref, rest_ref)):
            up_ref[l, :, b * width : (b + 1) * width] = ref[b, 0].astype(F32)
            down_ref[l, b * size : (b + 1) * size] = ref[b, 1].astype(F32)


def finish(*held):
    _, size, width = held[0].shape
    return call(
        finish_kernel,
        [
            struct((2, size, 3 * width), F32), struct((2, size, width), F32),
            struct((2, size, 4 * width), F32), struct((2, 4 * size, width), F32),
        ],
        held, micros=5,
    )


def pick_row(stacked, index):
    return lax.dynamic_index_in_dim(stacked, index, 0, keepdims=False)


def local(
    tokens, lengths, cotangent, attn_gain, attn_shift, qkv_weight, qv_bias, out_weight, out_bias,
    ffn_gain, ffn_shift, up_weight, up_bias, down_weight, down_bias,
):
    layers, size, width3 = qkv_weight.shape
    width = width3 // 3
    eighth = width // 8
    micro_count, cell_count, seq_len, _ = tokens.shape
    section_id = lax.axis_index("section")
    section_count = lax.axis_size("section")
    group = lax.axis_size("dp")
    dp_id = lax.axis_index("dp")
    share = section_count // micro_count
    assert cell_count == 1 and share == 2 and section_count == 4 and layers == 2
    cell = section_id // share
    half = section_id % share
    rows = seq_len // share
    direct = group == 8
    line = Line(jnp.zeros((1, 1), F32))

    def mine(stacked):
        return lax.dynamic_slice(
            stacked, (cell, 0, half * rows, 0), (1, 1, rows, width)
        ).reshape(rows, width)

    def pinned():
        length = lax.dynamic_slice(lengths, (cell, 0), (1, 1)).reshape(())
        return line.run(
            lambda one, two, size: (
                mine(one), mine(two), jnp.stack([size - half * rows, size - (1 - half) * rows])
            ),
            tokens, cotangent, length,
        )

    if direct:
        a1_block, f1_block, rest_block, last_block = line.run(
            pick_blocks, qkv_weight, out_weight, up_weight, down_weight,
            attn_gain, attn_shift, qv_bias, out_bias, ffn_gain, ffn_shift, up_bias, down_bias,
        )
        a1_near = gather_along(a1_block[None])
        f1_near = gather_along(f1_block)
        rest, last = [
            lax.all_gather(item, ("dp", "section"), axis=0, tiled=False).reshape(
                8, 4, item.shape[0], size, width
            )
            for item in (rest_block, last_block)
        ]
        a1 = Gather(line, *line.run(lambda near: split_near(near, (1,)), a1_near), size)
        stream, grad, lens = pinned()
        a1.middle()
        u1_d1 = line.run(lambda near: split_near(near, (1, 1)), f1_near)
        u1 = Gather(line, *u1_d1[:2], size)
        d1 = Gather(line, *u1_d1[2:], size)
        vec1, vec2 = a1.whole()
        u1.middle()
        attn1 = (a1.pair, 0)
    else:
        def gather(block, axis):
            return lax.all_gather(block, "dp", axis=axis, tiled=True)

        def relative(blocks):
            found = [pick_row(blocks, section_id ^ n) for n in range(4)]
            return jnp.stack([found[0], found[2]])[None], jnp.stack([found[1], found[3]])[None]

        def attn_blocks(l):
            whole = gather(jnp.concatenate([qkv_weight[l], out_weight[l]], axis=1), 0)
            return relative(whole.reshape(8, eighth, 4, width).transpose(2, 0, 1, 3))

        def up_blocks(l):
            return relative(gather(up_weight[l], 0).reshape(8, eighth, 4, width).transpose(2, 0, 1, 3))

        def down_blocks(l):
            return relative(gather(down_weight[l], 0).reshape(8, 4, eighth, width).transpose(1, 0, 2, 3))

        def spread_vectors():
            def at(block, row_count):
                empty = jnp.zeros((layers, row_count, width), BF16)
                flat = block.shape[-1] * dp_id
                return lax.dynamic_update_slice(empty, block, (0, flat // width, flat % width))

            six = jnp.stack([attn_gain, attn_shift, out_bias, ffn_gain, ffn_shift, down_bias], axis=1)
            six = lax.dynamic_update_slice(
                jnp.zeros((layers, 6, width), BF16), six, (0, 0, dp_id * size)
            )
            qv = at(qv_bias[:, None], 2)
            ups = at(up_bias[:, None], 4)
            return jnp.concatenate(
                [six[:, :2], qv, six[:, 2:5], ups, six[:, 5:], jnp.zeros((layers, 4, width), BF16)],
                axis=1,
            )

        vecs = lax.psum(spread_vectors().astype(F32), "dp")
        vec1, vec2 = vecs[0], vecs[1]
        attn1, ups1, downs1 = [(blocks(0), 0) for blocks in (attn_blocks, up_blocks, down_blocks)]
        attn2, ups2, downs2 = [(blocks(1), 0) for blocks in (attn_blocks, up_blocks, down_blocks)]

    def redistribute_start(*blocks):
        quarter = rows // 2
        route_a = [(2 * c + h, 2 * h + c) for c in range(2) for h in range(2)]
        route_b = [(2 * c + h, 2 * h + 1 - c) for c in range(2) for h in range(2)]
        first = cell == 0

        def choose(*items):
            low = jnp.stack([item[:quarter] for item in items])
            high = jnp.stack([item[quarter:] for item in items])
            return jnp.where(first, low, high), jnp.where(first, high, low)

        send_a, send_b = line.run(choose, *blocks)
        return lax.ppermute(send_a, "section", route_a), lax.ppermute(send_b, "section", route_b)

    def redistribute_end(got_a, got_b):
        even = section_id % 2 == 0

        def place(a, b):
            pair = jnp.where(even, a, b), jnp.where(even, b, a)
            return tuple(jnp.stack([item[n] for item in pair])[:, None] for n in range(2))

        return line.run(place, got_a, got_b)

    if not direct:
        stream, grad, lens = pinned()

    attn_in1 = stream
    normed1, queries1, own1 = line.run(qkv_part, stream, vec1, attn1)
    peer1 = to_core(own1)
    if direct:
        d1.middle()
    mixed1, raised1, scale1 = line.run(attend, queries1, own1, peer1, lens)
    if direct:
        u1.whole()
        ups1 = (u1.pair, 0)
    ffn_in1 = line.run(out_part, attn_in1, mixed1, vec1, attn1)
    if direct:
        d1.whole()
        downs1 = (d1.pair, 0)
    normed2_1, hidden1, slope1 = line.run(up_part, ffn_in1, vec1, ups1)
    stream = line.run(down_part, ffn_in1, hidden1, vec1, downs1)
    attn_in2 = stream
    if direct:
        ups2, downs2, attn2 = ((rest,), 0), ((last,), 0), ((rest,), 1)
    normed2, queries2, own2 = line.run(qkv_part, stream, vec2, attn2)
    peer2 = to_core(own2)
    mixed2, raised2, scale2 = line.run(attend, queries2, own2, peer2, lens)
    ffn_in2 = line.run(out_part, attn_in2, mixed2, vec2, attn2)
    normed2_2, hidden2, slope2 = line.run(up_part, ffn_in2, vec2, ups2)
    stream = line.run(down_part, ffn_in2, hidden2, vec2, downs2)

    encoded_mine = stream
    grad, grad_mixed, f2_keep, f2_up, f2_down, f2_vec = line.run(
        ffn_back, grad, ffn_in2, normed2_2, hidden2, slope2, vec2, ups2, downs2, attn2
    )
    if direct:
        f2_got = to_core(f2_up), to_core(f2_down)
    grad_q, kv_own, kv_peer = line.run(
        attend_back, queries2, own2, peer2, mixed2, grad_mixed, raised2, scale2
    )
    kv_got = to_core(kv_peer)
    if direct:
        f2_part = scatter_both(line.run(add_both, f2_keep, *f2_got))
    grad, a2_keep, a2_send, a2_vec = line.run(
        qkv_back, grad, attn_in2, normed2, mixed2, (grad_q, kv_own, kv_got), vec2, attn2
    )
    if direct:
        a2_got = to_core(a2_send)
        a2r = Reduce(line, *line.run(add_first, a2_keep, a2_got))
    grad, grad_mixed, f1_keep, f1_up, f1_down, f1_vec = line.run(
        ffn_back, grad, ffn_in1, normed2_1, hidden1, slope1, vec1, ups1, downs1, attn1
    )
    if direct:
        f1_got = to_core(f1_up), to_core(f1_down)
        a2r.second()
        f1r = Reduce(line, *line.run(add_first, f1_keep, *f1_got))
    grad_q, kv_own, kv_peer = line.run(
        attend_back, queries1, own1, peer1, mixed1, grad_mixed, raised1, scale1
    )
    kv_got = to_core(kv_peer)
    if direct:
        f1r.second()
        a2r.third(2)
    grad, a1_keep, a1_send, a1_vec = line.run(
        qkv_back, grad, attn_in1, normed1, mixed1, (grad_q, kv_own, kv_got), vec1, attn1
    )

    def vector_shares(a, b, c, d):
        total = jnp.stack([jnp.concatenate([a, b]), jnp.concatenate([c, d])])

        def share(lo, hi):
            wide = total[:, lo:hi].reshape(layers, group, hi - lo, size)
            return wide.transpose(1, 0, 2, 3)

        def each(lo, hi):
            wide = total[:, lo:hi].reshape(layers, hi - lo, group, size)
            return wide.transpose(2, 0, 1, 3)

        return jnp.concatenate(
            [each(0, 2), share(2, 4), each(4, 10), share(10, 14), each(14, 16)], axis=2
        )

    if direct:
        a1_got = to_core(a1_send)
        f2_near, f2_send = line.run(lambda part: (part[0], part[1]), f2_part)
        f1r.third(120)
        a1r = Reduce(line, *line.run(add_first, a1_keep, a1_got))
        f2_far = to_x(f2_send)
        shares = line.run(
            lambda *vecs: jnp.broadcast_to(
                vector_shares(*vecs)[:, None], (group, section_count, layers, 16, size)
            ).reshape(group * section_count, layers, 16, size),
            a1_vec, f1_vec, a2_vec, f2_vec,
        )
        shares = lax.all_to_all(shares, ("dp", "section"), 0, 0, tiled=True)
        a1r.second()
        moved = redistribute_start(encoded_mine, grad)
        rest_own = line.run(
            lambda near, far, attn: jnp.concatenate([near + far, attn]), f2_near, f2_far, a2r.shard
        )
        rest_held = lax.all_gather(rest_own, "section", axis=0)
        a1r.third_split()
        f1_held = lax.all_gather(f1r.shard, "section", axis=0)
        a1r.last()
        a1_held = across(a1r.shard)
        my_vec = line.run(lambda got: jnp.sum(got, axis=0), shares)
        encoded, grad_tokens = redistribute_end(*moved)
        g_qkv, g_out, g_up, g_down = line.run(finish, *a1_held, f1_held, rest_held)
    else:
        encoded, grad_tokens = redistribute_end(*redistribute_start(encoded_mine, grad))
        def canonical(keep, send):
            blocks = jnp.stack([keep[0], send[0], keep[1], send[1]])
            return jnp.stack([pick_row(blocks, section_id ^ n) for n in range(4)])

        def scatter(whole):
            part = lax.psum_scatter(whole, "dp", scatter_dimension=0, tiled=True)
            return lax.psum(part, "section").astype(F32)

        def wide(blocks):
            return blocks.transpose(1, 2, 0, 3).reshape(width, 4 * width)

        both = [
            (canonical(a1_keep, a1_send), canonical(f1_keep, jnp.concatenate([f1_up, f1_down], axis=1))),
            (canonical(a2_keep, a2_send), canonical(f2_keep, jnp.concatenate([f2_up, f2_down], axis=1))),
        ]
        attn_all = jnp.stack([scatter(wide(attn[:, 0])) for attn, _ in both])
        g_qkv, g_out = attn_all[:, :, :width3], attn_all[:, :, width3:]
        g_up = jnp.stack([scatter(wide(ffn[:, 0])) for _, ffn in both])
        g_down = jnp.stack(
            [scatter(ffn[:, 1].transpose(1, 0, 2, 3).reshape(4 * width, width)) for _, ffn in both]
        )
        shares = lax.psum(vector_shares(a1_vec, f1_vec, a2_vec, f2_vec), ("dp", "section"))
        my_vec = pick_row(shares, dp_id)

    my_vec = my_vec + line.token
    return (
        encoded, grad_tokens, my_vec[:, 0], my_vec[:, 1], g_qkv,
        my_vec[:, 2:4].reshape(layers, 2 * size), g_out, my_vec[:, 4], my_vec[:, 8], my_vec[:, 9],
        g_up, my_vec[:, 10:14].reshape(layers, 4 * size), g_down, my_vec[:, 14],
    )


def solution(mesh):
    flat, rows4 = P(None, "dp"), P(None, "dp", None, None)
    mat, spread = P(None, "dp", None), P(None, "dp", "section", None)
    in_specs = (
        rows4, flat, rows4, flat, flat, mat, flat, mat, flat, flat, flat, mat, flat, mat, flat,
    )
    out_specs = (
        spread, spread, flat, flat, mat, flat, mat, flat, flat, flat, mat, flat, mat, flat,
    )
    return jax.shard_map(local, mesh=mesh, in_specs=in_specs, out_specs=out_specs, check_vma=False)
```

```python
from functools import partial
import math

import jax
import jax.numpy as jnp
from jax import lax
from jax.experimental import pallas as pl
from jax.experimental.pallas import tpu as pltpu
from jax.sharding import PartitionSpec as P

HEAD = 64
PAIR = 2 * HEAD
NORM_EPS = 1e-05
MASK_FLOOR = -1e30
F32 = jnp.float32
BF16 = jnp.bfloat16
VMEM_ROOM = 56 << 20
WHOLE = pl.BlockSpec(memory_space=pltpu.VMEM)
PLACED = pl.BlockSpec(memory_space=pl.ANY)


def nt_dot(left, right):
    return lax.dot_general(left, right, (((1,), (1,)), ((), ())), preferred_element_type=F32)


def nn_dot(left, right):
    return jnp.dot(left, right, preferred_element_type=F32)


def tn_dot(left, right):
    return lax.dot_general(left, right, (((0,), (0,)), ((), ())), preferred_element_type=F32)


def lasting(micros):
    return pl.CostEstimate(flops=micros << 28, transcendentals=0, bytes_accessed=1 << 16)


def struct(shape, kind):
    return jax.ShapeDtypeStruct(shape, kind)


def call(body, outs, operands, placed=(), scratch=(), micros=2, out_placed=()):
    return pl.pallas_call(
        body,
        in_specs=[PLACED if n in placed else WHOLE for n in range(len(operands))],
        out_specs=[PLACED if n in out_placed else WHOLE for n in range(len(outs))],
        out_shape=outs,
        scratch_shapes=list(scratch),
        compiler_params=pltpu.CompilerParams(vmem_limit_bytes=VMEM_ROOM),
        cost_estimate=lasting(micros),
    )(*operands)


def start_copy(src, dst, sem):
    copy = pltpu.make_async_copy(src, dst, sem)
    copy.start()
    return copy


def head_lanes(block, head):
    lane = lax.broadcasted_iota(jnp.int32, block.shape, 1)
    keep = (lane < HEAD) if head == 0 else (lane >= HEAD)
    return jnp.where(keep, block, jnp.zeros_like(block))


def attend_kernel(lens_ref, q_ref, ko_ref, kp_ref, vo_ref, vp_ref, o_ref, raised_ref, scale_ref):
    rows = q_ref.shape[0]
    score_scale = 1.0 / math.sqrt(HEAD)
    query_pair = q_ref[...] * jnp.asarray(score_scale, BF16)
    value_t = [vo_ref[...].T, vp_ref[...].T]
    mixed, scales = [], []
    for head in range(2):
        query = head_lanes(query_pair, head)
        scores = []
        for part, key_ref in enumerate((ko_ref, kp_ref)):
            part_scores = nt_dot(key_ref[...], query)
            key_row = lax.broadcasted_iota(jnp.int32, part_scores.shape, 0)
            scores.append(jnp.where(key_row < lens_ref[part], part_scores, MASK_FLOOR))
        row_max = jnp.maximum(
            jnp.max(scores[0], axis=0, keepdims=True), jnp.max(scores[1], axis=0, keepdims=True)
        )
        total = jnp.zeros((1, rows), F32)
        head_out = jnp.zeros((HEAD, rows), F32)
        for part in range(2):
            raised = jnp.exp(scores[part] - row_max)
            total = total + jnp.sum(raised, axis=0, keepdims=True)
            low = raised.astype(BF16)
            raised_ref[head, part * rows : (part + 1) * rows, :] = low
            head_out = head_out + nn_dot(value_t[part][head * HEAD : (head + 1) * HEAD, :], low)
        inverse = 1.0 / total
        mixed.append(head_out * inverse)
        scales.append(jnp.broadcast_to(inverse, (HEAD, rows)))
    o_ref[...] = jnp.concatenate(mixed, axis=0).T.astype(BF16)
    scale_ref[...] = jnp.concatenate(scales, axis=0).T


def attend(queries, own, peer, lens):
    rows, width = queries.shape
    pairs = width // PAIR
    block = pl.BlockSpec((rows, PAIR), lambda p, lens: (0, p))
    key = pl.BlockSpec((None, rows, PAIR), lambda p, lens: (0, 0, p))
    value = pl.BlockSpec((None, rows, PAIR), lambda p, lens: (1, 0, p))
    return pl.pallas_call(
        attend_kernel,
        grid_spec=pltpu.PrefetchScalarGridSpec(
            num_scalar_prefetch=1,
            grid=(pairs,),
            in_specs=[block, key, key, value, value],
            out_specs=[
                block, pl.BlockSpec((2, 2 * rows, rows), lambda p, lens: (p, 0, 0)), block,
            ],
        ),
        out_shape=[
            struct((rows, width), BF16), struct((2 * pairs, 2 * rows, rows), BF16),
            struct((rows, width), F32),
        ],
        compiler_params=pltpu.CompilerParams(vmem_limit_bytes=48 << 20),
        cost_estimate=lasting(16),
    )(lens, queries, own, peer, own, peer)


def attend_back_kernel(
    q_ref, ko_ref, kp_ref, vo_ref, vp_ref, o_ref, go_ref, raised_ref, scale_ref,
    gq_ref, own_ref, peer_ref,
):
    rows = q_ref.shape[0]
    score_scale = 1.0 / math.sqrt(HEAD)
    query_pair = q_ref[...] * jnp.asarray(score_scale, BF16)
    query_t = query_pair.T
    grad_pair = (go_ref[...].astype(F32) * scale_ref[...]).astype(BF16)
    grad_t = grad_pair.T
    inner = (o_ref[...].astype(F32) * grad_pair.astype(F32)).T
    value_refs = (vo_ref, vp_ref)
    key_t = [ko_ref[...].T, kp_ref[...].T]
    grad_key = [[], []]
    grad_value = [[], []]
    grad_query = []
    for head in range(2):
        lanes = slice(head * HEAD, (head + 1) * HEAD)
        grad_out = head_lanes(grad_pair, head)
        inner_row = jnp.sum(inner[lanes, :], axis=0, keepdims=True)
        head_query = jnp.zeros((HEAD, rows), F32)
        for part in range(2):
            raised = raised_ref[head, part * rows : (part + 1) * rows, :]
            grad_prob = nt_dot(value_refs[part][...], grad_out)
            grad_score = (raised.astype(F32) * (grad_prob - inner_row)).astype(BF16)
            grad_value[part].append(nt_dot(grad_t[lanes, :], raised))
            grad_key[part].append(nt_dot(query_t[lanes, :], grad_score))
            head_query = head_query + nn_dot(key_t[part][lanes, :], grad_score)
        grad_query.append(head_query * score_scale)
    gq_ref[...] = jnp.concatenate(grad_query, axis=0).T.astype(BF16)
    for n, grads in enumerate((grad_key, grad_value)):
        own_ref[n] = jnp.concatenate(grads[0], axis=0).T
        peer_ref[n] = jnp.concatenate(grads[1], axis=0).T.astype(BF16)


def attend_back(queries, own, peer, mixed, grad_mixed, raised, scale):
    rows, width = queries.shape
    pairs = width // PAIR
    block = pl.BlockSpec((rows, PAIR), lambda p: (0, p))
    key = pl.BlockSpec((None, rows, PAIR), lambda p: (0, 0, p))
    value = pl.BlockSpec((None, rows, PAIR), lambda p: (1, 0, p))
    both = pl.BlockSpec((2, rows, PAIR), lambda p: (0, 0, p))
    low, full = struct((rows, width), BF16), struct((2, rows, width), F32)
    sent = struct((2, rows, width), BF16)
    return pl.pallas_call(
        attend_back_kernel,
        grid=(pairs,),
        in_specs=[
            block, key, key, value, value, block, block,
            pl.BlockSpec((2, 2 * rows, rows), lambda p: (p, 0, 0)), block,
        ],
        out_specs=[block, both, both],
        out_shape=[low, full, sent],
        compiler_params=pltpu.CompilerParams(vmem_limit_bytes=48 << 20),
        cost_estimate=lasting(16),
    )(queries, own, peer, own, peer, mixed, grad_mixed, raised, scale)


def norm_unit(stream):
    center = stream - jnp.mean(stream, axis=-1, keepdims=True)
    spread = jnp.mean(center * center, axis=-1, keepdims=True)
    root = lax.rsqrt(spread + NORM_EPS)
    return center * root, root


def norm_back(stream, gain, grad_normed, grad_low):
    unit, root = norm_unit(stream)
    grad_gain = jnp.sum(grad_normed * unit, axis=0, keepdims=True)
    grad_shift = jnp.sum(grad_normed, axis=0, keepdims=True)
    grad_unit = grad_normed * gain
    grad_stream = root * (
        grad_unit
        - jnp.mean(grad_unit, axis=-1, keepdims=True)
        - unit * jnp.mean(grad_unit * unit, axis=-1, keepdims=True)
    )
    return (grad_low.astype(F32) + grad_stream).astype(BF16), grad_gain, grad_shift


def block_ref(refs, n, which):
    if len(refs) == 2:
        return refs[n % 2].at[which, n // 2]
    return refs[0].at[:, jnp.bitwise_xor(lax.axis_index("section"), n), which]


def start_section(refs, which, wanted, dst_refs, sems):
    here = lax.axis_index("section")
    waits = []
    for slot, block in enumerate(wanted):
        if len(refs) == 1:
            waits.append(start_copy(refs[0].at[:, block, which], dst_refs.at[slot], sems.at[slot]))
            continue
        place = jnp.bitwise_xor(here, block)
        for n in range(4):
            @pl.when(place == n)
            def _():
                start_copy(block_ref(refs, n, which), dst_refs.at[slot], sems.at[slot])
        waits.append(
            pltpu.make_async_copy(block_ref(refs, 0, which), dst_refs.at[slot], sems.at[slot])
        )
    return waits


def block_shape(blocks):
    shape = blocks[0].shape
    return shape[-3:] if len(blocks) == 2 else shape[:1] + shape[-2:]


def square(block):
    return block.reshape(block.shape[-3] * block.shape[-2], block.shape[-1])


def qkv_kernel(which, count, h_ref, vec_ref, *refs):
    blocks = refs[:count]
    a_hbm, q_hbm, kv_hbm, mat, a_ref, q_ref, kv_ref, sems, outs = refs[count:]
    waits = start_section(blocks, which, (1, 2, 0), mat, sems)
    unit, _ = norm_unit(h_ref[...].astype(F32))
    normed = (unit * vec_ref[0:1, :] + vec_ref[1:2, :]).astype(BF16)
    a_ref[...] = normed
    copies = [start_copy(a_ref, a_hbm, outs.at[0])]
    waits[0].wait()
    kv_ref[0] = nn_dot(normed, square(mat[0])).astype(BF16)
    copies.append(start_copy(kv_ref.at[0], kv_hbm.at[0], outs.at[1]))
    waits[1].wait()
    kv_ref[1] = (nn_dot(normed, square(mat[1])) + vec_ref[3:4, :]).astype(BF16)
    copies.append(start_copy(kv_ref.at[1], kv_hbm.at[1], outs.at[2]))
    waits[2].wait()
    q_ref[...] = (nn_dot(normed, square(mat[2])) + vec_ref[2:3, :]).astype(BF16)
    copies.append(start_copy(q_ref, q_hbm, outs.at[3]))
    for item in copies:
        item.wait()


def qkv_part(stream, vec, attn):
    rows, width = stream.shape
    blocks, which = attn
    low, both = struct((rows, width), BF16), struct((2, rows, width), BF16)
    return call(
        partial(qkv_kernel, which, len(blocks)), [low, low, both], (stream, vec, *blocks), (2, 3),
        (
            pltpu.VMEM((3,) + block_shape(blocks), BF16), pltpu.VMEM(low.shape, BF16),
            pltpu.VMEM(low.shape, BF16), pltpu.VMEM(both.shape, BF16),
            pltpu.SemaphoreType.DMA((3,)), pltpu.SemaphoreType.DMA((4,)),
        ), micros=5, out_placed=(0, 1, 2),
    )


def out_kernel(which, count, h_ref, o_ref, vec_ref, *refs):
    y_ref, mat, sems = refs[count:]
    start_section(refs[:count], which, (3,), mat, sems)[0].wait()
    y_ref[...] = (
        h_ref[...].astype(F32) + nn_dot(o_ref[...], square(mat[0])) + vec_ref[4:5, :]
    ).astype(BF16)


def out_part(stream, mixed, vec, attn):
    rows, width = stream.shape
    blocks, which = attn
    return call(
        partial(out_kernel, which, len(blocks)), [struct((rows, width), BF16)],
        (stream, mixed, vec, *blocks), (3, 4),
        (pltpu.VMEM((1,) + block_shape(blocks), BF16), pltpu.SemaphoreType.DMA((1,))), micros=4,
    )[0]


def up_kernel(which, count, h_ref, vec_ref, *refs):
    a_ref, g_hbm, slope_hbm, mat, g_ref, slope_ref, sems, outs = refs[count:]
    here = lax.axis_index("section")
    waits = [
        start_copy(block_ref(refs[:count], n, which), mat.at[n], sems.at[n]) for n in range(4)
    ]
    unit, _ = norm_unit(h_ref[...].astype(F32))
    normed = (unit * vec_ref[5:6, :] + vec_ref[6:7, :]).astype(BF16)
    a_ref[...] = normed
    copies = []
    for n in range(4):
        waits[n].wait()
        bias = vec_ref[pl.ds(7 + jnp.bitwise_xor(here, n), 1), :]
        up_proj = nn_dot(normed, square(mat[n])) + bias
        below = 0.5 * (1.0 + lax.erf(up_proj * math.sqrt(0.5)))
        bell = jnp.exp(-0.5 * up_proj * up_proj) * (1.0 / math.sqrt(2.0 * math.pi))
        g_ref[n] = (up_proj * below).astype(BF16)
        slope_ref[n] = (below + up_proj * bell).astype(BF16)
        copies.append(start_copy(g_ref.at[n], g_hbm.at[n], outs.at[0, n]))
        copies.append(start_copy(slope_ref.at[n], slope_hbm.at[n], outs.at[1, n]))
    for item in copies:
        item.wait()


def up_part(stream, vec, ups):
    rows, width = stream.shape
    wide = struct((4, rows, width), BF16)
    blocks, which = ups
    return call(
        partial(up_kernel, which, len(blocks)), [struct((rows, width), BF16), wide, wide],
        (stream, vec, *blocks), (2, 3),
        (
            pltpu.VMEM((4,) + block_shape(blocks), BF16), pltpu.VMEM(wide.shape, BF16),
            pltpu.VMEM(wide.shape, BF16), pltpu.SemaphoreType.DMA((4,)),
            pltpu.SemaphoreType.DMA((2, 4)),
        ), micros=9, out_placed=(1, 2),
    )


def start_down(refs, which, n, mat, sems):
    here = lax.axis_index("section")
    size = mat.shape[1] // 8
    waits = []
    for side in range(2):
        owner = 2 * jnp.bitwise_xor(here, n) + side
        for k in range(4):
            if len(refs) == 1:
                src, start = refs[0].at[owner, k, which], (side * 4 + k) * size
            else:
                src = block_ref(refs, k, which).at[owner]
                start = side * 4 * size + jnp.bitwise_xor(here, k) * size
            waits.append(
                start_copy(
                    src, mat.at[n, pl.ds(pl.multiple_of(start, size), size)],
                    sems.at[n, 2 * k + side],
                )
            )
    return waits


def down_kernel(which, count, h_ref, g_hbm, vec_ref, *refs):
    y_ref, mat, g_ref, sems, g_sems = refs[count:]
    waits = []
    for n in range(4):
        found = start_down(refs[:count], which, n, mat, sems)
        waits.append(found + [start_copy(g_hbm.at[n], g_ref.at[n], g_sems.at[n])])
    total = h_ref[...].astype(F32) + vec_ref[11:12, :]
    for n in range(4):
        for item in waits[n]:
            item.wait()
        total = total + nn_dot(g_ref[n], mat[n])
    y_ref[...] = total.astype(BF16)


def down_part(stream, hidden, vec, downs):
    rows, width = stream.shape
    blocks, which = downs
    return call(
        partial(down_kernel, which, len(blocks)), [struct((rows, width), BF16)],
        (stream, hidden, vec, *blocks), (1, 3, 4),
        (
            pltpu.VMEM((4, width, width), BF16), pltpu.VMEM((4, rows, width), BF16),
            pltpu.SemaphoreType.DMA((4, 8)), pltpu.SemaphoreType.DMA((4,)),
        ), micros=6,
    )[0]


def ffn_back_kernel(
    places, counts, gy_ref, h_ref, a_ref, g_hbm, slope_hbm, vec_ref, *refs
):
    (up_at, down_at, attn_at), (up_count, down_count, attn_count) = places, counts
    up_refs, refs = refs[:up_count], refs[up_count:]
    down_refs, refs = refs[:down_count], refs[down_count:]
    attn_refs, refs = refs[:attn_count], refs[attn_count:]
    (
        gh_ref, go_ref, keep_hbm, send_up, send_down, vg_ref,
        g_ref, slope_ref, mat, up_mat, out_mat, up_grad, down_grad,
        in_sems, sems, out_sems, up_sems, down_sems,
    ) = refs
    here = lax.axis_index("section")
    size, width = keep_hbm.shape[-2:]
    waits = []
    for n in range(4):
        found = start_down(down_refs, down_at, n, mat, sems)
        found.append(start_copy(slope_hbm.at[n], slope_ref.at[n], in_sems.at[0, n]))
        found.append(start_copy(g_hbm.at[n], g_ref.at[n], in_sems.at[1, n]))
        found.append(
            start_copy(block_ref(up_refs, n, up_at), up_mat.at[n], in_sems.at[2, n])
        )
        waits.append(found)
    out_wait = start_section(attn_refs, attn_at, (3,), out_mat, out_sems)[0]
    grad = gy_ref[...]
    normed = a_ref[...]
    vg_ref[...] = jnp.zeros_like(vg_ref)
    vg_ref[6:7, :] = jnp.sum(grad.astype(F32), axis=0, keepdims=True)
    grad_normed = None
    copies = []
    for n in range(4):
        for item in waits[n]:
            item.wait()
        block = jnp.bitwise_xor(here, n)
        grad_up = nt_dot(grad, mat[n]) * slope_ref[n].astype(F32)
        grad_up = grad_up.astype(BF16)
        vg_ref[pl.ds(2 + block, 1), :] = jnp.sum(grad_up.astype(F32), axis=0, keepdims=True)
        up_grad[n] = tn_dot(normed, grad_up).astype(BF16).reshape(8, size, width)
        out = (keep_hbm.at[:, 0], send_up.at[:, 0])[n % 2]
        copies.append(start_copy(up_grad.at[n], out.at[n // 2], up_sems.at[n]))
        down_grad[n] = tn_dot(g_ref[n], grad).astype(BF16).reshape(8, size, width)
        for j in range(4):
            place = jnp.bitwise_xor(here, j)
            for side in range(2):
                src, sem = down_grad.at[n, 4 * side + j], down_sems.at[n, 4 * side + j]

                @pl.when(place % 2 == 0)
                def _():
                    start_copy(src, keep_hbm.at[place // 2, 1, 2 * block + side], sem)

                @pl.when(place % 2 == 1)
                def _():
                    start_copy(src, send_down.at[place // 2, 0, 2 * block + side], sem)

                copies.append(pltpu.make_async_copy(src, keep_hbm.at[0, 1, 0], sem))
        term = nt_dot(grad_up, square(up_mat[n]))
        grad_normed = term if n == 0 else grad_normed + term
    grad_in, grad_gain, grad_shift = norm_back(
        h_ref[...].astype(F32), vec_ref[5:6, :], grad_normed, grad
    )
    gh_ref[...] = grad_in
    vg_ref[0:1, :] = grad_gain
    vg_ref[1:2, :] = grad_shift
    out_wait.wait()
    go_ref[...] = nt_dot(grad_in, square(out_mat[0])).astype(BF16)
    for item in copies:
        item.wait()


def ffn_back(grad, stream, normed, hidden, slope, vec, ups, downs, attn):
    rows, width = grad.shape
    sets = (ups, downs, attn)
    counts, places = tuple(len(item[0]) for item in sets), tuple(item[1] for item in sets)
    blocks = [ref for item in sets for ref in item[0]]
    block = block_shape(ups[0])
    part, half = struct((2, 2) + block, BF16), struct((2, 1) + block, BF16)
    low = struct((rows, width), BF16)
    dma = pltpu.SemaphoreType.DMA
    return call(
        partial(ffn_back_kernel, places, counts),
        [low, low, part, half, half, struct((8, width), F32)],
        (grad, stream, normed, hidden, slope, vec, *blocks),
        (3, 4, *range(6, 6 + len(blocks))),
        (
            pltpu.VMEM((4, rows, width), BF16), pltpu.VMEM((4, rows, width), BF16),
            pltpu.VMEM((4, width, width), BF16), pltpu.VMEM((4,) + block, BF16),
            pltpu.VMEM((1,) + block, BF16), pltpu.VMEM((4,) + block, BF16),
            pltpu.VMEM((4,) + block, BF16), dma((3, 4)), dma((4, 8)), dma((1,)), dma((4,)),
            dma((4, 8)),
        ), micros=20, out_placed=(2, 3, 4),
    )


def qkv_back_kernel(
    which, count, gy_ref, h_ref, a_ref, o_ref, gq_ref, own_hbm, got_ref, vec_ref, *refs
):
    gh_ref, keep_hbm, send_hbm, vg_ref, mat, own_ref, term, sems, own_sems, out_sems = refs[count:]
    waits = start_section(refs[:count], which, (0, 1, 2), mat, sems)
    own_waits = [start_copy(own_hbm.at[n], own_ref.at[n], own_sems.at[n]) for n in range(2)]
    here = lax.axis_index("section")
    grad = gy_ref[...]
    normed = a_ref[...]
    vg_ref[...] = jnp.zeros_like(vg_ref)
    copies = []

    def give(block, left, right):
        term[block] = tn_dot(left, right).astype(BF16).reshape(term.shape[1:])
        place = jnp.bitwise_xor(here, block)

        @pl.when(place % 2 == 0)
        def _():
            start_copy(term.at[block], keep_hbm.at[place // 2, 0], out_sems.at[block])

        @pl.when(place % 2 == 1)
        def _():
            start_copy(term.at[block], send_hbm.at[place // 2, 0], out_sems.at[block])

        copies.append(pltpu.make_async_copy(term.at[block], keep_hbm.at[0, 0], out_sems.at[block]))

    vg_ref[4:5, :] = jnp.sum(grad.astype(F32), axis=0, keepdims=True)
    give(3, o_ref[...], grad)
    grad_q = gq_ref[...]
    vg_ref[2:3, :] = jnp.sum(grad_q.astype(F32), axis=0, keepdims=True)
    give(0, normed, grad_q)
    own_waits[0].wait()
    grad_k = (own_ref[0] + got_ref[0].astype(F32)).astype(BF16)
    give(1, normed, grad_k)
    own_waits[1].wait()
    grad_v = (own_ref[1] + got_ref[1].astype(F32)).astype(BF16)
    vg_ref[3:4, :] = jnp.sum(grad_v.astype(F32), axis=0, keepdims=True)
    give(2, normed, grad_v)
    for item in waits:
        item.wait()
    grad_normed = (
        nt_dot(grad_q, square(mat[0])) + nt_dot(grad_k, square(mat[1])) + nt_dot(grad_v, square(mat[2]))
    )
    gh_ref[...], grad_gain, grad_shift = norm_back(
        h_ref[...].astype(F32), vec_ref[0:1, :], grad_normed, grad
    )
    vg_ref[0:1, :] = grad_gain
    vg_ref[1:2, :] = grad_shift
    for item in copies:
        item.wait()


def qkv_back(grad, stream, normed, mixed, parts, vec, attn):
    rows, width = grad.shape
    blocks, which = attn
    block = block_shape(blocks)
    part = struct((2, 1) + block, BF16)
    dma = pltpu.SemaphoreType.DMA
    return call(
        partial(qkv_back_kernel, which, len(blocks)),
        [struct((rows, width), BF16), part, part, struct((8, width), F32)],
        (grad, stream, normed, mixed, *parts, vec, *blocks),
        (5, *range(8, 8 + len(blocks))),
        (
            pltpu.VMEM((3,) + block, BF16), pltpu.VMEM((2, rows, width), F32),
            pltpu.VMEM((4,) + block, BF16), dma((3,)), dma((2,)), dma((4,)),
        ), micros=10, out_placed=(1, 2),
    )


def over(block, axis, move):
    count = lax.axis_size(axis)
    return lax.ppermute(block, axis, [(i, move(i)) for i in range(count)])


def to_core(block):
    return over(block, "section", lambda i: i ^ 1)


def to_x(block):
    return over(block, "section", lambda i: i ^ 2)


def to_y(block):
    return over(block, "dp", lambda i: i ^ 1)


def to_z(block, steps):
    return over(block, "dp", lambda i: (i + 2 * steps) % 8)


ALONG = [[0, 2, 4, 6], [1, 3, 5, 7]]


def gather_along(block):
    return lax.all_gather(block, "dp", axis=0, axis_index_groups=ALONG)


def all_z(block):
    return tuple(to_z(block, k) for k in (1, 2, 3))


class Line:
    def __init__(self, start):
        self.token = start

    def fence(self, arrays):
        *arrays, self.token = lax.optimization_barrier(tuple(arrays) + (self.token,))
        return arrays

    def run(self, body, *operands):
        flat, shape = jax.tree.flatten(operands)
        arrays = self.fence([item for item in flat if not isinstance(item, int)])
        flat = [item if isinstance(item, int) else arrays.pop(0) for item in flat]
        flat, shape = jax.tree.flatten(body(*jax.tree.unflatten(shape, flat)))
        return jax.tree.unflatten(shape, self.fence(flat))


def pick_kernel(
    qkv_ref, out_ref, up_ref, down_ref, again, ashift, qvb, outb, fgain, fshift, upb, downb,
    a1, f1, rest, last, ride,
):
    size, width = f1.shape[1:]
    here = lax.axis_index("section")
    group = lax.axis_index("dp")
    ride[...] = jnp.zeros_like(ride)
    for i in range(8):
        @pl.when(group == i)
        def _():
            for l in range(2):
                def put(row, start, ref):
                    wide = ref.shape[1]
                    at = slice(start % width, start % width + wide)
                    ride[16 * l + row : 16 * l + row + 1, at] = ref[l : l + 1, :].astype(F32)

                put(0, size * i, again)
                put(1, size * i, ashift)
                put(2 + 2 * size * i // width, 2 * size * i, qvb)
                put(4, size * i, outb)
                put(5, size * i, fgain)
                put(6, size * i, fshift)
                put(7 + 4 * size * i // width, 4 * size * i, upb)
                put(11, size * i, downb)

    a1[size:] = ride[...].astype(BF16)
    for m in range(4):
        @pl.when(here == m)
        def _():
            for l in range(2):
                attn = qkv_ref[l, :, m * width : (m + 1) * width] if m < 3 else out_ref[l]
                ups, downs = (f1.at[0], f1.at[1]) if l == 0 else (rest.at[0], last.at[0])
                ups[...] = up_ref[l, :, m * width : (m + 1) * width]
                downs[...] = down_ref[l, m * size : (m + 1) * size]
                if l == 0:
                    a1[:size] = attn
                else:
                    rest[1] = attn


def pick_blocks(*operands):
    size = operands[0].shape[1]
    width = operands[1].shape[2]
    return call(
        pick_kernel,
        [
            struct((size + 32, width), BF16), struct((2, size, width), BF16),
            struct((2, size, width), BF16), struct((1, size, width), BF16),
        ],
        operands, (), (pltpu.VMEM((32, width), F32),), micros=4,
    )


def split_kernel(near_ref, *out_refs):
    at = 0
    for left_ref, right_ref in zip(out_refs[::2], out_refs[1::2]):
        count, wide = left_ref.shape[1], left_ref.shape[-1]
        left_ref[...] = near_ref[:, at : at + count, :, :wide]
        right_ref[...] = near_ref[:, at : at + count, :, wide:]
        at += count


def split_near(near, counts):
    size, width = near.shape[2:]
    outs = []
    for count in counts:
        outs += [struct((4, count, size, width // 2), BF16)] * 2
    return call(split_kernel, outs, (near,))


def middle_kernel(left_ref, left_got, right_ref, right_got, x_ref, y_ref):
    side = lax.axis_index("dp") % 2
    for along in range(4):
        x_ref[2 * along + side] = left_ref[along]
        x_ref[2 * along + 1 - side] = left_got[along]
    y_ref[0] = right_ref[...]
    y_ref[1] = right_got[...]


def middle(left, left_got, right, right_got):
    part = left.shape[1:]
    return call(
        middle_kernel, [struct((8,) + part, BF16), struct((2, 4) + part, BF16)],
        (left, left_got, right, right_got), micros=120,
    )


def whole_kernel(x_ref, x_got, y_ref, y_got, out_ref, *ride_refs):
    side = lax.axis_index("dp") % 2
    count, size, wide = out_ref.shape[0], out_ref.shape[3], x_ref.shape[3]
    for c in range(count):
        for n, ref in enumerate((x_ref, x_got)):
            out_ref[c, n, :, :, :wide] = ref[:, c, :size]
            for along in range(4):
                out_ref[c, n, 2 * along + side, :, wide:] = y_ref[n, along, c, :size]
                out_ref[c, n, 2 * along + 1 - side, :, wide:] = y_got[n, along, c, :size]
    if ride_refs:
        left = jnp.sum(x_ref[:, 0, size:].astype(F32), axis=0)
        right = jnp.sum(y_ref[0, :, 0, size:].astype(F32), axis=0)
        right = right + jnp.sum(y_got[0, :, 0, size:].astype(F32), axis=0)
        for l in range(2):
            ride_refs[l][:, :wide] = left[16 * l : 16 * l + 16]
            ride_refs[l][:, wide:] = right[16 * l : 16 * l + 16]


def whole_blocks(x_send, x_got, y_send, y_got, size):
    _, count, full, wide = x_send.shape
    outs = [struct((count, 2, 8, size, 2 * wide), BF16)]
    if full > size:
        outs += [struct((16, 2 * wide), F32)] * 2
    return call(whole_kernel, outs, (x_send, x_got, y_send, y_got))


class Gather:
    def __init__(self, line, left, right, size):
        self.line, self.left, self.right, self.size = line, left, right, size
        self.left_got, self.right_got = to_y(left), to_x(right)

    def middle(self):
        self.x_send, self.y_send = self.line.run(
            middle, self.left, self.left_got, self.right, self.right_got
        )
        self.x_got, self.y_got = to_x(self.x_send), to_y(self.y_send)

    def whole(self):
        found = self.line.run(
            lambda *items: whole_blocks(*items, self.size),
            self.x_send, self.x_got, self.y_send, self.y_got,
        )
        self.pair = (found[0], to_core(found[0]))
        return found[1:]


def first_kernel(keep_ref, *refs):
    got_refs, (x_ref, y_ref, left_ref, right_ref) = refs[:-4], refs[-4:]
    wide = x_ref.shape[-1]
    side = lax.axis_index("dp") % 2
    for c in range(keep_ref.shape[1]):
        for n, ref in enumerate((left_ref, x_ref)):
            ref[c] = (
                keep_ref[n, c, :, :, :wide].astype(F32)
                + got_refs[c][n, 0, :, :, :wide].astype(F32)
            ).astype(BF16)
        for n in range(2):
            for along in range(4):
                for ref, pick in ((right_ref, side), (y_ref, 1 - side)):
                    at = 2 * along + pick
                    ref[n, c, along] = (
                        keep_ref[n, c, at, :, wide:].astype(F32)
                        + got_refs[c][n, 0, at, :, wide:].astype(F32)
                    ).astype(BF16)


def add_first(keep, *got):
    _, count, _, size, width = keep.shape
    x_part = struct((count, 8, size, width // 2), BF16)
    y_part = struct((2, count, 4, size, width // 2), BF16)
    return call(first_kernel, [x_part, y_part, x_part, y_part], (keep, *got), micros=5)


def both_kernel(keep_ref, up_ref, down_ref, out_ref):
    for c, ref in enumerate((up_ref, down_ref)):
        for n in range(2):
            out_ref[:, n, c] = (
                keep_ref[n, c].astype(F32) + ref[n, 0].astype(F32)
            ).astype(BF16)


def add_both(keep, *got):
    _, count, parts, size, width = keep.shape
    step = parts // 2
    spec = pl.BlockSpec((2, count, step, size, width), lambda i: (0, 0, i, 0, 0))
    half = pl.BlockSpec((2, 1, step, size, width), lambda i: (0, 0, i, 0, 0))
    return pl.pallas_call(
        both_kernel,
        grid=(2,),
        in_specs=[spec, half, half],
        out_specs=pl.BlockSpec((step, 2, count, size, width), lambda i: (i, 0, 0, 0, 0)),
        out_shape=struct((parts, 2, count, size, width), BF16),
        compiler_params=pltpu.CompilerParams(vmem_limit_bytes=VMEM_ROOM),
        cost_estimate=lasting(80),
    )(keep, *got)


def scatter_both(block):
    return lax.psum_scatter(block, "dp", scatter_dimension=0, tiled=True)[0]


def second_kernel(left_ref, x_got, right_ref, y_got, y_ref, x_ref, near_ref, rest_ref):
    side = lax.axis_index("dp") % 2
    for c in range(left_ref.shape[0]):
        for along in range(4):
            for ref, pick in ((near_ref, side), (y_ref, 1 - side)):
                at = 2 * along + pick
                ref[c, along] = (
                    left_ref[c, at].astype(F32) + x_got[c, at].astype(F32)
                ).astype(BF16)
        for n, ref in enumerate((rest_ref, x_ref)):
            ref[c] = (right_ref[n, c].astype(F32) + y_got[n, c].astype(F32)).astype(BF16)


def add_second(left, x_got, right, y_got):
    part = struct(right.shape[1:], BF16)
    return call(second_kernel, [part] * 4, (left, x_got, right, y_got), micros=120)


def third_kernel(near_ref, y_got, rest_ref, x_got, out_ref):
    wide = near_ref.shape[-1]
    for c in range(near_ref.shape[0]):
        for along in range(4):
            out_ref[along, c, :, :wide] = (
                near_ref[c, along].astype(F32) + y_got[c, along].astype(F32)
            ).astype(BF16)
            out_ref[along, c, :, wide:] = (
                rest_ref[c, along].astype(F32) + x_got[c, along].astype(F32)
            ).astype(BF16)


def add_third(micros, near, y_got, rest, x_got):
    count, _, size, wide = near.shape
    return call(
        third_kernel, [struct((4, count, size, 2 * wide), BF16)], (near, y_got, rest, x_got),
        micros=micros,
    )[0]


def split_kernel_back(near_ref, y_got, rest_ref, x_got, o0, o1, o2, o3):
    along = lax.axis_index("dp") // 2
    wide = near_ref.shape[-1]
    for c in range(near_ref.shape[0]):
        for k, ref in enumerate((o0, o1, o2, o3)):
            pick = lax.rem(along + k, 4)
            ref[c, :, :wide] = (
                near_ref[c, pick].astype(F32) + y_got[c, pick].astype(F32)
            ).astype(BF16)
            ref[c, :, wide:] = (
                rest_ref[c, pick].astype(F32) + x_got[c, pick].astype(F32)
            ).astype(BF16)


def add_third_split(near, y_got, rest, x_got):
    count, _, size, wide = near.shape
    part = struct((count, size, 2 * wide), BF16)
    return call(split_kernel_back, [part] * 4, (near, y_got, rest, x_got), micros=60)


def last_kernel(o0, o1, o2, o3, out_ref):
    out_ref[...] = (
        o0[...].astype(F32) + o1[...].astype(F32) + o2[...].astype(F32) + o3[...].astype(F32)
    ).astype(BF16)


def add_last(*parts):
    return call(last_kernel, [struct(parts[0].shape, BF16)], parts)[0]


def across(own):
    far = to_x(own)
    return own, to_core(own), far, to_core(far)


class Reduce:
    def __init__(self, line, x_send, y_send, left, right):
        self.line, self.left, self.right = line, left, right
        self.x_got, self.y_got = to_x(x_send), to_y(y_send)

    def second(self):
        y_send, x_send, self.near, self.rest = self.line.run(
            add_second, self.left, self.x_got, self.right, self.y_got
        )
        self.y_got, self.x_got = to_y(y_send), to_x(x_send)

    def third(self, micros):
        whole = self.line.run(
            partial(add_third, micros), self.near, self.y_got, self.rest, self.x_got
        )
        self.shard = lax.psum_scatter(
            whole, "dp", scatter_dimension=0, tiled=True, axis_index_groups=ALONG
        )[0]

    def third_split(self):
        self.parts = self.line.run(
            add_third_split, self.near, self.y_got, self.rest, self.x_got
        )
        self.z_got = [to_z(self.parts[k], k) for k in (1, 2, 3)]

    def last(self):
        self.shard = self.line.run(add_last, self.parts[0], *self.z_got)


def finish_kernel(a0, a1, a2, a3, f1_ref, rest_ref, qkv_ref, out_ref, up_ref, down_ref):
    here = lax.axis_index("section")
    size, width = f1_ref.shape[-2:]

    def put(l, b, found):
        if b < 3:
            qkv_ref[l, :, b * width : (b + 1) * width] = found.astype(F32)
        else:
            out_ref[l] = found.astype(F32)

    for m in range(4):
        @pl.when(here == m)
        def _():
            for b in range(4):
                put(0, b, (a0, a1, a2, a3)[m ^ b][0])

    for b in range(4):
        put(1, b, rest_ref[b, 2])
        for l, ref in enumerate((f1_ref, rest_ref)):
            up_ref[l, :, b * width : (b + 1) * width] = ref[b, 0].astype(F32)
            down_ref[l, b * size : (b + 1) * size] = ref[b, 1].astype(F32)


def finish(*held):
    _, size, width = held[0].shape
    return call(
        finish_kernel,
        [
            struct((2, size, 3 * width), F32), struct((2, size, width), F32),
            struct((2, size, 4 * width), F32), struct((2, 4 * size, width), F32),
        ],
        held, micros=5,
    )


def pick_row(stacked, index):
    return lax.dynamic_index_in_dim(stacked, index, 0, keepdims=False)


def local(
    tokens, lengths, cotangent, attn_gain, attn_shift, qkv_weight, qv_bias, out_weight, out_bias,
    ffn_gain, ffn_shift, up_weight, up_bias, down_weight, down_bias,
):
    layers, size, width3 = qkv_weight.shape
    width = width3 // 3
    eighth = width // 8
    micro_count, cell_count, seq_len, _ = tokens.shape
    section_id = lax.axis_index("section")
    section_count = lax.axis_size("section")
    group = lax.axis_size("dp")
    dp_id = lax.axis_index("dp")
    share = section_count // micro_count
    assert cell_count == 1 and share == 2 and section_count == 4 and layers == 2
    cell = section_id // share
    half = section_id % share
    rows = seq_len // share
    direct = group == 8
    line = Line(jnp.zeros((1, 1), F32))

    def mine(stacked):
        return lax.dynamic_slice(
            stacked, (cell, 0, half * rows, 0), (1, 1, rows, width)
        ).reshape(rows, width)

    def pinned():
        length = lax.dynamic_slice(lengths, (cell, 0), (1, 1)).reshape(())
        return line.run(
            lambda one, two, size: (
                mine(one), mine(two), jnp.stack([size - half * rows, size - (1 - half) * rows])
            ),
            tokens, cotangent, length,
        )

    if direct:
        a1_block, f1_block, rest_block, last_block = line.run(
            pick_blocks, qkv_weight, out_weight, up_weight, down_weight,
            attn_gain, attn_shift, qv_bias, out_bias, ffn_gain, ffn_shift, up_bias, down_bias,
        )
        a1_near = gather_along(a1_block[None])
        f1_near = gather_along(f1_block)
        rest, last = [
            lax.all_gather(item, ("dp", "section"), axis=0, tiled=False).reshape(
                8, 4, item.shape[0], size, width
            )
            for item in (rest_block, last_block)
        ]
        a1 = Gather(line, *line.run(lambda near: split_near(near, (1,)), a1_near), size)
        stream, grad, lens = pinned()
        a1.middle()
        u1_d1 = line.run(lambda near: split_near(near, (1, 1)), f1_near)
        u1 = Gather(line, *u1_d1[:2], size)
        d1 = Gather(line, *u1_d1[2:], size)
        vec1, vec2 = a1.whole()
        u1.middle()
        attn1 = (a1.pair, 0)
    else:
        def gather(block, axis):
            return lax.all_gather(block, "dp", axis=axis, tiled=True)

        def relative(blocks):
            found = [pick_row(blocks, section_id ^ n) for n in range(4)]
            return jnp.stack([found[0], found[2]])[None], jnp.stack([found[1], found[3]])[None]

        def attn_blocks(l):
            whole = gather(jnp.concatenate([qkv_weight[l], out_weight[l]], axis=1), 0)
            return relative(whole.reshape(8, eighth, 4, width).transpose(2, 0, 1, 3))

        def up_blocks(l):
            return relative(gather(up_weight[l], 0).reshape(8, eighth, 4, width).transpose(2, 0, 1, 3))

        def down_blocks(l):
            return relative(gather(down_weight[l], 0).reshape(8, 4, eighth, width).transpose(1, 0, 2, 3))

        def spread_vectors():
            def at(block, row_count):
                empty = jnp.zeros((layers, row_count, width), BF16)
                flat = block.shape[-1] * dp_id
                return lax.dynamic_update_slice(empty, block, (0, flat // width, flat % width))

            six = jnp.stack([attn_gain, attn_shift, out_bias, ffn_gain, ffn_shift, down_bias], axis=1)
            six = lax.dynamic_update_slice(
                jnp.zeros((layers, 6, width), BF16), six, (0, 0, dp_id * size)
            )
            qv = at(qv_bias[:, None], 2)
            ups = at(up_bias[:, None], 4)
            return jnp.concatenate(
                [six[:, :2], qv, six[:, 2:5], ups, six[:, 5:], jnp.zeros((layers, 4, width), BF16)],
                axis=1,
            )

        vecs = lax.psum(spread_vectors().astype(F32), "dp")
        vec1, vec2 = vecs[0], vecs[1]
        attn1, ups1, downs1 = [(blocks(0), 0) for blocks in (attn_blocks, up_blocks, down_blocks)]
        attn2, ups2, downs2 = [(blocks(1), 0) for blocks in (attn_blocks, up_blocks, down_blocks)]

    def redistribute_start(*blocks):
        quarter = rows // 2
        route_a = [(2 * c + h, 2 * h + c) for c in range(2) for h in range(2)]
        route_b = [(2 * c + h, 2 * h + 1 - c) for c in range(2) for h in range(2)]
        first = cell == 0

        def choose(*items):
            low = jnp.stack([item[:quarter] for item in items])
            high = jnp.stack([item[quarter:] for item in items])
            return jnp.where(first, low, high), jnp.where(first, high, low)

        send_a, send_b = line.run(choose, *blocks)
        return lax.ppermute(send_a, "section", route_a), lax.ppermute(send_b, "section", route_b)

    def redistribute_end(got_a, got_b):
        even = section_id % 2 == 0

        def place(a, b):
            pair = jnp.where(even, a, b), jnp.where(even, b, a)
            return tuple(jnp.stack([item[n] for item in pair])[:, None] for n in range(2))

        return line.run(place, got_a, got_b)

    if not direct:
        stream, grad, lens = pinned()

    attn_in1 = stream
    normed1, queries1, own1 = line.run(qkv_part, stream, vec1, attn1)
    peer1 = to_core(own1)
    if direct:
        d1.middle()
    mixed1, raised1, scale1 = line.run(attend, queries1, own1, peer1, lens)
    if direct:
        u1.whole()
        ups1 = (u1.pair, 0)
    ffn_in1 = line.run(out_part, attn_in1, mixed1, vec1, attn1)
    if direct:
        d1.whole()
        downs1 = (d1.pair, 0)
    normed2_1, hidden1, slope1 = line.run(up_part, ffn_in1, vec1, ups1)
    stream = line.run(down_part, ffn_in1, hidden1, vec1, downs1)
    attn_in2 = stream
    if direct:
        ups2, downs2, attn2 = ((rest,), 0), ((last,), 0), ((rest,), 1)
    normed2, queries2, own2 = line.run(qkv_part, stream, vec2, attn2)
    peer2 = to_core(own2)
    mixed2, raised2, scale2 = line.run(attend, queries2, own2, peer2, lens)
    ffn_in2 = line.run(out_part, attn_in2, mixed2, vec2, attn2)
    normed2_2, hidden2, slope2 = line.run(up_part, ffn_in2, vec2, ups2)
    stream = line.run(down_part, ffn_in2, hidden2, vec2, downs2)

    encoded_mine = stream
    grad, grad_mixed, f2_keep, f2_up, f2_down, f2_vec = line.run(
        ffn_back, grad, ffn_in2, normed2_2, hidden2, slope2, vec2, ups2, downs2, attn2
    )
    if direct:
        f2_got = to_core(f2_up), to_core(f2_down)
    grad_q, kv_own, kv_peer = line.run(
        attend_back, queries2, own2, peer2, mixed2, grad_mixed, raised2, scale2
    )
    kv_got = to_core(kv_peer)
    if direct:
        f2_part = scatter_both(line.run(add_both, f2_keep, *f2_got))
    grad, a2_keep, a2_send, a2_vec = line.run(
        qkv_back, grad, attn_in2, normed2, mixed2, (grad_q, kv_own, kv_got), vec2, attn2
    )
    if direct:
        a2_got = to_core(a2_send)
        a2r = Reduce(line, *line.run(add_first, a2_keep, a2_got))
    grad, grad_mixed, f1_keep, f1_up, f1_down, f1_vec = line.run(
        ffn_back, grad, ffn_in1, normed2_1, hidden1, slope1, vec1, ups1, downs1, attn1
    )
    if direct:
        f1_got = to_core(f1_up), to_core(f1_down)
        a2r.second()
        f1r = Reduce(line, *line.run(add_first, f1_keep, *f1_got))
    grad_q, kv_own, kv_peer = line.run(
        attend_back, queries1, own1, peer1, mixed1, grad_mixed, raised1, scale1
    )
    kv_got = to_core(kv_peer)
    if direct:
        f1r.second()
        a2r.third(2)
    grad, a1_keep, a1_send, a1_vec = line.run(
        qkv_back, grad, attn_in1, normed1, mixed1, (grad_q, kv_own, kv_got), vec1, attn1
    )

    def vector_shares(a, b, c, d):
        total = jnp.stack([jnp.concatenate([a, b]), jnp.concatenate([c, d])])

        def share(lo, hi):
            wide = total[:, lo:hi].reshape(layers, group, hi - lo, size)
            return wide.transpose(1, 0, 2, 3)

        def each(lo, hi):
            wide = total[:, lo:hi].reshape(layers, hi - lo, group, size)
            return wide.transpose(2, 0, 1, 3)

        return jnp.concatenate(
            [each(0, 2), share(2, 4), each(4, 10), share(10, 14), each(14, 16)], axis=2
        )

    if direct:
        a1_got = to_core(a1_send)
        f2_near, f2_send = line.run(lambda part: (part[0], part[1]), f2_part)
        f1r.third(120)
        a1r = Reduce(line, *line.run(add_first, a1_keep, a1_got))
        f2_far = to_x(f2_send)
        shares = line.run(
            lambda *vecs: jnp.broadcast_to(
                vector_shares(*vecs)[:, None], (group, section_count, layers, 16, size)
            ).reshape(group * section_count, layers, 16, size),
            a1_vec, f1_vec, a2_vec, f2_vec,
        )
        shares = lax.all_to_all(shares, ("dp", "section"), 0, 0, tiled=True)
        a1r.second()
        moved = redistribute_start(encoded_mine, grad)
        rest_own = line.run(
            lambda near, far, attn: jnp.concatenate([near + far, attn]), f2_near, f2_far, a2r.shard
        )
        rest_held = lax.all_gather(rest_own, "section", axis=0)
        a1r.third_split()
        f1_held = lax.all_gather(f1r.shard, "section", axis=0)
        a1r.last()
        a1_held = across(a1r.shard)
        my_vec = line.run(lambda got: jnp.sum(got, axis=0), shares)
        encoded, grad_tokens = redistribute_end(*moved)
        g_qkv, g_out, g_up, g_down = line.run(finish, *a1_held, f1_held, rest_held)
    else:
        encoded, grad_tokens = redistribute_end(*redistribute_start(encoded_mine, grad))
        def canonical(keep, send):
            blocks = jnp.stack([keep[0], send[0], keep[1], send[1]])
            return jnp.stack([pick_row(blocks, section_id ^ n) for n in range(4)])

        def scatter(whole):
            part = lax.psum_scatter(whole, "dp", scatter_dimension=0, tiled=True)
            return lax.psum(part, "section").astype(F32)

        def wide(blocks):
            return blocks.transpose(1, 2, 0, 3).reshape(width, 4 * width)

        both = [
            (canonical(a1_keep, a1_send), canonical(f1_keep, jnp.concatenate([f1_up, f1_down], axis=1))),
            (canonical(a2_keep, a2_send), canonical(f2_keep, jnp.concatenate([f2_up, f2_down], axis=1))),
        ]
        attn_all = jnp.stack([scatter(wide(attn[:, 0])) for attn, _ in both])
        g_qkv, g_out = attn_all[:, :, :width3], attn_all[:, :, width3:]
        g_up = jnp.stack([scatter(wide(ffn[:, 0])) for _, ffn in both])
        g_down = jnp.stack(
            [scatter(ffn[:, 1].transpose(1, 0, 2, 3).reshape(4 * width, width)) for _, ffn in both]
        )
        shares = lax.psum(vector_shares(a1_vec, f1_vec, a2_vec, f2_vec), ("dp", "section"))
        my_vec = pick_row(shares, dp_id)

    my_vec = my_vec + line.token
    return (
        encoded, grad_tokens, my_vec[:, 0], my_vec[:, 1], g_qkv,
        my_vec[:, 2:4].reshape(layers, 2 * size), g_out, my_vec[:, 4], my_vec[:, 8], my_vec[:, 9],
        g_up, my_vec[:, 10:14].reshape(layers, 4 * size), g_down, my_vec[:, 14],
    )


def solution(mesh):
    flat, rows4 = P(None, "dp"), P(None, "dp", None, None)
    mat, spread = P(None, "dp", None), P(None, "dp", "section", None)
    in_specs = (
        rows4, flat, rows4, flat, flat, mat, flat, mat, flat, flat, flat, mat, flat, mat, flat,
    )
    out_specs = (
        spread, spread, flat, flat, mat, flat, mat, flat, flat, flat, mat, flat, mat, flat,
    )
    return jax.shard_map(local, mesh=mesh, in_specs=in_specs, out_specs=out_specs, check_vma=False)
```
